32 devices in a mesh: head: 2 (over y), blk: 16 (over z, x, core).
Axes of the slice: x: 2, y: 2, z: 4, core: 2. Of those that a mesh axis runs over, the one named last changes fastest.
Arguments:
- tokens: bfloat16 [4, 1024, 768], P('head', 'blk'), may hold values from -6 to 6
- previous_layer_logits: float32 [4, 1024, 12], P('head', 'blk'), may hold values from -6 to 6
- lengths: int32 [4], replicated, may hold values from 256 to 1024, as said below
- routes: int32 [4, 1024, 2], P('head', 'blk'), may hold values from 0 to 11, all different within a row
- pair_order: int32 [4, 1024, 2], P('head', 'blk'), may hold values from 0 to 255, as said below
- gain_attn: bfloat16 [768], P('blk'), may hold values from 0.5 to 1.5
- w_qkv: bfloat16 [768, 3, 768], P('blk', None, 'head'), may hold values from -0.21875 to 0.21875
- w_out: bfloat16 [768, 768], P('blk', 'head'), may hold values from -1.75 to 1.75
- gain_ffn: bfloat16 [768], P('blk'), may hold values from 0.5 to 1.5
- w_router: bfloat16 [768, 12], P('blk'), may hold values from -0.109375 to 0.109375
- w_residual: float32 [12, 12], replicated, may hold values from -0.875 to 0.875
- w_const: bfloat16 [768, 4], P('blk'), may hold values from -0.21875 to 0.21875
- const_vec: bfloat16 [768, 2], P('blk'), may hold values from -6 to 6
- w_in: bfloat16 [768, 8, 2, 2048], P(None, 'head', None, 'blk'), may hold values from -0.21875 to 0.21875
- w_down: bfloat16 [2048, 8, 768], P('blk', 'head'), may hold values from -0.125 to 0.125
- cotangent: float32 [4, 1024, 768], P('head', 'blk'), may hold values from -6 to 6
Outputs:
- output: float32 [4, 1024, 768], P('head', 'blk')
- grad_tokens: float32 [4, 1024, 768], P('head', 'blk')
- grad_gain_attn: float32 [768], P('blk')
- grad_w_qkv: float32 [768, 3, 768], P('blk', None, 'head')
- grad_w_out: float32 [768, 768], P('blk', 'head')
- grad_gain_ffn: float32 [768], P('blk')
- grad_w_router: float32 [768, 12], P('blk')
- grad_w_residual: float32 [12, 12], replicated
- grad_w_const: float32 [768, 4], P('blk')
- grad_const_vec: float32 [768, 2], P('blk')
- grad_w_in: float32 [768, 8, 2, 2048], P(None, 'head', None, 'blk')
- grad_w_down: float32 [2048, 8, 768], P('blk', 'head')
The draws below stay inside these ranges and needn't reach their ends.
Inputs may be any that keep to these rules, and one draw needn't show every extreme that they name: `lengths`: one sequence in every draw has all 1024 slots valid. `routes`: each token names two different experts: 0 to 7 feed-forward, 8 zero, 9 copy, 10 and 11 constant. `pair_order`: within each block (h, b) the values are a permutation of 0 to 255.
All inputs are finite; a program needn't handle non-finite values.
Results may differ from the reference program's by a relative error of at most 0.02.
Values may be sent and summed in bfloat16 or wider, within the bound.
No kernel may reach another device: no remote copies, remote signals or barrier semaphores. Data moves between devices by JAX's collectives and lax.ppermute only.
A program may use at most 256 MiB of HBM per device.

```python
import math
from functools import partial
import jax
import jax.numpy as jnp
from jax import lax

D = 768
NH = 12
HD = 64
FF = 2048
NEXP = 8
EALL = 12
SEQUENCE_COUNT = 4
SLOT_DEV = 64
SEQ_DEV = 2
SLOT_COUNT = 1024
TOK_DEV = 128
CAP = 24


def draw_lengths(key, part):
    first_key, second_key = jax.random.split(key)
    drawn_len = jax.random.randint(first_key, (SEQUENCE_COUNT,), SLOT_COUNT // 4, SLOT_COUNT + 1, dtype=jnp.int32)
    chosen = jax.random.randint(second_key, (), 0, SEQUENCE_COUNT, dtype=jnp.int32)
    return jnp.where(jnp.arange(SEQUENCE_COUNT, dtype=jnp.int32) == chosen, SLOT_COUNT, drawn_len).astype(jnp.int32)


def draw_pair_order(key, part):
    n_head_blk = SEQUENCE_COUNT // SEQ_DEV
    n_slot_blk = SLOT_COUNT // SLOT_DEV
    block_keys = jax.random.split(key, n_head_blk * n_slot_blk)
    permuted = jax.vmap(lambda one_key: jax.random.permutation(one_key, 2 * TOK_DEV))(block_keys)
    shaped = permuted.reshape(n_head_blk, n_slot_blk, SEQ_DEV, SLOT_DEV, 2)
    shaped = jnp.transpose(shaped, (0, 2, 1, 3, 4))
    return shaped.reshape(SEQUENCE_COUNT, SLOT_COUNT, 2).astype(jnp.int32)


def block_scale(stream_key, shape, cuts, low, high):
    loudness = 1.0
    for axis_at, parts in cuts:
        steps = jax.random.uniform(jax.random.fold_in(jax.random.fold_in(stream_key, 6), axis_at), (parts,), jnp.float32, low / len(cuts), high / len(cuts))
        loudness = loudness * jnp.repeat(jnp.exp(steps), shape[axis_at] // parts).reshape((-1,) + (1,) * (len(shape) - 1 - axis_at))
    return loudness


def choose_distinct(rng, rows, amount, top, lift):
    order = jax.random.permutation(jax.random.fold_in(rng, 1), amount)
    pull = order
    for power in range(3):
        pull = pull * pull // amount
    pull = pull * lift // amount
    tickets = jax.random.randint(jax.random.fold_in(rng, 2), (rows, amount), 0, 4096) + pull
    fixed_rows = jax.random.permutation(jax.random.fold_in(rng, 3), rows)[jnp.arange(amount) % rows]
    tickets = jnp.where(jnp.arange(rows)[:, None] == fixed_rows[None, :], 1 << 14, tickets)
    priority = tickets * amount + jnp.arange(amount)
    return lax.top_k(priority.astype(jnp.int32), top)[1].astype(jnp.int32)


def scatter_about(key, dims, deviation, bound, cuts=(), kind=jnp.bfloat16):
    drawn = deviation * jax.random.normal(key, dims, jnp.float32)
    if cuts:
        drawn = drawn * block_scale(key, dims, cuts, -0.22, 0.18)
    return jnp.clip(drawn, -bound, bound).astype(kind)


def setup_inputs(seed: int = 0) -> dict:
    key_of = jax.random.split(jax.random.key(seed), 17)
    return {
        "tokens": scatter_about(key_of[0], (SEQUENCE_COUNT, SLOT_COUNT, D), 1.0, 6.0, ((0, 2), (1, 16))),
        "previous_layer_logits": scatter_about(key_of[1], (SEQUENCE_COUNT, SLOT_COUNT, EALL), 1.0, 6.0, ((0, 2), (1, 16)), jnp.float32),
        "lengths": draw_lengths(jax.random.fold_in(key_of[16], 71), 0),
        "routes": choose_distinct(key_of[3], SEQUENCE_COUNT * SLOT_COUNT, EALL, 2, 1365).reshape((SEQUENCE_COUNT, SLOT_COUNT, 2)),
        "pair_order": draw_pair_order(jax.random.fold_in(key_of[16], 71), 0),
        "gain_attn": jnp.clip(1.0 + 0.1 * jax.random.normal(key_of[5], (D,), jnp.float32), 0.5, 1.5).astype(jnp.bfloat16),
        "w_qkv": scatter_about(key_of[6], (D, 3, D), D ** -0.5, 0.21875, ((0, 16), (2, 2))),
        "w_out": scatter_about(key_of[7], (D, D), (max(1, D * 16 // SLOT_COUNT)) ** -0.5, 1.75, ((0, 16), (1, 2))),
        "gain_ffn": jnp.clip(1.0 + 0.1 * jax.random.normal(key_of[8], (D,), jnp.float32), 0.5, 1.5).astype(jnp.bfloat16),
        "w_router": scatter_about(key_of[9], (D, EALL), (4 * D) ** -0.5, 0.109375, ((0, 16),)),
        "w_residual": scatter_about(key_of[10], (EALL, EALL), (4 * EALL) ** -0.5, 0.875, (), jnp.float32),
        "w_const": scatter_about(key_of[11], (D, 4), D ** -0.5, 0.21875, ((0, 16),)),
        "const_vec": scatter_about(key_of[12], (D, 2), 1.0, 6.0, ((0, 16),)),
        "w_in": scatter_about(key_of[13], (D, NEXP, 2, FF), D ** -0.5, 0.21875, ((1, 2), (3, 16))),
        "w_down": scatter_about(key_of[14], (FF, NEXP, D), FF ** -0.5, 0.125, ((0, 16), (1, 2))),
        "cotangent": scatter_about(key_of[15], (SEQUENCE_COUNT, SLOT_COUNT, D), 1.0, 6.0, ((0, 2), (1, 16)), jnp.float32),
    }


EPS_NORM = 1e-05
NEG_BIG = -1e+30
TOP_PRECISION = lax.Precision.HIGHEST

@jax.custom_vjp
def low(v):
    return lax.optimization_barrier(v.astype(jnp.bfloat16)).astype(jnp.float32)

@jax.custom_vjp
def lower_backward(v):
    return v

def low_keep(v):
    return (low(v), None)

def low_pass(kept, grad):
    return (grad,)

def back_keep(v):
    return (v, None)

def back_low(kept, grad):
    return (low(grad),)
low.defvjp(low_keep, low_pass)
lower_backward.defvjp(back_keep, back_low)

def rotate_half(values):
    half_width = values.shape[-1] // 2
    return jnp.concatenate([-values[..., half_width:], values[..., :half_width]], axis=-1)

def rotary_tables(positions, head_dim):
    frequency = 10000.0 ** (-(2.0 * jnp.arange(head_dim // 2, dtype=jnp.float32)) / head_dim)
    angles = positions.astype(jnp.float32)[:, None] * frequency[None, :]
    angles = jnp.concatenate([angles, angles], axis=-1)
    return (jnp.cos(angles), jnp.sin(angles))

def apply_rotary(values, cosine, sine_tab):
    return values * cosine + rotate_half(values) * sine_tab

def place_pairs(route_pairs, order_pairs, valid_pairs, n_ffn, capacity):
    n_pairs = route_pairs.shape[0]
    eligible = valid_pairs & (route_pairs < n_ffn)
    inverse = jnp.zeros((n_pairs,), jnp.int32).at[order_pairs].set(jnp.arange(n_pairs, dtype=jnp.int32))
    sorted_route = route_pairs[inverse]
    sorted_elig = eligible[inverse]
    onehot = ((sorted_route[:, None] == jnp.arange(n_ffn, dtype=jnp.int32)[None, :]) & sorted_elig[:, None]).astype(jnp.int32)
    running = jnp.cumsum(onehot, axis=0, dtype=jnp.int32) - onehot
    rank_sorted = lax.optimization_barrier(jnp.sum(running * onehot, axis=1, dtype=jnp.int32))
    rank_pos = rank_sorted[order_pairs]
    kept_pair = eligible & (rank_pos < capacity)
    slot_index = jnp.where(kept_pair, route_pairs * capacity + rank_pos, n_ffn * capacity).astype(jnp.int32)
    source = jnp.full((n_ffn * capacity + 1,), n_pairs, jnp.int32).at[slot_index].set(jnp.arange(n_pairs, dtype=jnp.int32))
    return (slot_index, source[:n_ffn * capacity])

def to_blocks(array_in):
    trailing = array_in.shape[2:]
    shaped = array_in.reshape((SEQUENCE_COUNT // SEQ_DEV, SEQ_DEV, SLOT_COUNT // SLOT_DEV, SLOT_DEV) + trailing)
    shaped = jnp.moveaxis(shaped, 2, 1)
    return shaped.reshape((SEQUENCE_COUNT // SEQ_DEV * (SLOT_COUNT // SLOT_DEV), TOK_DEV) + trailing)

def from_blocks(array_in):
    trailing = array_in.shape[2:]
    shaped = array_in.reshape((SEQUENCE_COUNT // SEQ_DEV, SLOT_COUNT // SLOT_DEV, SEQ_DEV, SLOT_DEV) + trailing)
    shaped = jnp.moveaxis(shaped, 2, 1)
    return shaped.reshape((SEQUENCE_COUNT, SLOT_COUNT) + trailing)

def take_rows(rows_in, index_in):
    return rows_in[index_in]

def attend_rows(query_blk, key_seq, value_seq, seq_len, query_start):
    score_scale = 1.0 / math.sqrt(HD)
    scores = lower_backward(jnp.einsum('qhd,khd->hqk', query_blk, key_seq, precision=TOP_PRECISION) * score_scale)
    query_pos = query_start + jnp.arange(query_blk.shape[0], dtype=jnp.int32)
    key_pos = jnp.arange(key_seq.shape[0], dtype=jnp.int32)
    allowed = (key_pos[None, :] <= query_pos[:, None]) & (key_pos[None, :] < seq_len)
    scores = jnp.where(allowed[None], scores, NEG_BIG)
    prob_rows = jax.nn.softmax(scores, axis=-1)
    return jnp.einsum('hqk,khd->qhd', low(prob_rows), value_seq, precision=TOP_PRECISION)

def expert_apply(packed):
    rows_in, weight_in, weight_down = packed
    gate_up = lower_backward(jnp.dot(rows_in, weight_in, precision=TOP_PRECISION))
    hidden = low(jax.nn.silu(gate_up[:, :FF]) * gate_up[:, FF:])
    return low(lower_backward(jnp.dot(hidden, weight_down, precision=TOP_PRECISION)))

def reference(tokens, previous_layer_logits, lengths, routes, pair_order, gain_attn, w_qkv, w_out, gain_ffn, w_router, w_residual, w_const, const_vec, w_in, w_down, cotangent):
    valid_mask = jnp.arange(SLOT_COUNT, dtype=jnp.int32)[None, :] < lengths[:, None]
    n_blocks = SEQUENCE_COUNT // SEQ_DEV * (SLOT_COUNT // SLOT_DEV)
    pair_valid = jnp.repeat(to_blocks(valid_mask), 2, axis=1)
    route_blocks = to_blocks(routes).reshape(n_blocks, 2 * TOK_DEV)
    order_blocks = to_blocks(pair_order).reshape(n_blocks, 2 * TOK_DEV)
    slot_index, source = jax.vmap(partial(place_pairs, n_ffn=NEXP, capacity=CAP))(route_blocks, order_blocks, pair_valid)
    positions = jnp.arange(SLOT_COUNT, dtype=jnp.int32)
    cosine, sine_tab = rotary_tables(positions, HD)
    cos_wide = cosine[None, :, None, :]
    sin_wide = sine_tab[None, :, None, :]
    query_rows = math.gcd(SLOT_COUNT, 512)
    n_qblk = SLOT_COUNT // query_rows
    seq_ids = jnp.repeat(jnp.arange(SEQUENCE_COUNT, dtype=jnp.int32), n_qblk)
    starts = jnp.tile(jnp.arange(n_qblk, dtype=jnp.int32) * query_rows, SEQUENCE_COUNT)
    valid_wide = valid_mask[..., None].astype(jnp.float32)

    def forward_pass(token_broadcast, gain_one, query_key_value_weight, out_w, gain_two, router_weight, residual_weight, constant_weight, vector_w, in_w, down_w):
        first_inverse_deviation = lax.rsqrt(lax.optimization_barrier(jnp.mean(token_broadcast * token_broadcast, axis=-1, keepdims=True)) + EPS_NORM)
        first_normalized = low(token_broadcast * first_inverse_deviation * gain_one)
        query_key_value_plain = lower_backward(jnp.einsum('owj,jtm->owtm', first_normalized, query_key_value_weight, precision=TOP_PRECISION))
        qkv_heads = query_key_value_plain.reshape(SEQUENCE_COUNT, SLOT_COUNT, 3, NH, HD)
        query_rot = low(apply_rotary(qkv_heads[:, :, 0], cos_wide, sin_wide))
        key_rot = low(apply_rotary(qkv_heads[:, :, 1], cos_wide, sin_wide))
        value_low = low(qkv_heads[:, :, 2])
        query_blocks = query_rot.reshape(SEQUENCE_COUNT * n_qblk, query_rows, NH, HD)

        def one_block(packed):
            query_blk, seq_id, query_start = packed
            key_seq = lax.dynamic_index_in_dim(key_rot, seq_id, 0, keepdims=False)
            value_seq = lax.dynamic_index_in_dim(value_low, seq_id, 0, keepdims=False)
            seq_len = lax.dynamic_index_in_dim(lengths, seq_id, 0, keepdims=False)
            return attend_rows(query_blk, key_seq, value_seq, seq_len, query_start)
        attn_vec = lax.map(jax.checkpoint(one_block), (query_blocks, seq_ids, starts)).reshape(SEQUENCE_COUNT, SLOT_COUNT, NH * HD)
        attn_low = low(lower_backward(attn_vec))
        attn_out = lower_backward(jnp.einsum('slc,jc->slj', attn_low, out_w, precision=TOP_PRECISION))
        residual = token_broadcast + attn_out
        second_inverse_deviation = lax.rsqrt(lax.optimization_barrier(jnp.mean(residual * residual, axis=-1, keepdims=True)) + EPS_NORM)
        normed_two = residual * second_inverse_deviation * gain_two
        normalized_lower = low(normed_two)
        router_scores = lower_backward(jnp.einsum('rmi,ix->rmx', normalized_lower, router_weight, precision=TOP_PRECISION) + jnp.einsum('cjp,pi->cji', previous_layer_logits, residual_weight, precision=TOP_PRECISION))
        chosen = jnp.take_along_axis(router_scores, routes, axis=-1)
        gate_probs = jax.nn.softmax(chosen, axis=-1)
        constant_logits = lower_backward(jnp.einsum('tpu,uz->tpz', normalized_lower, constant_weight, precision=TOP_PRECISION)).reshape(SEQUENCE_COUNT, SLOT_COUNT, 2, 2)
        alpha_mix = jax.nn.softmax(constant_logits, axis=-1)
        const_zero = alpha_mix[..., 0, 0:1] * normed_two + alpha_mix[..., 0, 1:2] * vector_w[:, 0]
        const_one = alpha_mix[..., 1, 0:1] * normed_two + alpha_mix[..., 1, 1:2] * vector_w[:, 1]
        low_blocks = to_blocks(normalized_lower)
        ext_rows = jnp.concatenate([low_blocks, jnp.zeros((n_blocks, 1, D), jnp.float32)], axis=1)
        dispatch = lower_backward(jax.vmap(take_rows)(ext_rows, source // 2))
        per_expert = jnp.moveaxis(dispatch.reshape(n_blocks, NEXP, CAP, D), 1, 0).reshape(NEXP, n_blocks * CAP, D)
        in_stack = jnp.moveaxis(in_w, 1, 0).reshape(NEXP, D, 2 * FF)
        expert_out = lax.map(jax.checkpoint(expert_apply), (per_expert, in_stack, jnp.moveaxis(down_w, 1, 0)))
        back_rows = jnp.moveaxis(expert_out.reshape(NEXP, n_blocks, CAP, D), 0, 1).reshape(n_blocks, NEXP * CAP, D)
        back_ext = jnp.concatenate([back_rows, jnp.zeros((n_blocks, 1, D), jnp.float32)], axis=1)
        ffn_pairs = from_blocks(jax.vmap(take_rows)(back_ext, slot_index).reshape(n_blocks, TOK_DEV, 2, D))
        route_wide = routes[..., None]
        pair_out = jnp.where(route_wide < NEXP, ffn_pairs, 0.0) + jnp.where(route_wide == NEXP + 1, normed_two[:, :, None, :], 0.0) + jnp.where(route_wide == NEXP + 2, const_zero[:, :, None, :], 0.0) + jnp.where(route_wide == NEXP + 3, const_one[:, :, None, :], 0.0)
        mixed_out = lax.optimization_barrier(jnp.sum(gate_probs[..., None] * pair_out, axis=2))
        return valid_wide * (residual + mixed_out)
    primal_in = (tokens.astype(jnp.float32), gain_attn.astype(jnp.float32), w_qkv.astype(jnp.float32), w_out.astype(jnp.float32), gain_ffn.astype(jnp.float32), w_router.astype(jnp.float32), w_residual, w_const.astype(jnp.float32), const_vec.astype(jnp.float32), w_in.astype(jnp.float32), w_down.astype(jnp.float32))
    output, pullback = jax.vjp(forward_pass, *primal_in)
    gradients = pullback(cotangent)
    return (output, gradients[0], gradients[1], gradients[2], gradients[3], gradients[4], gradients[5], gradients[6], gradients[7], gradients[8], gradients[9], gradients[10])
```

```python
import functools
import math

import jax
import jax.numpy as jnp
from jax import lax
from jax.experimental import pallas as pl
from jax.experimental.pallas import tpu as pltpu
from jax.sharding import PartitionSpec as P

HD = 64
NEXP = 8
EPS = 1e-05
NEG = -1e30
BF = jnp.bfloat16
F32 = jnp.float32
MIB = 1 << 20
ANY2 = (((1,), (1,)), ((), ()))
MM = (((1,), (0,)), ((), ()))
C_CONST, C_VEC, C_GAIN1, C_GAIN2 = 12, 16, 18, 19


def dot(a, b, dims=MM):
    return lax.dot_general(a, b, dims, preferred_element_type=F32)


def call(kernel, outs, args, smem=0, scratch=(), limit=40, flops=0, name=None):
    vm = pl.BlockSpec(memory_space=pltpu.VMEM)
    sm = pl.BlockSpec(memory_space=pltpu.SMEM)
    total = sum(math.prod(a.shape) * a.dtype.itemsize for a in list(args) + list(outs))
    return pl.pallas_call(
        kernel,
        out_shape=tuple(outs),
        in_specs=[sm] * smem + [vm] * (len(args) - smem),
        out_specs=tuple([vm] * len(outs)),
        scratch_shapes=list(scratch),
        compiler_params=pltpu.CompilerParams(vmem_limit_bytes=limit * MIB),
        cost_estimate=pl.CostEstimate(flops=flops, bytes_accessed=total, transcendentals=0),
        name=name,
    )(*args)


def sds(shape, dtype):
    return jax.ShapeDtypeStruct(shape, dtype)


def lower_lanes(shape):
    return (lax.broadcasted_iota(jnp.int32, shape, 1) & 63) < 32


def turned(values):
    return jnp.where(
        lower_lanes(values.shape), -pltpu.roll(values, 96, 1), pltpu.roll(values, 32, 1)
    )


def qkv_kernel(idx, mine, other, wpack, cos, sin, send, xn, small, xall):
    h = idx[0]
    rows = mine.shape[0]
    xall[pl.ds(h * rows, rows), :] = mine[...]
    xall[pl.ds((1 - h) * rows, rows), :] = other[...]
    width = mine.shape[1]
    small_t = jnp.transpose(wpack[:, wpack.shape[1] - 128 :].astype(F32))
    small[...] = small_t[: small.shape[0]]
    x = xall[...].astype(F32)
    rstd = lax.rsqrt(jnp.mean(x * x, axis=-1, keepdims=True) + EPS)
    normed = (x * rstd * small_t[C_GAIN1 : C_GAIN1 + 1]).astype(BF)
    xn[...] = normed
    part = (wpack.shape[1] - 128) // 4
    pairs = part // 128
    y = dot(normed, wpack[:, : 3 * part])
    slots = cos.shape[0]
    n_seq = xall.shape[0] // slots
    c = jnp.concatenate([cos[...]] * n_seq, axis=0)
    s = jnp.concatenate([sin[...]] * n_seq, axis=0)
    for p in range(pairs):
        for k in range(3):
            piece = y[:, k * part + p * 128 : k * part + (p + 1) * 128]
            if k < 2:
                piece = piece * c + turned(piece) * s
            if k == 0:
                piece = piece * (1.0 / math.sqrt(HD))
            piece = piece.astype(BF)
            for q in range(n_seq):
                send[p * n_seq + q, :, k * 128 : (k + 1) * 128] = piece[q * slots : (q + 1) * slots]
    used = pairs * n_seq
    if send.shape[0] > used:
        send[used:] = jnp.zeros((send.shape[0] - used,) + send.shape[1:], BF)


def head_mask(shape, which):
    lane = lax.broadcasted_iota(jnp.int32, shape, 1)
    return (lane >= 64) if which else (lane < 64)


def only(values, which):
    return jnp.where(head_mask(values.shape, which), values, jnp.zeros_like(values))


def scores_of(k_rows, q_head, first_query, limit_len):
    s = dot(k_rows, q_head, ANY2)
    key = lax.broadcasted_iota(jnp.int32, s.shape, 0)
    query = lax.broadcasted_iota(jnp.int32, (1, s.shape[1]), 1) + first_query
    last = jnp.minimum(query, limit_len - 1)
    return jnp.where(key <= last, s, NEG)


def each_block(total, block, fn):
    if total // block <= 4:
        for i in range(total // block):
            fn(i * block, (i + 1) * block)
    else:

        @pl.loop(0, total // block)
        def _(i):
            fn(pl.multiple_of(i * block, block), total)


def attend_kernel(idx, qkv, out, lse, vt):
    total = qkv.shape[0]
    block = 256
    limit_len = idx[1]
    vt[...] = jnp.transpose(qkv[:, 256:384])

    def step(start, n_keys):
        q = qkv[pl.ds(start, block), 0:128]
        parts = []
        for h in range(2):
            s = scores_of(qkv[0:n_keys, 128:256], only(q, h), start, limit_len)
            m = jnp.max(s, axis=0, keepdims=True)
            p = jnp.exp(s - m)
            total_p = jnp.sum(p, axis=0, keepdims=True)
            o = dot(vt[h * 64 : (h + 1) * 64, 0:n_keys], p.astype(BF))
            parts.append(o / total_p)
            lse[h : h + 1, pl.ds(start, block)] = m + jnp.log(total_p)
        out[pl.ds(start, block), :] = jnp.transpose(jnp.concatenate(parts, axis=0)).astype(BF)

    each_block(total, block, step)


def attend_back_kernel(idx, qkv, dout, out, lse, cos, sin, grad, kt, dk, dv):
    total = qkv.shape[0]
    block = 256
    limit_len = idx[1]
    kt[...] = jnp.transpose(qkv[:, 128:256])
    dk[...] = jnp.zeros_like(dk)
    dv[...] = jnp.zeros_like(dv)

    def unrotate(values, at, size):
        c, s = cos[pl.ds(at, size), :], sin[pl.ds(at, size), :]
        return values * c - turned(values) * s

    def step(start, n_keys):
        q = qkv[pl.ds(start, block), 0:128]
        do = dout[pl.ds(start, block), :]
        prod_t = jnp.transpose(do.astype(F32) * out[pl.ds(start, block), :].astype(F32))
        probs, ds, dq = [], [], []
        for h in range(2):
            q_head, do_head = only(q, h), only(do, h)
            s = scores_of(qkv[0:n_keys, 128:256], q_head, start, limit_len)
            p = jnp.exp(s - lse[h : h + 1, pl.ds(start, block)])
            delta = jnp.sum(prod_t[h * 64 : (h + 1) * 64], axis=0, keepdims=True)
            dp = dot(qkv[0:n_keys, 256:384], do_head, ANY2)
            d = (p * (dp - delta)).astype(BF)
            probs.append(p.astype(BF))
            ds.append(d)
            dq.append(dot(kt[h * 64 : (h + 1) * 64, 0:n_keys], d))
        both_q = jnp.concatenate([only(q, 0), only(q, 1)], axis=0)
        both_do = jnp.concatenate([only(do, 0), only(do, 1)], axis=0)
        dv[0:n_keys, :] += dot(jnp.concatenate(probs, axis=1), both_do)
        dk[0:n_keys, :] += dot(jnp.concatenate(ds, axis=1), both_q)
        gq = jnp.transpose(jnp.concatenate(dq, axis=0)) * (1.0 / math.sqrt(HD))
        grad[pl.ds(start, block), 0:128] = unrotate(gq, start, block).astype(BF)

    each_block(total, block, step)

    def finish(start, _):
        at = pl.ds(start, block)
        grad[at, 128:256] = unrotate(dk[at, :], start, block).astype(BF)
        grad[at, 256:384] = dv[at, :].astype(BF)

    each_block(total, block, finish)


def out_kernel(idx, recv, wpack, mine, other, attn, full):
    h = idx[0]
    part = attn.shape[1]
    n_seq = attn.shape[0] // recv.shape[1]
    for p in range(part // 128):
        rows = recv[p * n_seq : (p + 1) * n_seq].reshape(attn.shape[0], 128)
        attn[:, p * 128 : (p + 1) * 128] = rows
    full[...] = dot(attn[...], wpack[:, 3 * part : 4 * part], ANY2)
    rows = mine.shape[0]
    mine[...] = full[pl.ds(h * rows, rows), :]
    other[...] = full[pl.ds((1 - h) * rows, rows), :].astype(BF)


def onehot_rows(slots, n_rows):
    at = lax.broadcasted_iota(jnp.int32, (n_rows, slots.shape[1]), 0)
    return jnp.where((at == slots[0:1]) | (at == slots[1:2]), 1.0, 0.0).astype(BF)


def spread(rows, send):
    per = send.shape[1]
    copies = send.shape[0] * per // rows.shape[0]
    for i in range(send.shape[0]):
        at = (i // copies) * per
        send[i] = rows[at : at + per]


def send_grad_kernel(slots, cot, ints, send):
    g = (cot[...] * ints[:, 4:5].astype(F32)).astype(BF)
    n_rows = send.shape[1] * 2
    spread(dot(onehot_rows(slots[...], n_rows), g).astype(BF), send)


def norm_two(residual, gain):
    rstd = lax.rsqrt(jnp.mean(residual * residual, axis=-1, keepdims=True) + EPS)
    xhat = residual * rstd
    return rstd, xhat, xhat * gain


def route_kernel(tokens, mine, other, wpack, small, prev_logits, ints, slots, send, residual, aux):
    res = tokens[...].astype(F32) + mine[...] + other[...].astype(F32)
    residual[...] = res
    _, _, normed = norm_two(res, small[C_GAIN2 : C_GAIN2 + 1])
    low = normed.astype(BF)
    logits = dot(low, wpack[:, wpack.shape[1] - 128 :]) + prev_logits[...]
    lane = lax.broadcasted_iota(jnp.int32, logits.shape, 1)

    def pick(which):
        return jnp.sum(jnp.where(lane == which, logits, 0.0), axis=1, keepdims=True)

    def pair_softmax(a, b):
        top = jnp.maximum(a, b)
        ea, eb = jnp.exp(a - top), jnp.exp(b - top)
        return ea / (ea + eb), eb / (ea + eb)

    p0, p1 = pair_softmax(pick(ints[:, 0:1]), pick(ints[:, 1:2]))
    a00, a01 = pair_softmax(pick(C_CONST), pick(C_CONST + 1))
    a10, a11 = pair_softmax(pick(C_CONST + 2), pick(C_CONST + 3))
    info = jnp.zeros_like(logits)
    for i, v in enumerate((p0, p1, a00, a01, a10, a11)):
        info = jnp.where(lane == i, v, info)
    aux[...] = info
    n_rows = send.shape[1] * 2
    tok = slots.shape[1]
    at = lax.broadcasted_iota(jnp.int32, (n_rows, tok), 0)
    first = jnp.where(at == slots[0:1], 1.0, 0.0).astype(BF)
    second = jnp.where(at == slots[1:2], 1.0, 0.0).astype(BF)

    def split(v, base):
        high = v.astype(BF).astype(F32)
        return jnp.where(lane == 0, high, jnp.where(lane == 1, v - high, base))

    extra = dot(first, split(p0, 0.0).astype(BF)) + dot(second, split(p1, 0.0).astype(BF))
    rows = jnp.concatenate([dot(first + second, low), extra], axis=1)
    spread(rows.astype(BF), send)


def expert_kernel(n_pieces, x_ref, g_ref, *refs):
    wi, wd = refs[:n_pieces], refs[n_pieces : 2 * n_pieces]
    rest = refs[2 * n_pieces :]
    back = rest[0]
    gi, gd = rest[1 : 1 + n_pieces], rest[1 + n_pieces : 1 + 2 * n_pieces]
    acc_i, acc_d, wd_all = rest[1 + 2 * n_pieces :]
    step = pl.program_id(0)
    width = g_ref.shape[1]
    unit = wd[0].shape[0]

    @pl.when(step == 0)
    def _():
        acc_i[...] = jnp.zeros_like(acc_i)
        acc_d[...] = jnp.zeros_like(acc_d)
        for d in range(n_pieces):
            wd_all[d * unit : (d + 1) * unit, :] = wd[d][...]

    x = x_ref[:, :width]
    g = g_ref[...]
    prob = jnp.sum(x_ref[:, width:].astype(F32), axis=1, keepdims=True)
    xt = jnp.transpose(x)
    up_grad = dot(g, wd_all[...], ANY2) * prob
    hiddens = []
    grad_in = jnp.zeros((x.shape[0], width), F32)
    for d in range(n_pieces):
        both = dot(x, wi[d][...])
        gate, up = both[:, :unit], both[:, unit:]
        sig = 1.0 / (1.0 + jnp.exp(-gate))
        act = gate * sig
        hiddens.append((act * up).astype(BF))
        gh = up_grad[:, d * unit : (d + 1) * unit]
        g_gate = gh * up * sig * (1.0 + gate * (1.0 - sig))
        g_both = jnp.concatenate([g_gate, gh * act], axis=1).astype(BF)
        grad_in += dot(g_both, wi[d][...], ANY2)
        acc_i[d] += dot(xt, g_both)
    hidden = jnp.concatenate(hiddens, axis=1)
    back[:, :width] = dot(hidden, wd_all[...]).astype(BF)
    back[:, width:] = grad_in.astype(BF)
    g_scaled = (g.astype(F32) * prob).astype(BF)
    acc_d[...] += dot(jnp.transpose(hidden), g_scaled)

    @pl.when(step == pl.num_programs(0) - 1)
    def _():
        for d in range(n_pieces):
            gi[d][...] = acc_i[d].astype(BF)
            gd[d][...] = acc_d[d * unit : (d + 1) * unit, :].astype(BF)


def experts(x_rows, g_rows, w_in_pieces, w_down_pieces):
    n = len(w_in_pieces)
    rows, wide = x_rows.shape
    width = g_rows.shape[1]
    unit = w_down_pieces[0].shape[0]
    block = 256 if rows % 256 == 0 else rows
    whole = lambda a: pl.BlockSpec(a.shape, lambda i: (0,) * len(a.shape))
    outs = (
        [sds((rows, 2 * width), BF)]
        + [sds((width, 2 * unit), BF)] * n
        + [sds((unit, width), BF)] * n
    )
    flops = 18 * rows * width * unit * n
    return pl.pallas_call(
        functools.partial(expert_kernel, n),
        grid=(rows // block,),
        in_specs=[
            pl.BlockSpec((block, wide), lambda i: (i, 0)),
            pl.BlockSpec((block, width), lambda i: (i, 0)),
        ]
        + [whole(a) for a in w_in_pieces]
        + [whole(a) for a in w_down_pieces],
        out_specs=tuple(
            [pl.BlockSpec((block, 2 * width), lambda i: (i, 0))] + [whole(o) for o in outs[1:]]
        ),
        out_shape=tuple(outs),
        scratch_shapes=[
            pltpu.VMEM((n, width, 2 * unit), F32),
            pltpu.VMEM((n * unit, width), F32),
            pltpu.VMEM((n * unit, width), BF),
        ],
        compiler_params=pltpu.CompilerParams(vmem_limit_bytes=48 * MIB),
        cost_estimate=pl.CostEstimate(
            flops=flops, bytes_accessed=8 * rows * width + 12 * width * unit * n, transcendentals=0
        ),
        name="experts",
    )(x_rows, g_rows, *w_in_pieces, *w_down_pieces)


def combine_kernel(recv, residual, cot, small, wpack, ints, aux, prev, out, grad_res, grad_low, sums, resid):
    res = residual[...]
    gain = small[C_GAIN2 : C_GAIN2 + 1]
    rstd, xhat, normed = norm_two(res, gain)
    low = normed.astype(BF)
    width = res.shape[1]
    heads = 2
    copies = recv.shape[0] // heads
    groups = []
    for h in range(heads):
        total = recv[h * copies].astype(F32)
        for r in range(1, copies):
            total = total + recv[h * copies + r].astype(F32)
        groups.append(total.astype(BF))
    rows = jnp.concatenate(groups, axis=0)
    valid = ints[:, 4:5].astype(F32)
    go = cot[...] * valid
    lane = lax.broadcasted_iota(jnp.int32, (res.shape[0], rows.shape[0]), 1)
    first = jnp.where(lane == ints[:, 2:3], 1.0, 0.0).astype(BF)
    second = jnp.where(lane == ints[:, 3:4], 1.0, 0.0).astype(BF)
    eo0 = dot(first, rows[:, :width])
    eo1 = dot(second, rows[:, :width])
    gin = dot(first + second, rows[:, width:])
    info = aux[...]
    p0, p1 = info[:, 0:1], info[:, 1:2]
    alpha = ((info[:, 2:3], info[:, 3:4]), (info[:, 4:5], info[:, 5:6]))
    r0, r1 = ints[:, 0:1], ints[:, 1:2]

    def at(route, which):
        return jnp.where(route == which, 1.0, 0.0)

    vec = (small[C_VEC : C_VEC + 1], small[C_VEC + 1 : C_VEC + 2])
    share0 = at(r0, NEXP + 1) + at(r0, NEXP + 2) * alpha[0][0] + at(r0, NEXP + 3) * alpha[1][0]
    share1 = at(r1, NEXP + 1) + at(r1, NEXP + 2) * alpha[0][0] + at(r1, NEXP + 3) * alpha[1][0]
    weight = [p0 * at(r0, NEXP + 2 + j) + p1 * at(r1, NEXP + 2 + j) for j in range(2)]
    mixed = (
        p0 * eo0
        + p1 * eo1
        + (p0 * share0 + p1 * share1) * normed
        + (weight[0] * alpha[0][1]) * vec[0]
        + (weight[1] * alpha[1][1]) * vec[1]
    )
    out[...] = valid * (res + mixed)

    def rowsum(v):
        return jnp.sum(v, axis=1, keepdims=True)

    s_norm = rowsum(go * normed)
    s_vec = [rowsum(go * vec[j]) for j in range(2)]
    gg0 = rowsum(go * eo0) + share0 * s_norm
    gg1 = rowsum(go * eo1) + share1 * s_norm
    for j in range(2):
        gg0 = gg0 + at(r0, NEXP + 2 + j) * alpha[j][1] * s_vec[j]
        gg1 = gg1 + at(r1, NEXP + 2 + j) * alpha[j][1] * s_vec[j]
    gsum = p0 * gg0 + p1 * gg1
    c0, c1 = p0 * (gg0 - gsum), p1 * (gg1 - gsum)
    wide = lax.broadcasted_iota(jnp.int32, (res.shape[0], 128), 1)
    dl = jnp.where(wide == r0, c0, 0.0) + jnp.where(wide == r1, c1, 0.0)
    coef = p0 * at(r0, NEXP + 1) + p1 * at(r1, NEXP + 1)
    vec_rows = []
    for j in range(2):
        ga0, ga1 = weight[j] * s_norm, weight[j] * s_vec[j]
        mean = alpha[j][0] * ga0 + alpha[j][1] * ga1
        dl = jnp.where(wide == C_CONST + 2 * j, alpha[j][0] * (ga0 - mean), dl)
        dl = jnp.where(wide == C_CONST + 2 * j + 1, alpha[j][1] * (ga1 - mean), dl)
        coef = coef + alpha[j][0] * weight[j]
        vec_rows.append(jnp.sum((alpha[j][1] * weight[j]) * go, axis=0, keepdims=True))
    dl = dl.astype(BF)
    dlt = jnp.transpose(dl)
    proj = dot(dlt, low)
    resid[...] = dot(jnp.transpose(prev[...]), dl.astype(F32), MM) if False else lax.dot_general(
        jnp.transpose(prev[...]), dl.astype(F32), MM, precision=lax.Precision.HIGHEST,
        preferred_element_type=F32,
    )
    gn = gin + coef * go + dot(dl, wpack[:, wpack.shape[1] - 128 :], ANY2)
    gain_row = jnp.sum(gn * xhat, axis=0, keepdims=True)
    row = lax.broadcasted_iota(jnp.int32, (sums.shape[0], 1), 0)
    table = jnp.where(row < C_VEC, proj[: sums.shape[0]], 0.0)
    table = jnp.where(row == C_VEC, vec_rows[0], table)
    table = jnp.where(row == C_VEC + 1, vec_rows[1], table)
    sums[...] = jnp.where(row == C_GAIN2, gain_row, table)
    ghat = gn * gain
    grad = go + rstd * (ghat - xhat * jnp.mean(ghat * xhat, axis=-1, keepdims=True))
    grad_res[...] = grad
    grad_low[...] = grad.astype(BF)


def grad_vec_kernel(idx, mine, other, attn, wpack, send, dw, both):
    h = idx[0]
    rows = mine.shape[0]
    both[pl.ds(h * rows, rows), :] = mine[...]
    both[pl.ds((1 - h) * rows, rows), :] = other[...]
    part = attn.shape[1]
    g = both[...]
    gv = dot(g, wpack[:, 3 * part : 4 * part]).astype(BF)
    slots = send.shape[1]
    n_seq = g.shape[0] // slots
    for p in range(part // 128):
        for s in range(n_seq):
            send[p * n_seq + s] = gv[s * slots : (s + 1) * slots, p * 128 : (p + 1) * 128]
    used = part // 128 * n_seq
    if send.shape[0] > used:
        send[used:] = jnp.zeros((send.shape[0] - used,) + send.shape[1:], BF)
    dw[...] = dot(jnp.transpose(g), attn[...]).astype(BF)


def grad_qkv_kernel(idx, recv, xn, wpack, mine, other, dw, both, full):
    h = idx[0]
    part = both.shape[1] // 3
    n_seq = both.shape[0] // recv.shape[1]
    for p in range(part // 128):
        rows = recv[p * n_seq : (p + 1) * n_seq].reshape(both.shape[0], 384)
        for k in range(3):
            at = k * part + p * 128
            both[:, at : at + 128] = rows[:, k * 128 : (k + 1) * 128]
    g = both[...]
    full[...] = dot(g, wpack[:, : 3 * part], ANY2)
    rows = mine.shape[0]
    mine[...] = full[pl.ds(h * rows, rows), :]
    other[...] = full[pl.ds((1 - h) * rows, rows), :].astype(BF)
    dw[...] = dot(jnp.transpose(xn[...]), g).astype(BF)


def final_kernel(tokens, mine, other, grad_res, small, grad, gain_row):
    x = tokens[...].astype(F32)
    rstd = lax.rsqrt(jnp.mean(x * x, axis=-1, keepdims=True) + EPS)
    xhat = x * rstd
    gn = mine[...] + other[...].astype(F32)
    gain_row[...] = jnp.broadcast_to(jnp.sum(gn * xhat, axis=0, keepdims=True), gain_row.shape)
    ghat = gn * small[C_GAIN1 : C_GAIN1 + 1]
    grad[...] = grad_res[...] + rstd * (
        ghat - xhat * jnp.mean(ghat * xhat, axis=-1, keepdims=True)
    )


def per_device(
    tokens, previous_layer_logits, lengths, routes, pair_order, gain_attn, w_qkv, w_out, gain_ffn,
    w_router, w_residual, w_const, const_vec, w_in, w_down, cotangent,
):
    seq_dev, slot_dev, width = tokens.shape
    n_all = previous_layer_logits.shape[2]
    tok = seq_dev * slot_dev
    heads = lax.axis_size("head")
    n_blk = lax.axis_size("blk")
    n_seq = seq_dev * heads
    n_slots = slot_dev * n_blk
    e_loc = w_in.shape[1]
    n_share = n_blk // e_loc
    unit = w_in.shape[3]
    rows_here = gain_attn.shape[0]
    part = w_qkv.shape[2]
    capacity = 9 * 2 * tok // (8 * n_all)
    h = lax.axis_index("head")
    b = lax.axis_index("blk")
    q = b % e_loc
    swap = [(0, 1), (1, 0)]
    everyone = ("head", "blk")

    def across(x):
        return lax.ppermute(x, "head", swap)

    def hop(x, d):
        return lax.ppermute(x, "blk", [(i, i ^ d) for i in range(n_blk)]) if d else x

    small_cols = jnp.concatenate(
        [w_router, w_const, const_vec, gain_attn[:, None], gain_ffn[:, None],
         jnp.zeros((rows_here, 128 - 20), BF)], axis=1)
    packed = jnp.concatenate([w_qkv.reshape(rows_here, 3 * part), w_out, small_cols], axis=1)
    wpack = lax.all_gather(packed, "blk", axis=0, tiled=True)
    flat_tokens = tokens.reshape(tok, width)
    other_tokens = across(flat_tokens)

    positions = b * slot_dev + jnp.arange(slot_dev, dtype=jnp.int32)
    own_len = lax.dynamic_slice_in_dim(lengths, h * seq_dev, seq_dev)
    valid = (positions[None, :] < own_len[:, None]).reshape(tok)
    route_rows = jnp.transpose(routes.reshape(tok, 2))
    order = jnp.transpose(pair_order.reshape(tok, 2)).reshape(2 * tok)
    route = route_rows.reshape(2 * tok)
    eligible = jnp.concatenate([valid, valid]) & (route < NEXP)
    before = (
        (route[:, None] == route[None, :]) & (order[None, :] < order[:, None]) & eligible[None, :]
    )
    rank = jnp.sum(before.astype(jnp.int32), axis=1)
    slot = jnp.where(eligible & (rank < capacity), route * capacity + rank, NEXP * capacity)
    slot = slot.reshape(2, tok)
    slot_rows = jnp.concatenate([slot, jnp.zeros((6, tok), jnp.int32)], axis=0)
    ints = jnp.concatenate(
        [routes.reshape(tok, 2), jnp.transpose(slot), valid[:, None].astype(jnp.int32),
         jnp.zeros((tok, 3), jnp.int32)], axis=1)

    cot = cotangent.reshape(tok, width)
    per_send = e_loc * capacity
    (send_g,) = call(
        send_grad_kernel, [sds((heads * n_share, per_send, width), BF)], [slot_rows, cot, ints],
        name="send_grad")

    def to_experts(rows):
        flat = rows.reshape(heads * n_blk * capacity, rows.shape[-1])
        return lax.all_to_all(flat, everyone, 0, 0, tiled=True)

    g_rows = to_experts(send_g)

    in_by_expert = jnp.transpose(w_in, (1, 0, 2, 3)).reshape(e_loc, width, 2 * unit)
    down_by_expert = jnp.transpose(w_down, (1, 0, 2))
    in_pieces = [
        hop(lax.dynamic_index_in_dim(in_by_expert, q ^ d, 0, keepdims=False), d) for d in range(e_loc)]
    down_pieces = [
        hop(lax.dynamic_index_in_dim(down_by_expert, q ^ d, 0, keepdims=False), d) for d in range(e_loc)]
    joined = unit % 128 != 0
    if joined:
        cube = [p.reshape(width, 2, unit) for p in in_pieces]
        in_pieces = [jnp.concatenate(cube, axis=2).reshape(width, 2 * unit * e_loc)]
        down_pieces = [jnp.concatenate(down_pieces, axis=0)]

    frequency = 10000.0 ** (-(2.0 * jnp.arange(HD // 2, dtype=F32)) / HD)
    angles = jnp.arange(n_slots, dtype=jnp.int32).astype(F32)[:, None] * frequency[None, :]
    cos_all = jnp.concatenate([jnp.cos(angles)] * 4, axis=1)
    sin_all = jnp.concatenate([jnp.sin(angles)] * 4, axis=1)
    cos_here = lax.dynamic_slice_in_dim(cos_all, b * slot_dev, slot_dev)
    sin_here = lax.dynamic_slice_in_dim(sin_all, b * slot_dev, slot_dev)
    idx = jnp.stack([h, lax.dynamic_index_in_dim(lengths, b % n_seq, 0, keepdims=False)])
    prev = previous_layer_logits.reshape(tok, n_all)
    prev_wide = jnp.pad(prev, ((0, 0), (0, 128 - n_all)))
    prev_logits = jnp.pad(
        jnp.dot(prev, w_residual, precision=lax.Precision.HIGHEST), ((0, 0), (0, 128 - n_all)))

    send_qkv, xn, small = call(
        qkv_kernel,
        [sds((n_blk, slot_dev, 384), BF), sds((n_seq * slot_dev, width), BF), sds((24, width), F32)],
        [idx, flat_tokens, other_tokens, wpack, cos_here, sin_here], smem=1,
        scratch=[pltpu.VMEM((n_seq * slot_dev, width), BF)],
        flops=2 * n_seq * slot_dev * width * 3 * part, name="qkv")

    def exchange(x):
        flat = x.reshape(n_blk * slot_dev, x.shape[-1])
        return lax.all_to_all(flat, "blk", 0, 0, tiled=True)

    qkv = exchange(send_qkv)
    attn_unit, lse = call(
        attend_kernel, [sds((n_slots, 128), BF), sds((8, n_slots), F32)], [idx, qkv], smem=1,
        scratch=[pltpu.VMEM((128, n_slots), BF)], flops=2 * n_slots * n_slots * 512, name="attend")
    attn_recv = exchange(attn_unit).reshape(n_blk, slot_dev, 128)
    mine, other, attn_low = call(
        out_kernel,
        [sds((tok, width), F32), sds((tok, width), BF), sds((n_seq * slot_dev, part), BF)],
        [idx, attn_recv, wpack], smem=1, scratch=[pltpu.VMEM((n_seq * slot_dev, width), F32)],
        flops=2 * n_seq * slot_dev * width * part, name="out")
    send_x, residual, aux = call(
        route_kernel,
        [sds((heads * n_share, per_send, width + 128), BF), sds((tok, width), F32), sds((tok, 128), F32)],
        [flat_tokens, mine, across(other), wpack, small, prev_logits, ints, slot_rows],
        flops=tok * width * 1000, name="route")
    x_rows = to_experts(send_x)
    n = 1 if joined else e_loc
    results = experts(x_rows, g_rows, in_pieces, down_pieces)
    back_rows, grad_in_pieces, grad_down_pieces = results[0], results[1 : 1 + n], results[1 + n :]
    recv = to_experts(back_rows).reshape(heads * n_share, per_send, 2 * width)

    if joined:
        cube = grad_in_pieces[0].reshape(width, 2, e_loc, unit)
        grad_in_pieces = [cube[:, :, d].reshape(width, 2 * unit) for d in range(e_loc)]
        grad_down_pieces = [grad_down_pieces[0][d * unit : (d + 1) * unit] for d in range(e_loc)]
    came_in = [hop(grad_in_pieces[d], d) for d in range(e_loc)]
    came_down = [hop(grad_down_pieces[d], d) for d in range(e_loc)]

    output, grad_res, grad_low, sums, resid = call(
        combine_kernel,
        [sds((tok, width), F32), sds((tok, width), F32), sds((tok, width), BF), sds((24, width), F32),
         sds((128, 128), F32)],
        [recv, residual, cot, small, wpack, ints, aux, prev_wide], flops=tok * width * 2000,
        name="combine")

    send_gv, dw_out = call(
        grad_vec_kernel, [sds((n_blk, slot_dev, 128), BF), sds((width, part), BF)],
        [idx, grad_low, across(grad_low), attn_low, wpack], smem=1,
        scratch=[pltpu.VMEM((n_seq * slot_dev, width), BF)],
        flops=4 * n_seq * slot_dev * width * part, name="grad_vec")
    dout = exchange(send_gv)
    (grad_unit,) = call(
        attend_back_kernel, [sds((n_slots, 384), BF)],
        [idx, qkv, dout, attn_unit, lse, cos_all, sin_all], smem=1,
        scratch=[pltpu.VMEM((128, n_slots), BF), pltpu.VMEM((n_slots, 128), F32),
                 pltpu.VMEM((n_slots, 128), F32)],
        flops=5 * n_slots * n_slots * 256, name="attend_back")
    grad_recv = exchange(grad_unit).reshape(n_blk, slot_dev, 384)
    gn_mine, gn_other, dw_qkv = call(
        grad_qkv_kernel,
        [sds((tok, width), F32), sds((tok, width), BF), sds((width, 3 * part), BF)],
        [idx, grad_recv, xn, wpack], smem=1,
        scratch=[pltpu.VMEM((n_seq * slot_dev, 3 * part), BF),
                 pltpu.VMEM((n_seq * slot_dev, width), F32)],
        flops=4 * n_seq * slot_dev * width * 3 * part, name="grad_qkv")
    grad_tokens, gain_row = call(
        final_kernel, [sds((tok, width), F32), sds((8, width), F32)],
        [flat_tokens, gn_mine, across(gn_other), grad_res, small], name="final")

    def own_rows_sum(partial):
        return lax.psum_scatter(partial, "blk", scatter_dimension=0, tiled=True).astype(F32)

    out_sum = own_rows_sum(dw_out)
    qkv_sum = own_rows_sum(dw_qkv).reshape(rows_here, 3, part)
    table = jnp.concatenate(
        [sums[:C_GAIN1], gain_row[:1], sums[C_GAIN2 : C_GAIN2 + 1]], axis=0)
    by_owner = jnp.transpose(table.reshape(20, n_blk, rows_here), (1, 0, 2)).reshape(n_blk, -1)
    extra = jnp.broadcast_to(resid[:n_all, :n_all].reshape(1, -1), (n_blk, n_all * n_all))
    chunk = jnp.concatenate([by_owner, extra], axis=1)
    chunk = jnp.concatenate([chunk] * heads, axis=0)
    total = jnp.sum(lax.all_to_all(chunk, everyone, 0, 0, tiled=True), axis=0)
    owned = total[: 20 * rows_here].reshape(20, rows_here)
    resid_sum = total[20 * rows_here :].reshape(n_all, n_all)

    def by_source(pieces):
        chosen = []
        for e in range(e_loc):
            value = pieces[e_loc - 1]
            for d in range(e_loc - 1):
                value = jnp.where((q ^ d) == e, pieces[d], value)
            chosen.append(value.astype(F32))
        return chosen

    in_sum = jnp.stack([v.reshape(width, 2, unit) for v in by_source(came_in)], axis=1)
    down_sum = jnp.stack(by_source(came_down), axis=1)
    return (
        output.reshape(tokens.shape),
        grad_tokens.reshape(tokens.shape),
        owned[C_GAIN1],
        qkv_sum,
        out_sum,
        owned[C_GAIN2],
        jnp.transpose(owned[:n_all]),
        resid_sum,
        jnp.transpose(owned[C_CONST:C_VEC]),
        jnp.transpose(owned[C_VEC : C_VEC + 2]),
        in_sum,
        down_sum,
    )


def solution(mesh):
    in_specs = (
        P("head", "blk", None),
        P("head", "blk", None),
        P(),
        P("head", "blk", None),
        P("head", "blk", None),
        P("blk"),
        P("blk", None, "head"),
        P("blk", "head"),
        P("blk"),
        P("blk", None),
        P(),
        P("blk", None),
        P("blk", None),
        P(None, "head", None, "blk"),
        P("blk", "head", None),
        P("head", "blk", None),
    )
    out_specs = (
        P("head", "blk", None),
        P("head", "blk", None),
        P("blk"),
        P("blk", None, "head"),
        P("blk", "head"),
        P("blk"),
        P("blk", None),
        P(),
        P("blk", None),
        P("blk", None),
        P(None, "head", None, "blk"),
        P("blk", "head", None),
    )
    return jax.shard_map(
        per_device, mesh=mesh, in_specs=in_specs, out_specs=out_specs, check_vma=False
    )
```

```python
import functools
import math

import jax
import jax.numpy as jnp
from jax import lax
from jax.experimental import pallas as pl
from jax.experimental.pallas import tpu as pltpu
from jax.sharding import Mesh
from jax.sharding import PartitionSpec as P

HD = 64
NEXP = 8
EPS = 1e-05
NEG = -1e30
BF = jnp.bfloat16
F32 = jnp.float32
MIB = 1 << 20
ANY2 = (((1,), (1,)), ((), ()))
MM = (((1,), (0,)), ((), ()))
C_CONST, C_VEC, C_GAIN1, C_GAIN2 = 12, 16, 18, 19
RESID = 32


def dot(a, b, dims=MM):
    return lax.dot_general(a, b, dims, preferred_element_type=F32)


def whole_block(shape):
    return pl.BlockSpec(shape, lambda i: (0,) * len(shape), pipeline_mode=pl.Buffered(1))


def far(x):
    return pltpu.with_memory_space_constraint(x, pltpu.HBM)


class Columns:
    def __init__(self, array, count, at):
        self.array, self.at, self.window = array, (0, at // count), (array.shape[0], count)
        self.shape, self.dtype = self.window, array.dtype


def call(kernel, outs, args, smem=0, scratch=(), room=12, flops=0, name=None,
         far_in=(), far_out=()):
    sm = pl.BlockSpec(memory_space=pltpu.SMEM)
    total = sum(math.prod(a.shape) * a.dtype.itemsize for a in list(args) + list(outs))
    limit = total + sum(math.prod(a.shape) * a.dtype.itemsize for a in scratch) + room * MIB
    specs = [
        pl.BlockSpec(a.window, functools.partial(lambda at, i: at, a.at), pipeline_mode=pl.Buffered(1))
        if isinstance(a, Columns) else whole_block(a.shape) for a in args[smem:]]
    args = [a.array if isinstance(a, Columns) else a for a in args]
    args = [far(a) if i in far_in else a for i, a in enumerate(args)]
    shapes = tuple(pltpu.HBM(o.shape, o.dtype) if i in far_out else o for i, o in enumerate(outs))
    return pl.pallas_call(
        kernel,
        grid=(1,),
        out_shape=shapes,
        in_specs=[sm] * smem + specs,
        out_specs=tuple(whole_block(o.shape) for o in outs),
        scratch_shapes=list(scratch),
        compiler_params=pltpu.CompilerParams(vmem_limit_bytes=min(limit, 60 * MIB)),
        cost_estimate=pl.CostEstimate(flops=flops, bytes_accessed=total, transcendentals=0),
        name=name,
    )(*args)


def sds(shape, dtype):
    return jax.ShapeDtypeStruct(shape, dtype)


def lower_lanes(shape):
    return (lax.broadcasted_iota(jnp.int32, shape, 1) & 63) < 32


def turned(values):
    return jnp.where(
        lower_lanes(values.shape), -pltpu.roll(values, 96, 1), pltpu.roll(values, 32, 1)
    )


def qkv_kernel(idx, mine, other, wq, wsmall, cos, sin, send, xn, small, xall):
    h = idx[0]
    rows = mine.shape[0]
    xall[pl.ds(h * rows, rows), :] = mine[...]
    xall[pl.ds((1 - h) * rows, rows), :] = other[...]
    width = mine.shape[1]
    small_t = jnp.transpose(wsmall[...].astype(F32))
    small[...] = small_t[: small.shape[0]]
    x = xall[...].astype(F32)
    rstd = lax.rsqrt(jnp.mean(x * x, axis=-1, keepdims=True) + EPS)
    normed = (x * rstd * small_t[C_GAIN1 : C_GAIN1 + 1]).astype(BF)
    xn[...] = normed
    part = wq.shape[1] // 3
    pairs = part // 128
    y = dot(normed, wq[...])
    slots = cos.shape[0]
    n_seq = xall.shape[0] // slots
    c = jnp.concatenate([cos[...]] * n_seq, axis=0)
    s = jnp.concatenate([sin[...]] * n_seq, axis=0)
    for p in range(pairs):
        for k in range(3):
            piece = y[:, k * part + p * 128 : k * part + (p + 1) * 128]
            if k < 2:
                piece = piece * c + turned(piece) * s
            if k == 0:
                piece = piece * (1.0 / math.sqrt(HD))
            piece = piece.astype(BF)
            for q in range(n_seq):
                send[p * n_seq + q, :, k * 128 : (k + 1) * 128] = piece[q * slots : (q + 1) * slots]
    used = pairs * n_seq
    if send.shape[0] > used:
        send[used:] = jnp.zeros((send.shape[0] - used,) + send.shape[1:], BF)


def head_mask(shape, which):
    lane = lax.broadcasted_iota(jnp.int32, shape, 1)
    return (lane >= 64) if which else (lane < 64)


def only(values, which):
    return jnp.where(head_mask(values.shape, which), values, jnp.zeros_like(values))


def scores_of(k_rows, q_head, first_query, limit_len):
    s = dot(k_rows, q_head, ANY2)
    key = lax.broadcasted_iota(jnp.int32, s.shape, 0)
    query = lax.broadcasted_iota(jnp.int32, (1, s.shape[1]), 1) + first_query
    last = jnp.minimum(query, limit_len - 1)
    return jnp.where(key <= last, s, NEG)


def each_block(total, block, fn):
    if total // block <= 4:
        for i in range(total // block):
            fn(i * block, (i + 1) * block)
    else:

        @pl.loop(0, total // block)
        def _(i):
            fn(pl.multiple_of(i * block, block), total)


def attend_kernel(idx, qkv, out, lse, vt):
    total = qkv.shape[0]
    block = 256
    limit_len = idx[1]
    vt[...] = jnp.transpose(qkv[:, 256:384])

    def step(start, n_keys):
        q = qkv[pl.ds(start, block), 0:128]
        parts = []
        for h in range(2):
            s = scores_of(qkv[0:n_keys, 128:256], only(q, h), start, limit_len)
            m = jnp.max(s, axis=0, keepdims=True)
            p = jnp.exp(s - m)
            total_p = jnp.sum(p, axis=0, keepdims=True)
            o = dot(vt[h * 64 : (h + 1) * 64, 0:n_keys], p.astype(BF))
            parts.append(o / total_p)
            lse[h : h + 1, pl.ds(start, block)] = m + jnp.log(total_p)
        out[pl.ds(start, block), :] = jnp.transpose(jnp.concatenate(parts, axis=0)).astype(BF)

    each_block(total, block, step)


def attend_back_kernel(idx, qkv, dout, out, lse, cos, sin, grad, kt, dk, dv):
    total = qkv.shape[0]
    block = 256
    limit_len = idx[1]
    kt[...] = jnp.transpose(qkv[:, 128:256])
    dk[...] = jnp.zeros_like(dk)
    dv[...] = jnp.zeros_like(dv)

    def unrotate(values, at, size):
        c, s = cos[pl.ds(at, size), :], sin[pl.ds(at, size), :]
        return values * c - turned(values) * s

    def step(start, n_keys):
        q = qkv[pl.ds(start, block), 0:128]
        do = dout[pl.ds(start, block), :]
        prod_t = jnp.transpose(do.astype(F32) * out[pl.ds(start, block), :].astype(F32))
        probs, ds, dq = [], [], []
        for h in range(2):
            q_head, do_head = only(q, h), only(do, h)
            s = scores_of(qkv[0:n_keys, 128:256], q_head, start, limit_len)
            p = jnp.exp(s - lse[h : h + 1, pl.ds(start, block)])
            delta = jnp.sum(prod_t[h * 64 : (h + 1) * 64], axis=0, keepdims=True)
            dp = dot(qkv[0:n_keys, 256:384], do_head, ANY2)
            d = (p * (dp - delta)).astype(BF)
            probs.append(p.astype(BF))
            ds.append(d)
            dq.append(dot(kt[h * 64 : (h + 1) * 64, 0:n_keys], d))
        both_q = jnp.concatenate([only(q, 0), only(q, 1)], axis=0)
        both_do = jnp.concatenate([only(do, 0), only(do, 1)], axis=0)
        dv[0:n_keys, :] += dot(jnp.concatenate(probs, axis=1), both_do)
        dk[0:n_keys, :] += dot(jnp.concatenate(ds, axis=1), both_q)
        gq = jnp.transpose(jnp.concatenate(dq, axis=0)) * (1.0 / math.sqrt(HD))
        grad[pl.ds(start, block), 0:128] = unrotate(gq, start, block).astype(BF)

    each_block(total, block, step)

    def finish(start, _):
        at = pl.ds(start, block)
        grad[at, 128:256] = unrotate(dk[at, :], start, block).astype(BF)
        grad[at, 256:384] = dv[at, :].astype(BF)

    each_block(total, block, finish)


def out_kernel(idx, recv, wpack, mine, other, attn, full):
    h = idx[0]
    part = attn.shape[1]
    n_seq = attn.shape[0] // recv.shape[1]
    for p in range(part // 128):
        rows = recv[p * n_seq : (p + 1) * n_seq].reshape(attn.shape[0], 128)
        attn[:, p * 128 : (p + 1) * 128] = rows
    full[...] = dot(attn[...], wpack[...], ANY2)
    rows = mine.shape[0]
    mine[...] = full[pl.ds(h * rows, rows), :]
    other[...] = full[pl.ds((1 - h) * rows, rows), :].astype(BF)


def onehot_rows(slots, n_rows):
    at = lax.broadcasted_iota(jnp.int32, (n_rows, slots.shape[1]), 0)
    return jnp.where((at == slots[0:1]) | (at == slots[1:2]), 1.0, 0.0).astype(BF)


def spread(rows, send):
    per = send.shape[1]
    copies = send.shape[0] * per // rows.shape[0]
    for i in range(send.shape[0]):
        at = (i // copies) * per
        send[i] = rows[at : at + per]


def send_grad_kernel(slots, cot, ints, send):
    g = (cot[...] * ints[:, 4:5].astype(F32)).astype(BF)
    n_rows = send.shape[1] * 2
    spread(dot(onehot_rows(slots[...], n_rows), g).astype(BF), send)


def norm_two(residual, gain):
    rstd = lax.rsqrt(jnp.mean(residual * residual, axis=-1, keepdims=True) + EPS)
    xhat = residual * rstd
    return rstd, xhat, xhat * gain


def route_kernel(tokens, mine, other, wpack, small, prev_logits, ints, slots, send, residual, aux):
    res = tokens[...].astype(F32) + mine[...] + other[...].astype(F32)
    residual[...] = res
    _, _, normed = norm_two(res, small[C_GAIN2 : C_GAIN2 + 1])
    low = normed.astype(BF)
    logits = dot(low, wpack[...]) + prev_logits[...]
    lane = lax.broadcasted_iota(jnp.int32, logits.shape, 1)

    def pick(which):
        return jnp.sum(jnp.where(lane == which, logits, 0.0), axis=1, keepdims=True)

    def pair_softmax(a, b):
        top = jnp.maximum(a, b)
        ea, eb = jnp.exp(a - top), jnp.exp(b - top)
        return ea / (ea + eb), eb / (ea + eb)

    p0, p1 = pair_softmax(pick(ints[:, 0:1]), pick(ints[:, 1:2]))
    a00, a01 = pair_softmax(pick(C_CONST), pick(C_CONST + 1))
    a10, a11 = pair_softmax(pick(C_CONST + 2), pick(C_CONST + 3))
    info = jnp.zeros_like(logits)
    for i, v in enumerate((p0, p1, a00, a01, a10, a11)):
        info = jnp.where(lane == i, v, info)
    aux[...] = info
    n_rows = send.shape[1] * 2
    tok = slots.shape[1]
    at = lax.broadcasted_iota(jnp.int32, (n_rows, tok), 0)
    first = jnp.where(at == slots[0:1], 1.0, 0.0).astype(BF)
    second = jnp.where(at == slots[1:2], 1.0, 0.0).astype(BF)

    def split(v, base):
        high = v.astype(BF).astype(F32)
        return jnp.where(lane == 0, high, jnp.where(lane == 1, v - high, base))

    extra = dot(first, split(p0, 0.0).astype(BF)) + dot(second, split(p1, 0.0).astype(BF))
    rows = jnp.concatenate([dot(first + second, low), extra], axis=1)
    spread(rows.astype(BF), send)


def expert_kernel(n_pieces, n_steps, x_ref, g_ref, *refs):
    w, back, grads = refs[:n_pieces], refs[n_pieces], refs[n_pieces + 1 : 2 * n_pieces + 1]
    wd_all = refs[2 * n_pieces + 1]
    acc = refs[2 * n_pieces + 2] if n_steps > 1 else None
    step = pl.program_id(0)
    width = g_ref.shape[1]
    two = w[0].shape[1]
    unit = two // 2
    strips = width // two

    @pl.when(step == 0)
    def _():
        for d in range(n_pieces):
            for j in range(strips):
                at = width + j * unit
                wd_all[d * unit : (d + 1) * unit, j * two : (j + 1) * two] = w[d][at : at + unit, :]

    x = x_ref[:, :width]
    g = g_ref[...]
    prob = jnp.sum(x_ref[:, width:].astype(F32), axis=1, keepdims=True)
    xt = jnp.transpose(x)
    g_scaled = (g.astype(F32) * prob).astype(BF)
    up_grad = dot(g, wd_all[...], ANY2) * prob
    hiddens = []
    grad_in = jnp.zeros((x.shape[0], width), F32)

    def keep(d, start, value):
        at = slice(start, start + value.shape[0])
        if n_steps == 1:
            grads[d][at, :] = value.astype(BF)
            return

        @pl.when(step == 0)
        def _():
            acc[d, at, :] = value

        @pl.when(step > 0)
        def _():
            acc[d, at, :] += value

        @pl.when(step == n_steps - 1)
        def _():
            grads[d][at, :] = acc[d, at, :].astype(BF)

    for d in range(n_pieces):
        both = dot(x, w[d][:width, :])
        gate, up = both[:, :unit], both[:, unit:]
        sig = 1.0 / (1.0 + jnp.exp(-gate))
        act = gate * sig
        hidden = (act * up).astype(BF)
        hiddens.append(hidden)
        gh = up_grad[:, d * unit : (d + 1) * unit]
        g_gate = gh * up * sig * (1.0 + gate * (1.0 - sig))
        g_both = jnp.concatenate([g_gate, gh * act], axis=1).astype(BF)
        grad_in += dot(g_both, w[d][:width, :], ANY2)
        keep(d, 0, dot(xt, g_both))
        gd = dot(jnp.transpose(hidden), g_scaled)
        for j in range(strips):
            keep(d, width + j * unit, gd[:, j * two : (j + 1) * two])
    back[:, :width] = dot(jnp.concatenate(hiddens, axis=1), wd_all[...]).astype(BF)
    back[:, width:] = grad_in.astype(BF)


def experts(x_rows, g_rows, pieces):
    n = len(pieces)
    rows, wide = x_rows.shape
    width = g_rows.shape[1]
    deep, two = pieces[0].shape
    unit = two // 2
    block = 384 if rows % 384 == 0 else rows
    steps = rows // block
    outs = [sds((rows, 2 * width), BF)] + [sds((deep, two), BF)] * n
    scratch = [pltpu.VMEM((n * unit, width), BF)]
    if steps > 1:
        scratch.append(pltpu.VMEM((n, deep, two), F32))
    return pl.pallas_call(
        functools.partial(expert_kernel, n, steps),
        grid=(steps,),
        in_specs=[
            pl.BlockSpec((block, wide), lambda i: (i, 0)),
            pl.BlockSpec((block, width), lambda i: (i, 0)),
        ]
        + [whole_block(a.shape) for a in pieces],
        out_specs=tuple(
            [pl.BlockSpec((block, 2 * width), lambda i: (i, 0))]
            + [whole_block(o.shape) for o in outs[1:]]
        ),
        out_shape=tuple(outs[:1] + [pltpu.HBM(o.shape, o.dtype) for o in outs[1:]]),
        scratch_shapes=scratch,
        compiler_params=pltpu.CompilerParams(vmem_limit_bytes=(30 if steps == 1 else 48) * MIB),
        cost_estimate=pl.CostEstimate(
            flops=18 * rows * width * unit * n,
            bytes_accessed=8 * rows * width + 12 * width * unit * n,
            transcendentals=0,
        ),
        name="experts",
    )(x_rows, far(g_rows), *[far(p) for p in pieces])


def combine_kernel(recv, residual, cot, small, wpack, ints, aux, prev, out, grad_res, grad_low, sums, resid):
    res = residual[...]
    gain = small[C_GAIN2 : C_GAIN2 + 1]
    rstd, xhat, normed = norm_two(res, gain)
    low = normed.astype(BF)
    width = res.shape[1]
    heads = 2
    copies = recv.shape[0] // heads
    groups = []
    for h in range(heads):
        total = recv[h * copies].astype(F32)
        for r in range(1, copies):
            total = total + recv[h * copies + r].astype(F32)
        groups.append(total.astype(BF))
    rows = jnp.concatenate(groups, axis=0)
    valid = ints[:, 4:5].astype(F32)
    go = cot[...] * valid
    lane = lax.broadcasted_iota(jnp.int32, (res.shape[0], rows.shape[0]), 1)
    first = jnp.where(lane == ints[:, 2:3], 1.0, 0.0).astype(BF)
    second = jnp.where(lane == ints[:, 3:4], 1.0, 0.0).astype(BF)
    eo0 = dot(first, rows[:, :width])
    eo1 = dot(second, rows[:, :width])
    gin = dot(first + second, rows[:, width:])
    info = aux[...]
    p0, p1 = info[:, 0:1], info[:, 1:2]
    alpha = ((info[:, 2:3], info[:, 3:4]), (info[:, 4:5], info[:, 5:6]))
    r0, r1 = ints[:, 0:1], ints[:, 1:2]

    def at(route, which):
        return jnp.where(route == which, 1.0, 0.0)

    vec = (small[C_VEC : C_VEC + 1], small[C_VEC + 1 : C_VEC + 2])
    share0 = at(r0, NEXP + 1) + at(r0, NEXP + 2) * alpha[0][0] + at(r0, NEXP + 3) * alpha[1][0]
    share1 = at(r1, NEXP + 1) + at(r1, NEXP + 2) * alpha[0][0] + at(r1, NEXP + 3) * alpha[1][0]
    weight = [p0 * at(r0, NEXP + 2 + j) + p1 * at(r1, NEXP + 2 + j) for j in range(2)]
    mixed = (
        p0 * eo0
        + p1 * eo1
        + (p0 * share0 + p1 * share1) * normed
        + (weight[0] * alpha[0][1]) * vec[0]
        + (weight[1] * alpha[1][1]) * vec[1]
    )
    out[...] = valid * (res + mixed)

    def rowsum(v):
        return jnp.sum(v, axis=1, keepdims=True)

    s_norm = rowsum(go * normed)
    s_vec = [rowsum(go * vec[j]) for j in range(2)]
    gg0 = rowsum(go * eo0) + share0 * s_norm
    gg1 = rowsum(go * eo1) + share1 * s_norm
    for j in range(2):
        gg0 = gg0 + at(r0, NEXP + 2 + j) * alpha[j][1] * s_vec[j]
        gg1 = gg1 + at(r1, NEXP + 2 + j) * alpha[j][1] * s_vec[j]
    gsum = p0 * gg0 + p1 * gg1
    c0, c1 = p0 * (gg0 - gsum), p1 * (gg1 - gsum)
    wide = lax.broadcasted_iota(jnp.int32, (res.shape[0], 128), 1)
    dl = jnp.where(wide == r0, c0, 0.0) + jnp.where(wide == r1, c1, 0.0)
    coef = p0 * at(r0, NEXP + 1) + p1 * at(r1, NEXP + 1)
    vec_rows = []
    for j in range(2):
        ga0, ga1 = weight[j] * s_norm, weight[j] * s_vec[j]
        mean = alpha[j][0] * ga0 + alpha[j][1] * ga1
        dl = jnp.where(wide == C_CONST + 2 * j, alpha[j][0] * (ga0 - mean), dl)
        dl = jnp.where(wide == C_CONST + 2 * j + 1, alpha[j][1] * (ga1 - mean), dl)
        coef = coef + alpha[j][0] * weight[j]
        vec_rows.append(jnp.sum((alpha[j][1] * weight[j]) * go, axis=0, keepdims=True))
    dl = dl.astype(BF)
    dlt = jnp.transpose(dl)
    proj = dot(dlt, low)
    resid[...] = lax.dot_general(
        jnp.transpose(prev[...]), jnp.where(wide < C_CONST, dl.astype(F32), 0.0), MM,
        precision=lax.Precision.HIGHEST, preferred_element_type=F32,
    )
    gn = gin + coef * go + dot(dl, wpack[...], ANY2)
    gain_row = jnp.sum(gn * xhat, axis=0, keepdims=True)
    row = lax.broadcasted_iota(jnp.int32, (sums.shape[0], 1), 0)
    table = jnp.where(row < C_VEC, proj[: sums.shape[0]], 0.0)
    table = jnp.where(row == C_VEC, vec_rows[0], table)
    table = jnp.where(row == C_VEC + 1, vec_rows[1], table)
    sums[...] = jnp.where(row == C_GAIN2, gain_row, table)
    ghat = gn * gain
    grad = go + rstd * (ghat - xhat * jnp.mean(ghat * xhat, axis=-1, keepdims=True))
    grad_res[...] = grad
    grad_low[...] = grad.astype(BF)


def grad_vec_kernel(idx, mine, other, attn, wpack, send, dw, both):
    h = idx[0]
    rows = mine.shape[0]
    both[pl.ds(h * rows, rows), :] = mine[...]
    both[pl.ds((1 - h) * rows, rows), :] = other[...]
    part = attn.shape[1]
    g = both[...]
    gv = dot(g, wpack[...]).astype(BF)
    slots = send.shape[1]
    n_seq = g.shape[0] // slots
    for p in range(part // 128):
        for s in range(n_seq):
            send[p * n_seq + s] = gv[s * slots : (s + 1) * slots, p * 128 : (p + 1) * 128]
    used = part // 128 * n_seq
    if send.shape[0] > used:
        send[used:] = jnp.zeros((send.shape[0] - used,) + send.shape[1:], BF)
    dw[...] = dot(jnp.transpose(g), attn[...])


def grad_qkv_kernel(idx, recv, xn, mine_tok, other_tok, wpack, sums, resid, dw_out, mine, other, keep, give,
                    both, full, pay, xall):
    h, c = idx[0], idx[2]
    part = both.shape[1] // 3
    n_seq = both.shape[0] // recv.shape[1]
    for p in range(part // 128):
        rows = recv[p * n_seq : (p + 1) * n_seq].reshape(both.shape[0], 384)
        for k in range(3):
            at = k * part + p * 128
            both[:, at : at + 128] = rows[:, k * 128 : (k + 1) * 128]
    g = both[...]
    gn = dot(g, wpack[...], ANY2)
    full[...] = gn
    rows = mine.shape[0]
    mine[...] = full[pl.ds(h * rows, rows), :]
    other[...] = full[pl.ds((1 - h) * rows, rows), :].astype(BF)
    xall[pl.ds(h * rows, rows), :] = mine_tok[...]
    xall[pl.ds((1 - h) * rows, rows), :] = other_tok[...]
    x = xall[...].astype(F32)
    rstd = lax.rsqrt(jnp.mean(x * x, axis=-1, keepdims=True) + EPS)
    gain_row = jnp.sum(gn * (x * rstd), axis=0, keepdims=True)
    row = lax.broadcasted_iota(jnp.int32, (sums.shape[0], 1), 0)
    table = jnp.where(row == C_GAIN1, gain_row, sums[...])
    table = jnp.concatenate([table, jnp.zeros((128 - table.shape[0], table.shape[1]), F32)], axis=0)
    columns = jnp.transpose(table)
    dw = dot(jnp.transpose(xn[...]), g)
    half, _, owned, _ = pay.shape
    block = pltpu.roll(resid[:owned, :], RESID, 1)
    for i in range(half):
        for j in range(2):
            at = (2 * i + j) * owned
            pay[i, j, :, : 3 * part] = dw[at : at + owned]
            pay[i, j, :, 3 * part : 4 * part] = dw_out[at : at + owned, :]
            pay[i, j, :, 4 * part :] = columns[at : at + owned] + block
    for i in range(half):
        keep[i] = pay[i, c]
        give[i] = pay[i, 1 - c].astype(BF)


def add_kernel(a, b, out):
    out[...] = (a[...] + b[...].astype(F32)).astype(BF)


def total_kernel(recv, dw, dw_out, small):
    total = recv[0].astype(F32)
    for i in range(1, recv.shape[0]):
        total = total + recv[i].astype(F32)
    part = dw.shape[2]
    for k in range(3):
        dw[k] = total[:, k * part : (k + 1) * part]
    dw_out[...] = total[:, 3 * part : 4 * part]
    small[...] = total[:, 4 * part :]


def small_kernel(n_all, mine, other, gain1, gain2, router, const, vec, resid):
    total = mine[...] + other[...]
    rows = jnp.transpose(total)
    router[...] = rows[:n_all]
    const[...] = rows[C_CONST:C_VEC]
    vec[...] = rows[C_VEC : C_VEC + 2]
    gain1[...] = rows[C_GAIN1 : C_GAIN1 + 1]
    gain2[...] = rows[C_GAIN2 : C_GAIN2 + 1]
    resid[...] = total[:n_all, RESID : RESID + n_all]


def pair_add_kernel(n, *refs):
    for i in range(n):
        refs[2 * n + i][...] = (refs[i][...].astype(F32) + refs[n + i][...].astype(F32)).astype(BF)


def place_kernel(e_loc, idx, *refs):
    came, gin, gdown = refs[:e_loc], refs[e_loc], refs[e_loc + 1]
    width = gin.shape[0] // (2 * e_loc)
    strips = width // 256
    per = strips * 2 * e_loc
    for q in range(e_loc):

        @pl.when(idx[3] == q)
        def _():
            for d in range(e_loc):
                e = q ^ d
                for i in range(2):
                    lanes = slice(i * 128, (i + 1) * 128)
                    rows = came[d][0:width, lanes].astype(F32)
                    gin[pl.ds(2 * e + i, width, stride=2 * e_loc), :] = rows
                    for j in range(strips):
                        at = width + j * 128
                        rows = came[d][at : at + 128, lanes].astype(F32)
                        start = (2 * j + i) * e_loc + e
                        gdown[pl.ds(start, 128, stride=per), :] = rows


def pack_kernel(w_qkv, w_out, router, const, vec, gain1, gain2, out):
    part = w_out.shape[1]
    for k in range(3):
        out[:, k * part : (k + 1) * part] = w_qkv[k]
    out[:, 3 * part : 4 * part] = w_out[...]
    rows = [r[...].astype(F32) for r in (router, const, vec, gain1, gain2)]
    rows.append(jnp.zeros((128 - 20, out.shape[0]), F32))
    out[:, 4 * part :] = jnp.transpose(jnp.concatenate(rows, axis=0)).astype(BF)


def final_kernel(tokens, mine, other, grad_res, small, grad):
    x = tokens[...].astype(F32)
    rstd = lax.rsqrt(jnp.mean(x * x, axis=-1, keepdims=True) + EPS)
    xhat = x * rstd
    gn = mine[...] + other[...].astype(F32)
    ghat = gn * small[C_GAIN1 : C_GAIN1 + 1]
    grad[...] = grad_res[...] + rstd * (
        ghat - xhat * jnp.mean(ghat * xhat, axis=-1, keepdims=True)
    )


def per_device(
    tokens, previous_layer_logits, lengths, routes, pair_order, gain_attn, w_qkv, w_out, gain_ffn,
    w_router, w_residual, w_const, const_vec, w_in, w_down, cotangent,
):
    seq_dev, slot_dev, width = tokens.shape
    n_all = previous_layer_logits.shape[2]
    tok = seq_dev * slot_dev
    heads = lax.axis_size("head")
    ring = lax.axis_size("ring")
    n_blk = 2 * ring
    n_seq = seq_dev * heads
    n_slots = slot_dev * n_blk
    e_loc = w_in.shape[1]
    n_share = ring // e_loc
    unit = w_in.shape[3]
    rows_here = gain_attn.shape[0]
    part = w_qkv.shape[2]
    capacity = 9 * 2 * tok // (8 * n_all)
    h = lax.axis_index("head")
    ring_at = lax.axis_index("ring")
    core = lax.axis_index("core")
    b = ring_at * 2 + core
    q = ring_at % e_loc
    swap = [(0, 1), (1, 0)]
    blk = ("ring", "core")
    barrier = lax.optimization_barrier

    def across(x):
        return lax.ppermute(x, "head", swap)

    def partner(x):
        return lax.ppermute(x, "core", swap)

    def join(parts):
        total = unit * len(parts)
        cube = jnp.concatenate([p[:width].reshape(width, 2, unit) for p in parts], axis=2)
        down = [p[width:].reshape(strips, unit, 2 * unit) for p in parts]
        down = [jnp.transpose(p, (1, 0, 2)).reshape(unit, -1, 2 * total) for p in down]
        down = jnp.transpose(jnp.concatenate(down, axis=0), (1, 0, 2))
        return jnp.concatenate(
            [cube.reshape(width, 2 * total), down.reshape(-1, 2 * total)], axis=0)

    def divide(full):
        total = full.shape[1] // 2
        cube = full[:width].reshape(width, 2, total // unit, unit)
        down = jnp.transpose(full[width:].reshape(-1, total, 2 * total), (1, 0, 2))
        down = down.reshape(total // unit, unit, strips, 2 * unit)
        return [
            jnp.concatenate(
                [cube[:, :, d].reshape(width, 2 * unit),
                 jnp.transpose(down[d], (1, 0, 2)).reshape(-1, 2 * unit)], axis=0)
            for d in range(total // unit)]

    def hop(x, d):
        return lax.ppermute(x, "ring", [(i, i ^ d) for i in range(ring)]) if d else x

    (packed,) = call(
        pack_kernel, [sds((rows_here, 4 * part + 128), BF)],
        [jnp.transpose(w_qkv, (1, 0, 2)), w_out, jnp.transpose(w_router), jnp.transpose(w_const),
         jnp.transpose(const_vec), gain_attn[None, :], gain_ffn[None, :]],
        name="pack")
    wpack = lax.all_gather(packed, blk, axis=0, tiled=True)
    flat_tokens = tokens.reshape(tok, width)
    other_tokens = across(flat_tokens)

    strips = width // (2 * unit)
    bundle = jnp.concatenate(
        [jnp.transpose(w_in, (1, 0, 2, 3)).reshape(e_loc, width, 2 * unit),
         jnp.transpose(w_down.reshape(unit, e_loc, strips, 2 * unit), (1, 2, 0, 3)).reshape(
             e_loc, strips * unit, 2 * unit)], axis=1)

    shares = [lax.dynamic_index_in_dim(bundle, q ^ d, 0, keepdims=False) for d in range(e_loc)]

    positions = b * slot_dev + jnp.arange(slot_dev, dtype=jnp.int32)
    own_len = lax.dynamic_slice_in_dim(lengths, h * seq_dev, seq_dev)
    valid = (positions[None, :] < own_len[:, None]).reshape(tok)
    route_rows = jnp.transpose(routes.reshape(tok, 2))
    order = jnp.transpose(pair_order.reshape(tok, 2)).reshape(2 * tok)
    route = route_rows.reshape(2 * tok)
    eligible = jnp.concatenate([valid, valid]) & (route < NEXP)
    before = (
        (route[:, None] == route[None, :]) & (order[None, :] < order[:, None]) & eligible[None, :]
    )
    rank = jnp.sum(before.astype(jnp.int32), axis=1)
    slot = jnp.where(eligible & (rank < capacity), route * capacity + rank, NEXP * capacity)
    slot = slot.reshape(2, tok)
    slot_rows = jnp.concatenate([slot, jnp.zeros((6, tok), jnp.int32)], axis=0)
    ints = jnp.concatenate(
        [routes.reshape(tok, 2), jnp.transpose(slot), valid[:, None].astype(jnp.int32),
         jnp.zeros((tok, 3), jnp.int32)], axis=1)

    cot = cotangent.reshape(tok, width)
    per_send = e_loc * capacity
    (send_g,) = call(
        send_grad_kernel, [sds((heads * n_share, per_send, width), BF)], [slot_rows, cot, ints],
        name="send_grad")

    def to_experts(rows):
        flat = rows.reshape(heads * ring * capacity, rows.shape[-1])
        return lax.all_to_all(flat, ("head", "ring"), 0, 0, tiled=True)

    g_rows = to_experts(send_g)
    g_rows, shares = barrier((g_rows, shares))
    pieces = [hop(shares[d], d) for d in range(e_loc)]

    frequency = 10000.0 ** (-(2.0 * jnp.arange(HD // 2, dtype=F32)) / HD)
    angles = jnp.arange(n_slots, dtype=jnp.int32).astype(F32)[:, None] * frequency[None, :]
    cos_all = jnp.concatenate([jnp.cos(angles)] * 4, axis=1)
    sin_all = jnp.concatenate([jnp.sin(angles)] * 4, axis=1)
    cos_here = lax.dynamic_slice_in_dim(cos_all, b * slot_dev, slot_dev)
    sin_here = lax.dynamic_slice_in_dim(sin_all, b * slot_dev, slot_dev)
    idx = jnp.stack([h, lax.dynamic_index_in_dim(lengths, b % n_seq, 0, keepdims=False), core, q])
    prev = previous_layer_logits.reshape(tok, n_all)
    prev_wide = jnp.pad(prev, ((0, 0), (0, 128 - n_all)))
    prev_logits = jnp.pad(
        jnp.dot(prev, w_residual, precision=lax.Precision.HIGHEST), ((0, 0), (0, 128 - n_all)))
    (wpack, g_rows, pieces[:-1], prev_wide, prev_logits, cos_all, sin_all, ints, slot_rows) = barrier(
        (wpack, g_rows, pieces[:-1], prev_wide, prev_logits, cos_all, sin_all, ints, slot_rows))

    w_qkv_all = Columns(wpack, 3 * part, 0)
    w_out_all = Columns(wpack, part, 3 * part)
    w_small_all = Columns(wpack, 128, 4 * part)

    send_qkv, xn, small = call(
        qkv_kernel,
        [sds((n_blk, slot_dev, 384), BF), sds((n_seq * slot_dev, width), BF), sds((24, width), F32)],
        [idx, flat_tokens, other_tokens, w_qkv_all, w_small_all, cos_here, sin_here], smem=1,
        scratch=[pltpu.VMEM((n_seq * slot_dev, width), BF)],
        flops=2 * n_seq * slot_dev * width * 3 * part, name="qkv", far_in=(3, 4), far_out=(1, 2))

    def exchange(x):
        flat = x.reshape(n_blk * slot_dev, x.shape[-1])
        return lax.all_to_all(flat, blk, 0, 0, tiled=True)

    qkv = exchange(send_qkv)
    qkv, pieces[-1] = barrier((qkv, pieces[-1]))
    attn_unit, lse = call(
        attend_kernel, [sds((n_slots, 128), BF), sds((8, n_slots), F32)], [idx, qkv], smem=1,
        scratch=[pltpu.VMEM((128, n_slots), BF)], flops=2 * n_slots * n_slots * 512, name="attend", far_in=(1,), far_out=(0, 1))
    attn_recv = exchange(attn_unit).reshape(n_blk, slot_dev, 128)
    pieces = pieces + [partner(p) for p in pieces]
    mine, other, attn_low = call(
        out_kernel,
        [sds((tok, width), F32), sds((tok, width), BF), sds((n_seq * slot_dev, part), BF)],
        [idx, attn_recv, w_out_all], smem=1, scratch=[pltpu.VMEM((n_seq * slot_dev, width), F32)],
        flops=2 * n_seq * slot_dev * width * part, name="out", far_in=(2,), far_out=(2,))
    send_x, residual, aux = call(
        route_kernel,
        [sds((heads * n_share, per_send, width + 128), BF), sds((tok, width), F32), sds((tok, 128), F32)],
        [flat_tokens, mine, across(other), w_small_all, small, prev_logits, ints, slot_rows],
        flops=tok * width * 1000, name="route", far_in=(3, 4, 5), far_out=(1, 2))
    x_rows = to_experts(send_x)
    x_rows, pieces = barrier((x_rows, pieces))
    group = max(1, 128 // unit)
    if group > 1:
        pieces = [join(pieces[i : i + group]) for i in range(0, len(pieces), group)]
    back_rows, *grad_pieces = experts(x_rows, g_rows, pieces)
    back_recv = to_experts(back_rows)

    if group > 1:
        grad_pieces = [part_of for full in grad_pieces for part_of in divide(full)]
    ours = list(grad_pieces[:e_loc])
    theirs = [partner(p) for p in grad_pieces[e_loc:]]
    recv = back_recv.reshape(heads * n_share, per_send, 2 * width)
    added = call(
        functools.partial(pair_add_kernel, e_loc), [sds(p.shape, BF) for p in ours], ours + theirs,
        name="pair_add", far_in=range(2 * e_loc), far_out=range(e_loc))

    recv, added = barrier((recv, added))
    output, grad_res, grad_low, sums, resid = call(
        combine_kernel,
        [sds((tok, width), F32), sds((tok, width), F32), sds((tok, width), BF), sds((24, width), F32),
         sds((128, 128), F32)],
        [recv, residual, cot, small, w_small_all, ints, aux, prev_wide], flops=tok * width * 2000,
        name="combine", far_in=(1, 2, 3, 4, 5, 6, 7), far_out=(0, 1, 3, 4))

    came = [hop(added[d], d) for d in range(e_loc)]
    send_gv, dw_out = call(
        grad_vec_kernel, [sds((n_blk, slot_dev, 128), BF), sds((width, part), F32)],
        [idx, grad_low, across(grad_low), attn_low, w_out_all], smem=1,
        scratch=[pltpu.VMEM((n_seq * slot_dev, width), BF)],
        flops=4 * n_seq * slot_dev * width * part, name="grad_vec", far_in=(3, 4), far_out=(1,))
    dout = exchange(send_gv)
    dout, came = barrier((dout, came))
    (grad_unit,) = call(
        attend_back_kernel, [sds((n_slots, 384), BF)],
        [idx, qkv, dout, attn_unit, lse, cos_all, sin_all], smem=1,
        scratch=[pltpu.VMEM((128, n_slots), BF), pltpu.VMEM((n_slots, 128), F32),
                 pltpu.VMEM((n_slots, 128), F32)],
        flops=5 * n_slots * n_slots * 256, name="attend_back", far_in=(1, 3, 4, 5, 6), far_out=())
    grad_recv = exchange(grad_unit).reshape(n_blk, slot_dev, 384)
    def by_source(parts):
        chosen = []
        for e in range(e_loc):
            value = parts[e_loc - 1]
            for d in range(e_loc - 1):
                value = jnp.where((q ^ d) == e, parts[d], value)
            chosen.append(value.astype(F32))
        return chosen

    if group == 1:
        in_sum, down_sum = call(
            functools.partial(place_kernel, e_loc),
            [sds((width * e_loc * 2, 128), F32), sds((width // 128 * e_loc * unit, 128), F32)],
            [idx, *came], smem=1, name="place", far_in=range(1, e_loc + 1), far_out=(0, 1))
        in_sum = in_sum.reshape(width, e_loc, 2, unit)
        down_sum = jnp.transpose(down_sum.reshape(unit, -1, e_loc, 128), (0, 2, 1, 3))
        down_sum = down_sum.reshape(unit, e_loc, width)
    else:
        in_sum = jnp.stack(by_source([p[:width].reshape(width, 2, unit) for p in came]), axis=1)
        down_sum = by_source([p[width:].reshape(strips, unit, 2 * unit) for p in came])
        down_sum = jnp.transpose(jnp.stack(down_sum, axis=0), (2, 0, 1, 3))
        down_sum = down_sum.reshape(unit, e_loc, width)
    grad_recv, in_sum, down_sum = barrier((grad_recv, in_sum, down_sum))
    pay = (ring, rows_here, 4 * part + 128)
    gn_mine, gn_other, keep, give = call(
        grad_qkv_kernel,
        [sds((tok, width), F32), sds((tok, width), BF), sds(pay, F32), sds(pay, BF)],
        [idx, grad_recv, xn, flat_tokens, other_tokens, w_qkv_all, sums, resid, dw_out], smem=1,
        scratch=[pltpu.VMEM((n_seq * slot_dev, 3 * part), BF),
                 pltpu.VMEM((n_seq * slot_dev, width), F32),
                 pltpu.VMEM((ring, 2, rows_here, 4 * part + 128), F32),
                 pltpu.VMEM((n_seq * slot_dev, width), BF)],
        flops=4 * n_seq * slot_dev * width * 3 * part, name="grad_qkv", far_in=(2, 3, 4, 5, 6, 7, 8), far_out=(0,))
    gn_came = across(gn_other)
    (pair_sum,) = call(add_kernel, [sds(pay, BF)], [keep, partner(give)], name="add")
    ring_recv = lax.all_to_all(pair_sum, "ring", 0, 0, tiled=True)
    (grad_tokens,) = call(
        final_kernel, [sds((tok, width), F32)],
        [flat_tokens, gn_mine, gn_came, grad_res, small], name="final", far_in=(0, 1, 3, 4), far_out=(0,))
    ring_recv, grad_tokens = barrier((ring_recv, grad_tokens))
    qkv_sum, out_sum, small_sum = call(
        total_kernel,
        [sds((3, rows_here, part), F32), sds((rows_here, part), F32), sds((rows_here, 128), F32)],
        [ring_recv], name="total")
    gain1_sum, gain2_sum, router_sum, const_sum, vec_sum, resid_sum = call(
        functools.partial(small_kernel, n_all),
        [sds((1, rows_here), F32), sds((1, rows_here), F32), sds((n_all, rows_here), F32),
         sds((4, rows_here), F32), sds((2, rows_here), F32), sds((n_all, n_all), F32)],
        [small_sum, across(small_sum)], name="small")

    return (
        output.reshape(tokens.shape),
        grad_tokens.reshape(tokens.shape),
        gain1_sum.reshape(rows_here),
        jnp.transpose(qkv_sum, (1, 0, 2)),
        out_sum,
        gain2_sum.reshape(rows_here),
        jnp.transpose(router_sum),
        resid_sum,
        jnp.transpose(const_sum),
        jnp.transpose(vec_sum),
        in_sum,
        down_sum,
    )


def solution(mesh):
    heads, blocks = mesh.devices.shape
    split = Mesh(mesh.devices.reshape(heads, blocks // 2, 2), ("head", "ring", "core"))
    blk = ("ring", "core")
    in_specs = (
        P("head", blk, None),
        P("head", blk, None),
        P(),
        P("head", blk, None),
        P("head", blk, None),
        P(blk),
        P(blk, None, "head"),
        P(blk, "head"),
        P(blk),
        P(blk, None),
        P(),
        P(blk, None),
        P(blk, None),
        P(None, "head", None, blk),
        P(blk, "head", None),
        P("head", blk, None),
    )
    out_specs = (
        P("head", blk, None),
        P("head", blk, None),
        P(blk),
        P(blk, None, "head"),
        P(blk, "head"),
        P(blk),
        P(blk, None),
        P(),
        P(blk, None),
        P(blk, None),
        P(None, "head", None, blk),
        P(blk, "head", None),
    )
    return jax.shard_map(
        per_device, mesh=split, in_specs=in_specs, out_specs=out_specs, check_vma=False
    )
```

```python
import functools
import math

import jax
import jax.numpy as jnp
import numpy as np
from jax import lax
from jax.experimental import pallas as pl
from jax.experimental.pallas import tpu as pltpu
from jax.sharding import Mesh
from jax.sharding import PartitionSpec as P

HD = 64
NEXP = 8
EPS = 1e-05
NEG = -1e30
BF = jnp.bfloat16
F32 = jnp.float32
MIB = 1 << 20
ANY2 = (((1,), (1,)), ((), ()))
MM = (((1,), (0,)), ((), ()))
C_CONST, C_VEC, C_GAIN1, C_GAIN2 = 12, 16, 18, 19
RESID = 32
S_HEAD, S_LEN, S_CORE, S_EXPERT, S_BLOCK, S_BIT, S_TABLE = 0, 1, 2, 3, 4, 5, 8


def dot(a, b, dims=MM):
    return lax.dot_general(a, b, dims, preferred_element_type=F32)


def whole_block(shape):
    return pl.BlockSpec(shape, lambda i: (0,) * len(shape), pipeline_mode=pl.Buffered(1))


def far(x):
    return pltpu.with_memory_space_constraint(x, pltpu.HBM)


class Columns:
    def __init__(self, array, count, at):
        self.array, self.at, self.window = array, (0, at // count), (array.shape[0], count)
        self.shape, self.dtype = self.window, array.dtype


def call(kernel, outs, args, smem=0, scratch=(), room=12, flops=0, name=None,
         far_in=(), far_out=()):
    sm = pl.BlockSpec(memory_space=pltpu.SMEM)
    total = sum(math.prod(a.shape) * a.dtype.itemsize for a in list(args) + list(outs))
    limit = total + sum(math.prod(a.shape) * a.dtype.itemsize for a in scratch) + room * MIB
    specs = [
        pl.BlockSpec(a.window, functools.partial(lambda at, i: at, a.at), pipeline_mode=pl.Buffered(1))
        if isinstance(a, Columns) else whole_block(a.shape) for a in args[smem:]]
    args = [a.array if isinstance(a, Columns) else a for a in args]
    args = [far(a) if i in far_in else a for i, a in enumerate(args)]
    shapes = tuple(pltpu.HBM(o.shape, o.dtype) if i in far_out else o for i, o in enumerate(outs))
    return pl.pallas_call(
        kernel,
        grid=(1,),
        out_shape=shapes,
        in_specs=[sm] * smem + specs,
        out_specs=tuple(whole_block(o.shape) for o in outs),
        scratch_shapes=list(scratch),
        compiler_params=pltpu.CompilerParams(vmem_limit_bytes=min(limit, 60 * MIB)),
        cost_estimate=pl.CostEstimate(flops=flops, bytes_accessed=total, transcendentals=0),
        name=name,
    )(*args)


def sds(shape, dtype):
    return jax.ShapeDtypeStruct(shape, dtype)


def unit_at(seq, pair):
    ring = (seq >> 1) * 4 + (pair >> 1) * 2 + (seq & 1)
    return ring * 2 + (pair & 1)


def idle_units(n_blk, n_seq, pairs):
    busy = {unit_at(q, p) for q in range(n_seq) for p in range(pairs)}
    return [u for u in range(n_blk) if u not in busy]


def halving_order(n):
    bits = n.bit_length() - 1
    return [sum(((k >> i) & 1) << (bits - 1 - i) for i in range(bits)) for k in range(n)]


def gather_rows(dst, arrays, idx, base, rows):
    j = base
    for a in arrays:
        for i in range(a.shape[0] // rows):
            at = idx[j] * rows
            if rows % 16 == 0:
                at = pl.multiple_of(at, 16)
            dst[pl.ds(at, rows), :] = a[i * rows : (i + 1) * rows, :]
            j += 1


def lower_lanes(shape):
    return (lax.broadcasted_iota(jnp.int32, shape, 1) & 63) < 32


def turned(values):
    return jnp.where(
        lower_lanes(values.shape), -pltpu.roll(values, 96, 1), pltpu.roll(values, 32, 1)
    )


def head_mask(shape, which):
    lane = lax.broadcasted_iota(jnp.int32, shape, 1)
    return (lane >= 64) if which else (lane < 64)


def only(values, which):
    return jnp.where(head_mask(values.shape, which), values, jnp.zeros_like(values))


def scores_of(k_rows, q_head, first_query, limit_len):
    s = dot(k_rows, q_head, ANY2)
    key = lax.broadcasted_iota(jnp.int32, s.shape, 0)
    query = lax.broadcasted_iota(jnp.int32, (1, s.shape[1]), 1) + first_query
    last = jnp.minimum(query, limit_len - 1)
    return jnp.where(key <= last, s, NEG)


def each_block(total, block, fn):
    if total // block <= 4:
        for i in range(total // block):
            fn(i * block, (i + 1) * block)
    else:

        @pl.loop(0, total // block)
        def _(i):
            fn(pl.multiple_of(i * block, block), total)


def attend_kernel(n_x, n_w, n_p, w_rows, p_rows, idx, *refs):
    xs, ws, ps = refs[:n_x], refs[n_x : n_x + n_w], refs[n_x + n_w : n_x + n_w + n_p]
    cos, sin, out, lse, xn, qkv, early, vt, wg = refs[n_x + n_w + n_p :]
    total = qkv.shape[0]
    block = 256
    slots = 64
    limit_len = idx[S_LEN]
    j = S_TABLE + sum(a.shape[0] // slots for a in xs)
    gather_rows(wg, ws, idx, j, w_rows)
    gather_rows(early, ps, idx, j + sum(a.shape[0] // w_rows for a in ws), p_rows)
    columns = early[:, early.shape[1] - 128 :].astype(F32)
    gain = jnp.transpose(columns)[C_GAIN1 : C_GAIN1 + 1]
    j = S_TABLE
    for a in xs:
        for i in range(a.shape[0] // slots):
            x = a[i * slots : (i + 1) * slots, :].astype(F32)
            rstd = lax.rsqrt(jnp.mean(x * x, axis=-1, keepdims=True) + EPS)
            at = pl.ds(pl.multiple_of(idx[j] * slots, slots), slots)
            xn[at, :] = (x * rstd * gain).astype(BF)
            j += 1

    def project(start, _):
        at = pl.ds(start, block)
        y = dot(xn[at, :], wg[...])
        c, s = cos[at, :], sin[at, :]
        q, k = y[:, 0:128], y[:, 128:256]
        q = (q * c + turned(q) * s) * (1.0 / math.sqrt(HD))
        qkv[at, 0:128] = q.astype(BF)
        qkv[at, 128:256] = (k * c + turned(k) * s).astype(BF)
        qkv[at, 256:384] = y[:, 256:384].astype(BF)

    each_block(total, block, project)
    vt[...] = jnp.transpose(qkv[:, 256:384])

    def step(start, n_keys):
        q = qkv[pl.ds(start, block), 0:128]
        parts = []
        for h in range(2):
            s = scores_of(qkv[0:n_keys, 128:256], only(q, h), start, limit_len)
            m = jnp.max(s, axis=0, keepdims=True)
            p = jnp.exp(s - m)
            total_p = jnp.sum(p, axis=0, keepdims=True)
            o = dot(vt[h * 64 : (h + 1) * 64, 0:n_keys], p.astype(BF))
            parts.append(o / total_p)
            lse[h : h + 1, pl.ds(start, block)] = m + jnp.log(total_p)
        out[pl.ds(start, block), :] = jnp.transpose(jnp.concatenate(parts, axis=0)).astype(BF)

    each_block(total, block, step)


def unit_dw_kernel(xn, grad, dw):
    dw[...] = dot(jnp.transpose(xn[...]), grad[...]).astype(BF)


def attend_back_kernel(idx, qkv, dout, out, lse, cos, sin, grad, kt, dk, dv):
    total = qkv.shape[0]
    block = 256
    limit_len = idx[S_LEN]
    kt[...] = jnp.transpose(qkv[:, 128:256])
    dk[...] = jnp.zeros_like(dk)
    dv[...] = jnp.zeros_like(dv)

    def unrotate(values, at, size):
        c, s = cos[pl.ds(at, size), :], sin[pl.ds(at, size), :]
        return values * c - turned(values) * s

    def step(start, n_keys):
        q = qkv[pl.ds(start, block), 0:128]
        do = dout[pl.ds(start, block), :]
        prod_t = jnp.transpose(do.astype(F32) * out[pl.ds(start, block), :].astype(F32))
        probs, ds, dq = [], [], []
        for h in range(2):
            q_head, do_head = only(q, h), only(do, h)
            s = scores_of(qkv[0:n_keys, 128:256], q_head, start, limit_len)
            p = jnp.exp(s - lse[h : h + 1, pl.ds(start, block)])
            delta = jnp.sum(prod_t[h * 64 : (h + 1) * 64], axis=0, keepdims=True)
            dp = dot(qkv[0:n_keys, 256:384], do_head, ANY2)
            d = (p * (dp - delta)).astype(BF)
            probs.append(p.astype(BF))
            ds.append(d)
            dq.append(dot(kt[h * 64 : (h + 1) * 64, 0:n_keys], d))
        both_q = jnp.concatenate([only(q, 0), only(q, 1)], axis=0)
        both_do = jnp.concatenate([only(do, 0), only(do, 1)], axis=0)
        dv[0:n_keys, :] += dot(jnp.concatenate(probs, axis=1), both_do)
        dk[0:n_keys, :] += dot(jnp.concatenate(ds, axis=1), both_q)
        gq = jnp.transpose(jnp.concatenate(dq, axis=0)) * (1.0 / math.sqrt(HD))
        grad[pl.ds(start, block), 0:128] = unrotate(gq, start, block).astype(BF)

    each_block(total, block, step)

    def finish(start, _):
        at = pl.ds(start, block)
        grad[at, 128:256] = unrotate(dk[at, :], start, block).astype(BF)
        grad[at, 256:384] = dv[at, :].astype(BF)

    each_block(total, block, finish)


def out_kernel(idx, recv, wos, mine, other, attn, full):
    h = idx[S_HEAD]
    part = attn.shape[1]
    slots = recv.shape[1]
    n_seq = attn.shape[0] // slots
    for p in range(part // 128):
        for q in range(n_seq):
            attn[q * slots : (q + 1) * slots, p * 128 : (p + 1) * 128] = recv[unit_at(q, p)]
    full[...] = dot(attn[...], wos[...], ANY2)
    rows = mine.shape[0]
    mine[...] = full[pl.ds(h * rows, rows), :]
    other[...] = full[pl.ds((1 - h) * rows, rows), :].astype(BF)


def onehot_rows(slots, n_rows):
    at = lax.broadcasted_iota(jnp.int32, (n_rows, slots.shape[1]), 0)
    return jnp.where((at == slots[0:1]) | (at == slots[1:2]), 1.0, 0.0).astype(BF)


def spread(rows, send):
    per = send.shape[1]
    copies = send.shape[0] * per // rows.shape[0]
    for i in range(send.shape[0]):
        at = (i // copies) * per
        send[i] = rows[at : at + per]


def send_grad_kernel(slots, cot, ints, send):
    g = (cot[...] * ints[:, 4:5].astype(F32)).astype(BF)
    n_rows = send.shape[1] * 2
    spread(dot(onehot_rows(slots[...], n_rows), g).astype(BF), send)


def norm_two(residual, gain):
    rstd = lax.rsqrt(jnp.mean(residual * residual, axis=-1, keepdims=True) + EPS)
    xhat = residual * rstd
    return rstd, xhat, xhat * gain


def route_kernel(tokens, mine, other, wpack, prev_logits, ints, slots, send, residual, aux, small):
    res = tokens[...].astype(F32) + mine[...] + other[...].astype(F32)
    residual[...] = res
    small[...] = jnp.transpose(wpack[...].astype(F32))[: small.shape[0]]
    _, _, normed = norm_two(res, small[C_GAIN2 : C_GAIN2 + 1])
    low = normed.astype(BF)
    logits = dot(low, wpack[...]) + prev_logits[...]
    lane = lax.broadcasted_iota(jnp.int32, logits.shape, 1)

    def pick(which):
        return jnp.sum(jnp.where(lane == which, logits, 0.0), axis=1, keepdims=True)

    def pair_softmax(a, b):
        top = jnp.maximum(a, b)
        ea, eb = jnp.exp(a - top), jnp.exp(b - top)
        return ea / (ea + eb), eb / (ea + eb)

    p0, p1 = pair_softmax(pick(ints[:, 0:1]), pick(ints[:, 1:2]))
    a00, a01 = pair_softmax(pick(C_CONST), pick(C_CONST + 1))
    a10, a11 = pair_softmax(pick(C_CONST + 2), pick(C_CONST + 3))
    info = jnp.zeros_like(logits)
    for i, v in enumerate((p0, p1, a00, a01, a10, a11)):
        info = jnp.where(lane == i, v, info)
    aux[...] = info
    n_rows = send.shape[1] * 2
    tok = slots.shape[1]
    at = lax.broadcasted_iota(jnp.int32, (n_rows, tok), 0)
    first = jnp.where(at == slots[0:1], 1.0, 0.0).astype(BF)
    second = jnp.where(at == slots[1:2], 1.0, 0.0).astype(BF)

    def split(v, base):
        high = v.astype(BF).astype(F32)
        return jnp.where(lane == 0, high, jnp.where(lane == 1, v - high, base))

    extra = dot(first, split(p0, 0.0).astype(BF)) + dot(second, split(p1, 0.0).astype(BF))
    rows = jnp.concatenate([dot(first + second, low), extra], axis=1)
    spread(rows.astype(BF), send)


def expert_kernel(n_pieces, n_steps, x_ref, g_ref, *refs):
    w, back, grads = refs[:n_pieces], refs[n_pieces], refs[n_pieces + 1 : 2 * n_pieces + 1]
    wd_all = refs[2 * n_pieces + 1]
    acc = refs[2 * n_pieces + 2] if n_steps > 1 else None
    step = pl.program_id(0)
    width = g_ref.shape[1]
    two = w[0].shape[1]
    unit = two // 2
    strips = width // two

    @pl.when(step == 0)
    def _():
        for d in range(n_pieces):
            for j in range(strips):
                at = width + j * unit
                wd_all[d * unit : (d + 1) * unit, j * two : (j + 1) * two] = w[d][at : at + unit, :]

    x = x_ref[:, :width]
    g = g_ref[...]
    prob = jnp.sum(x_ref[:, width:].astype(F32), axis=1, keepdims=True)
    xt = jnp.transpose(x)
    g_scaled = (g.astype(F32) * prob).astype(BF)
    up_grad = dot(g, wd_all[...], ANY2) * prob
    hiddens = []
    grad_in = jnp.zeros((x.shape[0], width), F32)

    def keep(d, start, value):
        at = slice(start, start + value.shape[0])
        if n_steps == 1:
            grads[d][at, :] = value.astype(BF)
            return

        @pl.when(step == 0)
        def _():
            acc[d, at, :] = value

        @pl.when(step > 0)
        def _():
            acc[d, at, :] += value

        @pl.when(step == n_steps - 1)
        def _():
            grads[d][at, :] = acc[d, at, :].astype(BF)

    for d in range(n_pieces):
        both = dot(x, w[d][:width, :])
        gate, up = both[:, :unit], both[:, unit:]
        sig = 1.0 / (1.0 + jnp.exp(-gate))
        act = gate * sig
        hidden = (act * up).astype(BF)
        hiddens.append(hidden)
        gh = up_grad[:, d * unit : (d + 1) * unit]
        g_gate = gh * up * sig * (1.0 + gate * (1.0 - sig))
        g_both = jnp.concatenate([g_gate, gh * act], axis=1).astype(BF)
        grad_in += dot(g_both, w[d][:width, :], ANY2)
        keep(d, 0, dot(xt, g_both))
        gd = dot(jnp.transpose(hidden), g_scaled)
        for j in range(strips):
            keep(d, width + j * unit, gd[:, j * two : (j + 1) * two])
    back[:, :width] = dot(jnp.concatenate(hiddens, axis=1), wd_all[...]).astype(BF)
    back[:, width:] = grad_in.astype(BF)


def experts(x_rows, g_rows, pieces):
    n = len(pieces)
    rows, wide = x_rows.shape
    width = g_rows.shape[1]
    deep, two = pieces[0].shape
    unit = two // 2
    block = 384 if rows % 384 == 0 else rows
    steps = rows // block
    outs = [sds((rows, 2 * width), BF)] + [sds((deep, two), BF)] * n
    scratch = [pltpu.VMEM((n * unit, width), BF)]
    if steps > 1:
        scratch.append(pltpu.VMEM((n, deep, two), F32))
    return pl.pallas_call(
        functools.partial(expert_kernel, n, steps),
        grid=(steps,),
        in_specs=[
            pl.BlockSpec((block, wide), lambda i: (i, 0)),
            pl.BlockSpec((block, width), lambda i: (i, 0)),
        ]
        + [whole_block(a.shape) for a in pieces],
        out_specs=tuple(
            [pl.BlockSpec((block, 2 * width), lambda i: (i, 0))]
            + [whole_block(o.shape) for o in outs[1:]]
        ),
        out_shape=tuple(outs[:1] + [pltpu.HBM(o.shape, o.dtype) for o in outs[1:]]),
        scratch_shapes=scratch,
        compiler_params=pltpu.CompilerParams(vmem_limit_bytes=(30 if steps == 1 else 48) * MIB),
        cost_estimate=pl.CostEstimate(
            flops=18 * rows * width * unit * n,
            bytes_accessed=8 * rows * width + 12 * width * unit * n,
            transcendentals=0,
        ),
        name="experts",
    )(x_rows, far(g_rows), *[far(p) for p in pieces])


def combine_kernel(recv, residual, cot, small, wpack, ints, aux, prev, out, grad_res, grad_low, sums, resid):
    res = residual[...]
    gain = small[C_GAIN2 : C_GAIN2 + 1]
    rstd, xhat, normed = norm_two(res, gain)
    low = normed.astype(BF)
    width = res.shape[1]
    heads = 2
    copies = recv.shape[0] // heads
    groups = []
    for h in range(heads):
        total = recv[h * copies].astype(F32)
        for r in range(1, copies):
            total = total + recv[h * copies + r].astype(F32)
        groups.append(total.astype(BF))
    rows = jnp.concatenate(groups, axis=0)
    valid = ints[:, 4:5].astype(F32)
    go = cot[...] * valid
    lane = lax.broadcasted_iota(jnp.int32, (res.shape[0], rows.shape[0]), 1)
    first = jnp.where(lane == ints[:, 2:3], 1.0, 0.0).astype(BF)
    second = jnp.where(lane == ints[:, 3:4], 1.0, 0.0).astype(BF)
    eo0 = dot(first, rows[:, :width])
    eo1 = dot(second, rows[:, :width])
    gin = dot(first + second, rows[:, width:])
    info = aux[...]
    p0, p1 = info[:, 0:1], info[:, 1:2]
    alpha = ((info[:, 2:3], info[:, 3:4]), (info[:, 4:5], info[:, 5:6]))
    r0, r1 = ints[:, 0:1], ints[:, 1:2]

    def at(route, which):
        return jnp.where(route == which, 1.0, 0.0)

    vec = (small[C_VEC : C_VEC + 1], small[C_VEC + 1 : C_VEC + 2])
    share0 = at(r0, NEXP + 1) + at(r0, NEXP + 2) * alpha[0][0] + at(r0, NEXP + 3) * alpha[1][0]
    share1 = at(r1, NEXP + 1) + at(r1, NEXP + 2) * alpha[0][0] + at(r1, NEXP + 3) * alpha[1][0]
    weight = [p0 * at(r0, NEXP + 2 + j) + p1 * at(r1, NEXP + 2 + j) for j in range(2)]
    mixed = (
        p0 * eo0
        + p1 * eo1
        + (p0 * share0 + p1 * share1) * normed
        + (weight[0] * alpha[0][1]) * vec[0]
        + (weight[1] * alpha[1][1]) * vec[1]
    )
    out[...] = valid * (res + mixed)

    def rowsum(v):
        return jnp.sum(v, axis=1, keepdims=True)

    s_norm = rowsum(go * normed)
    s_vec = [rowsum(go * vec[j]) for j in range(2)]
    gg0 = rowsum(go * eo0) + share0 * s_norm
    gg1 = rowsum(go * eo1) + share1 * s_norm
    for j in range(2):
        gg0 = gg0 + at(r0, NEXP + 2 + j) * alpha[j][1] * s_vec[j]
        gg1 = gg1 + at(r1, NEXP + 2 + j) * alpha[j][1] * s_vec[j]
    gsum = p0 * gg0 + p1 * gg1
    c0, c1 = p0 * (gg0 - gsum), p1 * (gg1 - gsum)
    wide = lax.broadcasted_iota(jnp.int32, (res.shape[0], 128), 1)
    dl = jnp.where(wide == r0, c0, 0.0) + jnp.where(wide == r1, c1, 0.0)
    coef = p0 * at(r0, NEXP + 1) + p1 * at(r1, NEXP + 1)
    vec_rows = []
    for j in range(2):
        ga0, ga1 = weight[j] * s_norm, weight[j] * s_vec[j]
        mean = alpha[j][0] * ga0 + alpha[j][1] * ga1
        dl = jnp.where(wide == C_CONST + 2 * j, alpha[j][0] * (ga0 - mean), dl)
        dl = jnp.where(wide == C_CONST + 2 * j + 1, alpha[j][1] * (ga1 - mean), dl)
        coef = coef + alpha[j][0] * weight[j]
        vec_rows.append(jnp.sum((alpha[j][1] * weight[j]) * go, axis=0, keepdims=True))
    dl = dl.astype(BF)
    dlt = jnp.transpose(dl)
    proj = dot(dlt, low)
    resid[...] = lax.dot_general(
        jnp.transpose(prev[...]), jnp.where(wide < C_CONST, dl.astype(F32), 0.0), MM,
        precision=lax.Precision.HIGHEST, preferred_element_type=F32,
    )
    gn = gin + coef * go + dot(dl, wpack[...], ANY2)
    gain_row = jnp.sum(gn * xhat, axis=0, keepdims=True)
    row = lax.broadcasted_iota(jnp.int32, (sums.shape[0], 1), 0)
    table = jnp.where(row < C_VEC, proj[: sums.shape[0]], 0.0)
    table = jnp.where(row == C_VEC, vec_rows[0], table)
    table = jnp.where(row == C_VEC + 1, vec_rows[1], table)
    sums[...] = jnp.where(row == C_GAIN2, gain_row, table)
    ghat = gn * gain
    grad = go + rstd * (ghat - xhat * jnp.mean(ghat * xhat, axis=-1, keepdims=True))
    grad_res[...] = grad
    grad_low[...] = grad.astype(BF)


def grad_vec_kernel(idx, mine, other, attn, wos, sums, resid, send, keep, give, both, pay):
    h = idx[S_HEAD]
    rows = mine.shape[0]
    both[pl.ds(h * rows, rows), :] = mine[...]
    both[pl.ds((1 - h) * rows, rows), :] = other[...]
    part = attn.shape[1]
    g = both[...]
    gv = dot(g, wos[...]).astype(BF)
    slots = send.shape[1]
    n_seq = g.shape[0] // slots
    for p in range(part // 128):
        for q in range(n_seq):
            send[unit_at(q, p)] = gv[q * slots : (q + 1) * slots, p * 128 : (p + 1) * 128]
    for u in idle_units(send.shape[0], n_seq, part // 128):
        send[u] = jnp.zeros(send.shape[1:], BF)
    dw = dot(jnp.transpose(g), attn[...])
    table = jnp.concatenate([sums[...], jnp.zeros((128 - sums.shape[0], sums.shape[1]), F32)], axis=0)
    columns = jnp.transpose(table)
    n, owned, _ = pay.shape
    block = pltpu.roll(resid[:owned, :], RESID, 1)
    for i in range(n):
        at = i * owned
        pay[i, :, :part] = dw[at : at + owned]
        pay[i, :, part:] = columns[at : at + owned] + block
    for k, offset in enumerate(halving_order(n)):
        value = pay[idx[S_BLOCK] ^ offset]
        if k < n // 2:
            keep[k] = value
        else:
            give[k - n // 2] = value.astype(BF)


def halve_kernel(mine, came, keep, give):
    half = keep.shape[0]
    keep[...] = mine[:half] + came[:half].astype(F32)
    give[...] = (mine[half:] + came[half:].astype(F32)).astype(BF)


def last_add_kernel(mine, came, dw, table):
    total = mine[0] + came[0].astype(F32)
    dw[...] = total[:, : dw.shape[1]]
    table[...] = total[:, dw.shape[1] :]


def grad_qkv_kernel(n_w, rows_here, base, idx, recv, *refs):
    ws = refs[:n_w]
    mine, other, both, full, wall = refs[n_w:]
    h = idx[S_HEAD]
    part = both.shape[1] // 3
    slots = recv.shape[1]
    n_seq = both.shape[0] // slots
    gather_rows(wall, ws, idx, base, rows_here)
    for p in range(part // 128):
        for q in range(n_seq):
            unit = recv[unit_at(q, p)]
            for k in range(3):
                at = k * part + p * 128
                both[q * slots : (q + 1) * slots, at : at + 128] = unit[:, k * 128 : (k + 1) * 128]
    full[...] = dot(both[...], wall[...], ANY2)
    rows = mine.shape[0]
    mine[...] = full[pl.ds(h * rows, rows), :]
    other[...] = full[pl.ds((1 - h) * rows, rows), :].astype(BF)


def total_kernel(recv, w, gain, dw, gain_row):
    part = dw.shape[2]
    owned = dw.shape[1]
    column = jnp.transpose(jnp.broadcast_to(gain[...].astype(F32), (8, owned)))[:, 0:1]
    rowsum = jnp.zeros((owned, 1), F32)
    for p in range(part // 128):
        total = recv[unit_at(0, p)].astype(F32)
        for q in range(1, 4):
            total = total + recv[unit_at(q, p)].astype(F32)
        for k in range(3):
            piece = total[:, k * 128 : (k + 1) * 128]
            at = slice(p * 128, (p + 1) * 128)
            rowsum = rowsum + jnp.sum(piece * w[k, :, at].astype(F32), axis=1, keepdims=True)
            dw[k, :, at] = piece
    rowsum = rowsum / column
    gain_row[...] = jnp.transpose(jnp.broadcast_to(rowsum, (owned, 128)))[: gain_row.shape[0]]


def small_kernel(n_all, mine, other, gain2, router, const, vec, resid):
    total = mine[...] + other[...]
    rows = jnp.transpose(total)
    router[...] = rows[:n_all]
    const[...] = rows[C_CONST:C_VEC]
    vec[...] = rows[C_VEC : C_VEC + 2]
    gain2[...] = rows[C_GAIN2 : C_GAIN2 + 1]
    resid[...] = total[:n_all, RESID : RESID + n_all]


def pair_add_kernel(n, *refs):
    for i in range(n):
        refs[2 * n + i][...] = (refs[i][...].astype(F32) + refs[n + i][...].astype(F32)).astype(BF)


def place_kernel(e_loc, idx, *refs):
    came, gin, gdown = refs[:e_loc], refs[e_loc], refs[e_loc + 1]
    width = gin.shape[0] // (2 * e_loc)
    strips = width // 256
    per = strips * 2 * e_loc
    for q in range(e_loc):

        @pl.when(idx[S_EXPERT] == q)
        def _():
            for d in range(e_loc):
                e = q ^ d
                for i in range(2):
                    lanes = slice(i * 128, (i + 1) * 128)
                    rows = came[d][0:width, lanes].astype(F32)
                    gin[pl.ds(2 * e + i, width, stride=2 * e_loc), :] = rows
                    for j in range(strips):
                        at = width + j * 128
                        rows = came[d][at : at + 128, lanes].astype(F32)
                        start = (2 * j + i) * e_loc + e
                        gdown[pl.ds(start, 128, stride=per), :] = rows


def pack_kernel(idx, w_qkv, w_out, router, const, vec, gain1, gain2, keep, swap, give, early, late, pairs):
    part = w_out.shape[1]
    owned = w_out.shape[0]
    rows = [r[...].astype(F32) for r in (router, const, vec, gain1, gain2)]
    rows.append(jnp.zeros((128 - 20, owned), F32))
    columns = jnp.transpose(jnp.concatenate(rows, axis=0))
    early[:, :part] = w_out[...]
    early[:, part:] = columns.astype(BF)
    for k in range(3):
        late[:, k * part : (k + 1) * part] = w_qkv[k]
        for p in range(4):
            if p < part // 128:
                pairs[p, :, k * 128 : (k + 1) * 128] = w_qkv[k, :, p * 128 : (p + 1) * 128]
            else:
                pairs[p, :, k * 128 : (k + 1) * 128] = jnp.zeros((owned, 128), BF)
    near, away = 2 * idx[S_BIT], 2 * (1 - idx[S_BIT])
    core = idx[S_CORE]
    keep[...] = pairs[near + core]
    swap[...] = pairs[away + core]
    give[:owned, :] = pairs[near + 1 - core]
    give[owned:, :] = pairs[away + 1 - core]


def final_kernel(tokens, mine, other, grad_res, small, grad):
    x = tokens[...].astype(F32)
    rstd = lax.rsqrt(jnp.mean(x * x, axis=-1, keepdims=True) + EPS)
    xhat = x * rstd
    gn = mine[...] + other[...].astype(F32)
    ghat = gn * small[C_GAIN1 : C_GAIN1 + 1]
    grad[...] = grad_res[...] + rstd * (
        ghat - xhat * jnp.mean(ghat * xhat, axis=-1, keepdims=True)
    )


def per_device(
    tokens, previous_layer_logits, lengths, routes, pair_order, gain_attn, w_qkv, w_out, gain_ffn,
    w_router, w_residual, w_const, const_vec, w_in, w_down, cotangent,
):
    seq_dev, slot_dev, width = tokens.shape
    n_all = previous_layer_logits.shape[2]
    tok = seq_dev * slot_dev
    heads = lax.axis_size("head")
    ring = lax.axis_size("ring")
    n_blk = 2 * ring
    n_seq = seq_dev * heads
    n_slots = slot_dev * n_blk
    e_loc = w_in.shape[1]
    n_share = ring // e_loc
    unit = w_in.shape[3]
    rows_here = gain_attn.shape[0]
    part = w_qkv.shape[2]
    capacity = 9 * 2 * tok // (8 * n_all)
    h = lax.axis_index("head")
    ring_at = lax.axis_index("ring")
    core = lax.axis_index("core")
    b = ring_at * 2 + core
    q = ring_at % e_loc
    swap = [(0, 1), (1, 0)]
    blk = ("ring", "core")
    barrier = lax.optimization_barrier

    def across(x):
        return lax.ppermute(x, "head", swap)

    def partner(x):
        return lax.ppermute(x, "core", swap)

    def join(parts):
        total = unit * len(parts)
        cube = jnp.concatenate([p[:width].reshape(width, 2, unit) for p in parts], axis=2)
        down = [p[width:].reshape(strips, unit, 2 * unit) for p in parts]
        down = [jnp.transpose(p, (1, 0, 2)).reshape(unit, -1, 2 * total) for p in down]
        down = jnp.transpose(jnp.concatenate(down, axis=0), (1, 0, 2))
        return jnp.concatenate(
            [cube.reshape(width, 2 * total), down.reshape(-1, 2 * total)], axis=0)

    def divide(full):
        total = full.shape[1] // 2
        cube = full[:width].reshape(width, 2, total // unit, unit)
        down = jnp.transpose(full[width:].reshape(-1, total, 2 * total), (1, 0, 2))
        down = down.reshape(total // unit, unit, strips, 2 * unit)
        return [
            jnp.concatenate(
                [cube[:, :, d].reshape(width, 2 * unit),
                 jnp.transpose(down[d], (1, 0, 2)).reshape(-1, 2 * unit)], axis=0)
            for d in range(total // unit)]

    def hop(x, d):
        return lax.ppermute(x, "ring", [(i, i ^ d) for i in range(ring)]) if d else x

    bit = [(ring_at >> i) & 1 for i in range(3)]
    more = [1 << i for i in range(3, ring.bit_length() - 1)]
    both_axes = ("head", "ring")

    def to_head(same):
        pairs = []
        for i in range(heads):
            for r in range(ring):
                third = (r >> 2) & 1
                target = third if same else 1 - third
                pairs.append((i * ring + r, target * ring + ((r & ~4) | (i << 2))))
        return pairs

    def xor_blocks(ring_base, offsets):
        ring_off = np.array([d for d, _ in offsets], np.int32)
        core_off = np.array([k for _, k in offsets], np.int32)
        return (ring_base ^ ring_off) * 2 + (core ^ core_off)

    seq_base = (ring_at & ~4) | (h << 2)
    x_off = [(0, 0), (1, 0), (4, 0), (5, 0)]
    for d in more:
        x_off = x_off + [(r ^ d, k) for r, k in x_off]
    x_off = x_off + [(r ^ 2, k) for r, k in x_off]
    x_off = x_off + [(r, 1) for r, _ in x_off]
    w_off = [(0, 0), (0, 1), (2, 0), (2, 1)]
    w_off = w_off + [(r ^ 4, k) for r, k in w_off]
    w_off = w_off + [(r ^ 1, k) for r, k in w_off]
    p_off = [(0, 0)]
    for d in (4, 2, 1):
        p_off = p_off + [(r ^ d, 0) for r, _ in p_off]
    p_off = p_off + [(r, 1) for r, _ in p_off]
    direct = ring == 8
    seq = 2 * bit[2] + bit[0]
    seq_len = lax.dynamic_index_in_dim(lengths, seq, 0, keepdims=False)
    scalars = [jnp.stack([h, seq_len, core, q, b, bit[1], h * 0, h * 0]), xor_blocks(seq_base, x_off)]
    w_table = S_TABLE + len(x_off)
    if direct:
        scalars += [xor_blocks(ring_at, w_off), xor_blocks(ring_at, p_off)]
        p_table = w_table + len(w_off)
    else:
        scalars += [jnp.zeros((8,), jnp.int32)]
        p_table = w_table
    idx = jnp.concatenate(scalars)

    flat_tokens = tokens.reshape(tok, width)
    near_rows = lax.dynamic_index_in_dim(tokens, bit[0], 0, keepdims=False)
    away_rows = lax.dynamic_index_in_dim(tokens, 1 - bit[0], 0, keepdims=False)
    w_phys = jnp.transpose(w_qkv, (1, 0, 2))
    gain_row_in = gain_attn[None, :]
    keep_w, swap_w, give_w, early, late = call(
        pack_kernel,
        [sds((rows_here, part), BF), sds((rows_here, part), BF), sds((2 * rows_here, part), BF),
         sds((rows_here, part + 128), BF), sds((rows_here, 3 * part), BF)],
        [idx, w_phys, w_out, jnp.transpose(w_router), jnp.transpose(w_const),
         jnp.transpose(const_vec), gain_row_in, gain_ffn[None, :]], smem=1,
        scratch=[pltpu.VMEM((4, rows_here, part), BF)], name="pack", far_in=range(1, 8))

    def spread_to(x, d):
        return jnp.concatenate([x, hop(x, d)], axis=0)

    def gathered(x):
        return [lax.all_gather(x, blk, axis=0, tiled=True)]

    p_rows = rows_here if direct else width
    w_rows = rows_here if direct else width
    two_blocks = jnp.concatenate([near_rows, hop(away_rows, 1)], axis=0)
    if direct:
        came_w = partner(give_w)
        early = spread_to(early, 4)
        two_blocks, came_w, early, routes, pair_order, cotangent = barrier(
            (two_blocks, came_w, early, routes, pair_order, cotangent))
        swapped = [hop(swap_w, 2), hop(came_w[rows_here:], 2)]
        early = spread_to(early, 2)
    x_parts = [lax.ppermute(two_blocks, both_axes, to_head(same)) for same in (True, False)]

    positions = b * slot_dev + jnp.arange(slot_dev, dtype=jnp.int32)
    own_len = lax.dynamic_slice_in_dim(lengths, h * seq_dev, seq_dev)
    valid = (positions[None, :] < own_len[:, None]).reshape(tok)
    route_rows = jnp.transpose(routes.reshape(tok, 2))
    order = jnp.transpose(pair_order.reshape(tok, 2)).reshape(2 * tok)
    route = route_rows.reshape(2 * tok)
    eligible = jnp.concatenate([valid, valid]) & (route < NEXP)
    before = (
        (route[:, None] == route[None, :]) & (order[None, :] < order[:, None]) & eligible[None, :]
    )
    rank = jnp.sum(before.astype(jnp.int32), axis=1)
    slot = jnp.where(eligible & (rank < capacity), route * capacity + rank, NEXP * capacity)
    slot = slot.reshape(2, tok)
    slot_rows = jnp.concatenate([slot, jnp.zeros((6, tok), jnp.int32)], axis=0)
    ints = jnp.concatenate(
        [routes.reshape(tok, 2), jnp.transpose(slot), valid[:, None].astype(jnp.int32),
         jnp.zeros((tok, 3), jnp.int32)], axis=1)

    cot = cotangent.reshape(tok, width)
    per_send = e_loc * capacity
    (send_g,) = call(
        send_grad_kernel, [sds((heads * n_share, per_send, width), BF)], [slot_rows, cot, ints],
        name="send_grad")

    def to_experts(rows):
        flat = rows.reshape(heads * ring * capacity, rows.shape[-1])
        return lax.all_to_all(flat, ("head", "ring"), 0, 0, tiled=True)

    if direct:
        x_parts, swapped, early, send_g, ints, slot_rows, w_in, w_down = barrier(
            (x_parts, swapped, early, send_g, ints, slot_rows, w_in, w_down))
    for d in more:
        x_parts = x_parts + [hop(a, d) for a in x_parts]
    x_parts = x_parts + [hop(a, 2) for a in x_parts]
    if direct:
        first = jnp.concatenate([keep_w, came_w[:rows_here], *swapped], axis=0)
        w_parts = [first, hop(first, 4)]
        early = spread_to(early, 1)
    g_rows = to_experts(send_g)

    strips = width // (2 * unit)
    bundle = jnp.concatenate(
        [jnp.transpose(w_in, (1, 0, 2, 3)).reshape(e_loc, width, 2 * unit),
         jnp.transpose(w_down.reshape(unit, e_loc, strips, 2 * unit), (1, 2, 0, 3)).reshape(
             e_loc, strips * unit, 2 * unit)], axis=1)
    shares = [lax.dynamic_index_in_dim(bundle, q ^ d, 0, keepdims=False) for d in range(e_loc)]

    frequency = 10000.0 ** (-(2.0 * jnp.arange(HD // 2, dtype=F32)) / HD)
    angles = jnp.arange(n_slots, dtype=jnp.int32).astype(F32)[:, None] * frequency[None, :]
    cos_all = jnp.concatenate([jnp.cos(angles)] * 4, axis=1)
    sin_all = jnp.concatenate([jnp.sin(angles)] * 4, axis=1)
    prev = previous_layer_logits.reshape(tok, n_all)
    prev_wide = jnp.pad(prev, ((0, 0), (0, 128 - n_all)))
    prev_logits = jnp.pad(
        jnp.dot(prev, w_residual, precision=lax.Precision.HIGHEST), ((0, 0), (0, 128 - n_all)))
    if direct:
        x_parts, w_parts, early, shares, prev_wide, prev_logits, cos_all, sin_all = barrier(
            (x_parts, w_parts, early, shares, prev_wide, prev_logits, cos_all, sin_all))
        w_parts = w_parts + [hop(a, 1) for a in w_parts]
        early_parts = [early, partner(early)]
    else:
        wide_w = jnp.pad(w_qkv, ((0, 0), (0, 0), (0, 512 - part))).reshape(rows_here, 3, 4, 128)
        wide_w = jnp.transpose(wide_w, (0, 2, 1, 3)).reshape(rows_here, -1)
        (whole_w,) = gathered(wide_w)
        w_parts = [lax.dynamic_slice_in_dim(whole_w, (2 * bit[1] + core) * part, part, 1)]
        early_parts = gathered(early)
    x_parts = x_parts + [partner(a) for a in x_parts]
    x_parts, w_parts, early_parts, g_rows, shares, late = barrier(
        (x_parts, w_parts, early_parts, g_rows, shares, late))
    pieces = [hop(shares[d], d) for d in range(e_loc)]
    if direct:
        late = spread_to(late, 4)

    attn_unit, lse, xn, qkv, early_all = call(
        functools.partial(
            attend_kernel, len(x_parts), len(w_parts), len(early_parts), w_rows, p_rows),
        [sds((n_slots, 128), BF), sds((8, n_slots), F32), sds((n_slots, width), BF),
         sds((n_slots, 384), BF), sds((width, part + 128), BF)],
        [idx, *x_parts, *w_parts, *early_parts, cos_all, sin_all], smem=1,
        scratch=[pltpu.VMEM((128, n_slots), BF), pltpu.VMEM((width, 384), BF)],
        flops=2 * n_slots * n_slots * 512 + 2 * n_slots * width * 384, name="attend",
        far_in=range(1, 3 + len(x_parts) + len(w_parts) + len(early_parts)),
        far_out=(0, 1, 2, 3, 4))
    attn_unit, late = barrier((attn_unit, late))

    def exchange(x):
        flat = x.reshape(n_blk * (x.size // x.shape[-1] // n_blk), x.shape[-1])
        return lax.all_to_all(flat, blk, 0, 0, tiled=True)

    attn_recv = exchange(attn_unit).reshape(n_blk, slot_dev, 128)
    attn_recv, pieces = barrier((attn_recv, pieces))
    pieces = pieces + [partner(p) for p in pieces]
    w_out_all = Columns(early_all, part, 0)
    mine, other, attn_low = call(
        out_kernel,
        [sds((tok, width), F32), sds((tok, width), BF), sds((n_seq * slot_dev, part), BF)],
        [idx, attn_recv, w_out_all], smem=1,
        scratch=[pltpu.VMEM((n_seq * slot_dev, width), F32)],
        flops=2 * n_seq * slot_dev * width * part, name="out", far_in=(2,), far_out=(2,))
    w_small_all = Columns(early_all, 128, part)
    send_x, residual, aux, small = call(
        route_kernel,
        [sds((heads * n_share, per_send, width + 128), BF), sds((tok, width), F32),
         sds((tok, 128), F32), sds((24, width), F32)],
        [flat_tokens, mine, across(other), w_small_all, prev_logits, ints, slot_rows],
        flops=tok * width * 1000, name="route", far_in=(3, 4, 5), far_out=(1, 2, 3))
    x_rows = to_experts(send_x)
    x_rows, pieces, late = barrier((x_rows, pieces, late))
    if direct:
        late = spread_to(late, 2)
    group = max(1, 128 // unit)
    if group > 1:
        pieces = [join(pieces[i : i + group]) for i in range(0, len(pieces), group)]
    back_rows, *grad_pieces = experts(x_rows, g_rows, pieces)
    back_rows, late = barrier((back_rows, late))
    back_recv = to_experts(back_rows)

    if group > 1:
        grad_pieces = [part_of for full in grad_pieces for part_of in divide(full)]
    ours = list(grad_pieces[:e_loc])
    theirs = [partner(p) for p in grad_pieces[e_loc:]]
    recv = back_recv.reshape(heads * n_share, per_send, 2 * width)
    added = call(
        functools.partial(pair_add_kernel, e_loc), [sds(p.shape, BF) for p in ours], ours + theirs,
        name="pair_add", far_in=range(2 * e_loc), far_out=range(e_loc))

    recv, added = barrier((recv, added))
    output, grad_res, grad_low, sums, resid = call(
        combine_kernel,
        [sds((tok, width), F32), sds((tok, width), F32), sds((tok, width), BF), sds((24, width), F32),
         sds((128, 128), F32)],
        [recv, residual, cot, small, w_small_all, ints, aux, prev_wide], flops=tok * width * 2000,
        name="combine", far_in=(1, 2, 3, 4, 5, 6, 7), far_out=(0, 1, 3, 4))

    came = [hop(added[d], d) for d in range(e_loc)]
    pay = (n_blk // 2, rows_here, part + 128)
    send_gv, keep, give = call(
        grad_vec_kernel,
        [sds((n_blk, slot_dev, 128), BF), sds(pay, F32), sds(pay, BF)],
        [idx, grad_low, across(grad_low), attn_low, w_out_all, sums, resid], smem=1,
        scratch=[pltpu.VMEM((n_seq * slot_dev, width), BF),
                 pltpu.VMEM((n_blk, rows_here, part + 128), F32)],
        flops=4 * n_seq * slot_dev * width * part, name="grad_vec", far_in=(3, 4), far_out=(1, 2))
    dout = exchange(send_gv)
    came_sum = partner(give)
    dout, came, came_sum, late = barrier((dout, came, came_sum, late))
    if direct:
        late = spread_to(late, 1)

    def halve(keep, came_sum, d):
        half = (keep.shape[0] // 2,) + keep.shape[1:]
        keep, give = call(
            halve_kernel, [sds(half, F32), sds(half, BF)], [keep, came_sum], name="halve")
        return keep, hop(give, d)

    steps = [1 << i for i in range(ring.bit_length() - 1)]
    keep, came_sum = halve(keep, came_sum, steps[0])
    (grad_unit,) = call(
        attend_back_kernel, [sds((n_slots, 384), BF)],
        [idx, qkv, dout, attn_unit, lse, cos_all, sin_all], smem=1,
        scratch=[pltpu.VMEM((128, n_slots), BF), pltpu.VMEM((n_slots, 128), F32),
                 pltpu.VMEM((n_slots, 128), F32)],
        flops=5 * n_slots * n_slots * 256, name="attend_back", far_in=(1, 3, 4, 5, 6), far_out=())
    grad_unit, came_sum = barrier((grad_unit, came_sum))
    grad_recv = exchange(grad_unit).reshape(n_blk, slot_dev, 384)
    late_parts = [late, partner(late)] if direct else gathered(late)
    (unit_dw,) = call(
        unit_dw_kernel, [sds((width, 384), BF)], [xn, grad_unit],
        flops=2 * n_slots * width * 384, name="unit_dw", far_in=(0,), room=20)

    for d in steps[1:]:
        keep, came_sum = halve(keep, came_sum, d)
    def by_source(parts):
        chosen = []
        for e in range(e_loc):
            value = parts[e_loc - 1]
            for d in range(e_loc - 1):
                value = jnp.where((q ^ d) == e, parts[d], value)
            chosen.append(value.astype(F32))
        return chosen

    if group == 1:
        in_sum, down_sum = call(
            functools.partial(place_kernel, e_loc),
            [sds((width * e_loc * 2, 128), F32), sds((width // 128 * e_loc * unit, 128), F32)],
            [idx, *came], smem=1, name="place", far_in=range(1, e_loc + 1), far_out=(0, 1))
        in_sum = in_sum.reshape(width, e_loc, 2, unit)
        down_sum = jnp.transpose(down_sum.reshape(unit, -1, e_loc, 128), (0, 2, 1, 3))
        down_sum = down_sum.reshape(unit, e_loc, width)
    else:
        in_sum = jnp.stack(by_source([p[:width].reshape(width, 2, unit) for p in came]), axis=1)
        down_sum = by_source([p[width:].reshape(strips, unit, 2 * unit) for p in came])
        down_sum = jnp.transpose(jnp.stack(down_sum, axis=0), (2, 0, 1, 3))
        down_sum = down_sum.reshape(unit, e_loc, width)
    grad_recv, unit_dw, in_sum, down_sum, came_sum = barrier(
        (grad_recv, unit_dw, in_sum, down_sum, came_sum))
    dw_recv = exchange(unit_dw).reshape(n_blk, rows_here, 384)
    out_sum, table = call(
        last_add_kernel, [sds((rows_here, part), F32), sds((rows_here, 128), F32)],
        [keep, came_sum], name="last_add")
    gain2_sum, router_sum, const_sum, vec_sum, resid_sum = call(
        functools.partial(small_kernel, n_all),
        [sds((1, rows_here), F32), sds((n_all, rows_here), F32), sds((4, rows_here), F32),
         sds((2, rows_here), F32), sds((n_all, n_all), F32)],
        [table, across(table)], name="small")

    gn_mine, gn_other = call(
        functools.partial(grad_qkv_kernel, len(late_parts), p_rows, p_table),
        [sds((tok, width), F32), sds((tok, width), BF)], [idx, grad_recv, *late_parts], smem=1,
        scratch=[pltpu.VMEM((n_seq * slot_dev, 3 * part), BF),
                 pltpu.VMEM((n_seq * slot_dev, width), F32), pltpu.VMEM((width, 3 * part), BF)],
        flops=2 * n_seq * slot_dev * width * 3 * part, name="grad_qkv", far_in=(2, 3), far_out=(0,))
    (grad_tokens,) = call(
        final_kernel, [sds((tok, width), F32)],
        [flat_tokens, gn_mine, across(gn_other), grad_res, small], name="final",
        far_in=(0, 1, 3, 4), far_out=(0,))
    dw_recv, grad_tokens, gain2_sum = barrier((dw_recv, grad_tokens, gain2_sum))
    qkv_sum, gain1_part = call(
        total_kernel, [sds((3, rows_here, part), F32), sds((8, rows_here), F32)],
        [dw_recv, w_phys, gain_row_in], name="total", far_in=(1, 2))
    gain1_sum = gain1_part[0] + across(gain1_part)[0]

    return (
        output.reshape(tokens.shape),
        grad_tokens.reshape(tokens.shape),
        gain1_sum,
        jnp.transpose(qkv_sum, (1, 0, 2)),
        out_sum,
        gain2_sum.reshape(rows_here),
        jnp.transpose(router_sum),
        resid_sum,
        jnp.transpose(const_sum),
        jnp.transpose(vec_sum),
        in_sum,
        down_sum,
    )


def solution(mesh):
    heads, blocks = mesh.devices.shape
    split = Mesh(mesh.devices.reshape(heads, blocks // 2, 2), ("head", "ring", "core"))
    blk = ("ring", "core")
    in_specs = (
        P("head", blk, None),
        P("head", blk, None),
        P(),
        P("head", blk, None),
        P("head", blk, None),
        P(blk),
        P(blk, None, "head"),
        P(blk, "head"),
        P(blk),
        P(blk, None),
        P(),
        P(blk, None),
        P(blk, None),
        P(None, "head", None, blk),
        P(blk, "head", None),
        P("head", blk, None),
    )
    out_specs = (
        P("head", blk, None),
        P("head", blk, None),
        P(blk),
        P(blk, None, "head"),
        P(blk, "head"),
        P(blk),
        P(blk, None),
        P(),
        P(blk, None),
        P(blk, None),
        P(None, "head", None, blk),
        P(blk, "head", None),
    )
    return jax.shard_map(
        per_device, mesh=split, in_specs=in_specs, out_specs=out_specs, check_vma=False
    )
```

```python
import functools
import math

import jax
import jax.numpy as jnp
import numpy as np
from jax import lax
from jax.experimental import pallas as pl
from jax.experimental.pallas import tpu as pltpu
from jax.sharding import Mesh
from jax.sharding import PartitionSpec as P

HD = 64
NEXP = 8
EPS = 1e-05
NEG = -1e30
BF = jnp.bfloat16
F32 = jnp.float32
MIB = 1 << 20
ANY2 = (((1,), (1,)), ((), ()))
MM = (((1,), (0,)), ((), ()))
C_CONST, C_VEC, C_GAIN1, C_GAIN2 = 12, 16, 18, 19
RESID = 32
S_HEAD, S_LEN, S_BASE, S_EXPERT, S_BLOCK, S_BIT, S_TABLE = 0, 1, 2, 3, 4, 5, 8


def dot(a, b, dims=MM):
    return lax.dot_general(a, b, dims, preferred_element_type=F32)


def whole_block(shape):
    return pl.BlockSpec(shape, lambda i: (0,) * len(shape), pipeline_mode=pl.Buffered(1))


def far(x):
    return pltpu.with_memory_space_constraint(x, pltpu.HBM)


class Columns:
    def __init__(self, array, count, at):
        self.array, self.at, self.window = array, (0, at // count), (array.shape[0], count)
        self.shape, self.dtype = self.window, array.dtype


def call(kernel, outs, args, smem=0, scratch=(), room=12, flops=0, name=None,
         far_in=(), far_out=()):
    sm = pl.BlockSpec(memory_space=pltpu.SMEM)
    total = sum(math.prod(a.shape) * a.dtype.itemsize for a in list(args) + list(outs))
    limit = total + sum(math.prod(a.shape) * a.dtype.itemsize for a in scratch) + room * MIB
    specs = [
        pl.BlockSpec(a.window, functools.partial(lambda at, i: at, a.at), pipeline_mode=pl.Buffered(1))
        if isinstance(a, Columns) else whole_block(a.shape) for a in args[smem:]]
    args = [a.array if isinstance(a, Columns) else a for a in args]
    args = [far(a) if i in far_in else a for i, a in enumerate(args)]
    shapes = tuple(pltpu.HBM(o.shape, o.dtype) if i in far_out else o for i, o in enumerate(outs))
    return pl.pallas_call(
        kernel,
        grid=(1,),
        out_shape=shapes,
        in_specs=[sm] * smem + specs,
        out_specs=tuple(whole_block(o.shape) for o in outs),
        scratch_shapes=list(scratch),
        compiler_params=pltpu.CompilerParams(vmem_limit_bytes=min(limit, 60 * MIB)),
        cost_estimate=pl.CostEstimate(flops=flops, bytes_accessed=total, transcendentals=0),
        name=name,
    )(*args)


def sds(shape, dtype):
    return jax.ShapeDtypeStruct(shape, dtype)


def unit_at(seq, pair):
    ring = (seq >> 1) * 4 + (pair >> 1) * 2 + (seq & 1)
    return ring * 2 + (pair & 1)


def idle_units(n_blk, n_seq, pairs):
    busy = {unit_at(q, p) for q in range(n_seq) for p in range(pairs)}
    return [u for u in range(n_blk) if u not in busy]


def halving_bits(n):
    return [0, 1, 3, 2] + list(range(4, n.bit_length() - 1))


def halving_order(n):
    bits = halving_bits(n)
    last = len(bits) - 1
    return [sum(((k >> (last - i)) & 1) << b for i, b in enumerate(bits)) for k in range(n)]


def gather_rows(dst, arrays, idx, base, rows):
    j = base
    for a in arrays:
        for i in range(a.shape[0] // rows):
            at = idx[j] * rows
            if rows % 16 == 0:
                at = pl.multiple_of(at, 16)
            dst[pl.ds(at, rows), :] = a[i * rows : (i + 1) * rows, :]
            j += 1


def lower_lanes(shape):
    return (lax.broadcasted_iota(jnp.int32, shape, 1) & 63) < 32


def turned(values):
    return jnp.where(
        lower_lanes(values.shape), -pltpu.roll(values, 96, 1), pltpu.roll(values, 32, 1)
    )


def head_mask(shape, which):
    lane = lax.broadcasted_iota(jnp.int32, shape, 1)
    return (lane >= 64) if which else (lane < 64)


def only(values, which):
    return jnp.where(head_mask(values.shape, which), values, jnp.zeros_like(values))


def scores_of(k_rows, q_head, first_query, limit_len):
    s = dot(k_rows, q_head, ANY2)
    key = lax.broadcasted_iota(jnp.int32, s.shape, 0)
    query = lax.broadcasted_iota(jnp.int32, (1, s.shape[1]), 1) + first_query
    last = jnp.minimum(query, limit_len - 1)
    return jnp.where(key <= last, s, NEG)


def each_block(total, block, fn):
    if total // block <= 4:
        for i in range(total // block):
            fn(i * block, (i + 1) * block)
    else:

        @pl.loop(0, total // block)
        def _(i):
            fn(pl.multiple_of(i * block, block), total)


def attend_kernel(n_x, n_w, n_p, w_rows, p_rows, idx, *refs):
    xs, ws, ps = refs[:n_x], refs[n_x : n_x + n_w], refs[n_x + n_w : n_x + n_w + n_p]
    cos, sin, out, lse, xn, qkv, early, wg, vt = refs[n_x + n_w + n_p :]
    total = qkv.shape[0]
    block = 256
    slots = 64
    limit_len = idx[S_LEN]
    j = S_TABLE + sum(a.shape[0] // slots for a in xs)
    gather_rows(wg, ws, idx, j, w_rows)
    gather_rows(early, ps, idx, j + sum(a.shape[0] // w_rows for a in ws), p_rows)
    columns = early[:, early.shape[1] - 128 :].astype(F32)
    gain = jnp.transpose(columns)[C_GAIN1 : C_GAIN1 + 1]
    j = S_TABLE
    for a in xs:
        for i in range(a.shape[0] // slots):
            x = a[i * slots : (i + 1) * slots, :].astype(F32)
            rstd = lax.rsqrt(jnp.mean(x * x, axis=-1, keepdims=True) + EPS)
            at = pl.ds(pl.multiple_of(idx[j] * slots, slots), slots)
            xn[at, :] = (x * rstd * gain).astype(BF)
            j += 1

    def project(start, _):
        at = pl.ds(start, block)
        y = dot(xn[at, :], wg[...])
        c, s = cos[at, :], sin[at, :]
        q, k = y[:, 0:128], y[:, 128:256]
        q = (q * c + turned(q) * s) * (1.0 / math.sqrt(HD))
        qkv[at, 0:128] = q.astype(BF)
        qkv[at, 128:256] = (k * c + turned(k) * s).astype(BF)
        qkv[at, 256:384] = y[:, 256:384].astype(BF)

    each_block(total, block, project)
    vt[...] = jnp.transpose(qkv[:, 256:384])

    def step(start, n_keys):
        q = qkv[pl.ds(start, block), 0:128]
        parts = []
        for h in range(2):
            s = scores_of(qkv[0:n_keys, 128:256], only(q, h), start, limit_len)
            m = jnp.max(s, axis=0, keepdims=True)
            p = jnp.exp(s - m)
            total_p = jnp.sum(p, axis=0, keepdims=True)
            o = dot(vt[h * 64 : (h + 1) * 64, 0:n_keys], p.astype(BF))
            parts.append(o / total_p)
            lse[h : h + 1, pl.ds(start, block)] = m + jnp.log(total_p)
        out[pl.ds(start, block), :] = jnp.transpose(jnp.concatenate(parts, axis=0)).astype(BF)

    each_block(total, block, step)


def unit_dw_kernel(xn, grad, dw):
    dw[...] = dot(jnp.transpose(xn[...]), grad[...]).astype(BF)


def attend_back_kernel(idx, qkv, dout, out, lse, cos, sin, grad, kt, dk, dv):
    total = qkv.shape[0]
    block = 256
    limit_len = idx[S_LEN]
    kt[...] = jnp.transpose(qkv[:, 128:256])
    dk[...] = jnp.zeros_like(dk)
    dv[...] = jnp.zeros_like(dv)

    def unrotate(values, at, size):
        c, s = cos[pl.ds(at, size), :], sin[pl.ds(at, size), :]
        return values * c - turned(values) * s

    def step(start, n_keys):
        q = qkv[pl.ds(start, block), 0:128]
        do = dout[pl.ds(start, block), :]
        prod_t = jnp.transpose(do.astype(F32) * out[pl.ds(start, block), :].astype(F32))
        probs, ds, dq = [], [], []
        for h in range(2):
            q_head, do_head = only(q, h), only(do, h)
            s = scores_of(qkv[0:n_keys, 128:256], q_head, start, limit_len)
            p = jnp.exp(s - lse[h : h + 1, pl.ds(start, block)])
            delta = jnp.sum(prod_t[h * 64 : (h + 1) * 64], axis=0, keepdims=True)
            dp = dot(qkv[0:n_keys, 256:384], do_head, ANY2)
            d = (p * (dp - delta)).astype(BF)
            probs.append(p.astype(BF))
            ds.append(d)
            dq.append(dot(kt[h * 64 : (h + 1) * 64, 0:n_keys], d))
        both_q = jnp.concatenate([only(q, 0), only(q, 1)], axis=0)
        both_do = jnp.concatenate([only(do, 0), only(do, 1)], axis=0)
        dv[0:n_keys, :] += dot(jnp.concatenate(probs, axis=1), both_do)
        dk[0:n_keys, :] += dot(jnp.concatenate(ds, axis=1), both_q)
        gq = jnp.transpose(jnp.concatenate(dq, axis=0)) * (1.0 / math.sqrt(HD))
        grad[pl.ds(start, block), 0:128] = unrotate(gq, start, block).astype(BF)

    each_block(total, block, step)

    def finish(start, _):
        at = pl.ds(start, block)
        grad[at, 128:256] = unrotate(dk[at, :], start, block).astype(BF)
        grad[at, 256:384] = dv[at, :].astype(BF)

    each_block(total, block, finish)


def out_kernel(idx, recv, wos, mine, other, attn, full):
    h = idx[S_HEAD]
    part = attn.shape[1]
    slots = recv.shape[1]
    n_seq = attn.shape[0] // slots
    for p in range(part // 128):
        for q in range(n_seq):
            attn[q * slots : (q + 1) * slots, p * 128 : (p + 1) * 128] = recv[unit_at(q, p)]
    full[...] = dot(attn[...], wos[...], ANY2)
    rows = mine.shape[0]
    mine[...] = full[pl.ds(h * rows, rows), :]
    other[...] = full[pl.ds((1 - h) * rows, rows), :].astype(BF)


def onehot_rows(slots, n_rows):
    at = lax.broadcasted_iota(jnp.int32, (n_rows, slots.shape[1]), 0)
    return jnp.where((at == slots[0:1]) | (at == slots[1:2]), 1.0, 0.0).astype(BF)


def spread(rows, send):
    per = send.shape[1]
    copies = send.shape[0] * per // rows.shape[0]
    for i in range(send.shape[0]):
        at = (i // copies) * per
        send[i] = rows[at : at + per]


def send_grad_kernel(slots, cot, ints, send):
    g = (cot[...] * ints[:, 4:5].astype(F32)).astype(BF)
    n_rows = send.shape[1] * 2
    spread(dot(onehot_rows(slots[...], n_rows), g).astype(BF), send)


def norm_two(residual, gain):
    rstd = lax.rsqrt(jnp.mean(residual * residual, axis=-1, keepdims=True) + EPS)
    xhat = residual * rstd
    return rstd, xhat, xhat * gain


def route_kernel(tokens, mine, other, wpack, prev_logits, ints, slots, send, residual, aux, small):
    res = tokens[...].astype(F32) + mine[...] + other[...].astype(F32)
    residual[...] = res
    small[...] = jnp.transpose(wpack[...].astype(F32))[: small.shape[0]]
    _, _, normed = norm_two(res, small[C_GAIN2 : C_GAIN2 + 1])
    low = normed.astype(BF)
    logits = dot(low, wpack[...]) + prev_logits[...]
    lane = lax.broadcasted_iota(jnp.int32, logits.shape, 1)

    def pick(which):
        return jnp.sum(jnp.where(lane == which, logits, 0.0), axis=1, keepdims=True)

    def pair_softmax(a, b):
        top = jnp.maximum(a, b)
        ea, eb = jnp.exp(a - top), jnp.exp(b - top)
        return ea / (ea + eb), eb / (ea + eb)

    p0, p1 = pair_softmax(pick(ints[:, 0:1]), pick(ints[:, 1:2]))
    a00, a01 = pair_softmax(pick(C_CONST), pick(C_CONST + 1))
    a10, a11 = pair_softmax(pick(C_CONST + 2), pick(C_CONST + 3))
    info = jnp.zeros_like(logits)
    for i, v in enumerate((p0, p1, a00, a01, a10, a11)):
        info = jnp.where(lane == i, v, info)
    aux[...] = info
    n_rows = send.shape[1] * 2
    tok = slots.shape[1]
    at = lax.broadcasted_iota(jnp.int32, (n_rows, tok), 0)
    first = jnp.where(at == slots[0:1], 1.0, 0.0).astype(BF)
    second = jnp.where(at == slots[1:2], 1.0, 0.0).astype(BF)

    def split(v, base):
        high = v.astype(BF).astype(F32)
        return jnp.where(lane == 0, high, jnp.where(lane == 1, v - high, base))

    extra = dot(first, split(p0, 0.0).astype(BF)) + dot(second, split(p1, 0.0).astype(BF))
    rows = jnp.concatenate([dot(first + second, low), extra], axis=1)
    spread(rows.astype(BF), send)


def expert_kernel(n_pieces, n_steps, x_ref, g_ref, *refs):
    w, back, grads = refs[:n_pieces], refs[n_pieces], refs[n_pieces + 1 : 2 * n_pieces + 1]
    wd_all = refs[2 * n_pieces + 1]
    acc = refs[2 * n_pieces + 2] if n_steps > 1 else None
    step = pl.program_id(0)
    width = g_ref.shape[1]
    two = w[0].shape[1]
    unit = two // 2
    strips = width // two

    @pl.when(step == 0)
    def _():
        for d in range(n_pieces):
            for j in range(strips):
                at = width + j * unit
                wd_all[d * unit : (d + 1) * unit, j * two : (j + 1) * two] = w[d][at : at + unit, :]

    x = x_ref[:, :width]
    g = g_ref[...]
    prob = jnp.sum(x_ref[:, width:].astype(F32), axis=1, keepdims=True)
    xt = jnp.transpose(x)
    g_scaled = (g.astype(F32) * prob).astype(BF)
    up_grad = dot(g, wd_all[...], ANY2) * prob
    hiddens = []
    grad_in = jnp.zeros((x.shape[0], width), F32)

    def keep(d, start, value):
        at = slice(start, start + value.shape[0])
        if n_steps == 1:
            grads[d][at, :] = value.astype(BF)
            return

        @pl.when(step == 0)
        def _():
            acc[d, at, :] = value

        @pl.when(step > 0)
        def _():
            acc[d, at, :] += value

        @pl.when(step == n_steps - 1)
        def _():
            grads[d][at, :] = acc[d, at, :].astype(BF)

    for d in range(n_pieces):
        both = dot(x, w[d][:width, :])
        gate, up = both[:, :unit], both[:, unit:]
        sig = 1.0 / (1.0 + jnp.exp(-gate))
        act = gate * sig
        hidden = (act * up).astype(BF)
        hiddens.append(hidden)
        gh = up_grad[:, d * unit : (d + 1) * unit]
        g_gate = gh * up * sig * (1.0 + gate * (1.0 - sig))
        g_both = jnp.concatenate([g_gate, gh * act], axis=1).astype(BF)
        grad_in += dot(g_both, w[d][:width, :], ANY2)
        keep(d, 0, dot(xt, g_both))
        gd = dot(jnp.transpose(hidden), g_scaled)
        for j in range(strips):
            keep(d, width + j * unit, gd[:, j * two : (j + 1) * two])
    back[:, :width] = dot(jnp.concatenate(hiddens, axis=1), wd_all[...]).astype(BF)
    back[:, width:] = grad_in.astype(BF)


def experts(x_rows, g_rows, pieces):
    n = len(pieces)
    rows, wide = x_rows.shape
    width = g_rows.shape[1]
    deep, two = pieces[0].shape
    unit = two // 2
    block = 384 if rows % 384 == 0 else rows
    steps = rows // block
    outs = [sds((rows, 2 * width), BF)] + [sds((deep, two), BF)] * n
    scratch = [pltpu.VMEM((n * unit, width), BF)]
    if steps > 1:
        scratch.append(pltpu.VMEM((n, deep, two), F32))
    return pl.pallas_call(
        functools.partial(expert_kernel, n, steps),
        grid=(steps,),
        in_specs=[
            pl.BlockSpec((block, wide), lambda i: (i, 0)),
            pl.BlockSpec((block, width), lambda i: (i, 0)),
        ]
        + [whole_block(a.shape) for a in pieces],
        out_specs=tuple(
            [pl.BlockSpec((block, 2 * width), lambda i: (i, 0))]
            + [whole_block(o.shape) for o in outs[1:]]
        ),
        out_shape=tuple(outs[:1] + [pltpu.HBM(o.shape, o.dtype) for o in outs[1:]]),
        scratch_shapes=scratch,
        compiler_params=pltpu.CompilerParams(vmem_limit_bytes=(30 if steps == 1 else 48) * MIB),
        cost_estimate=pl.CostEstimate(
            flops=18 * rows * width * unit * n,
            bytes_accessed=8 * rows * width + 12 * width * unit * n,
            transcendentals=0,
        ),
        name="experts",
    )(x_rows, far(g_rows), *[far(p) for p in pieces])


def combine_kernel(recv, residual, cot, small, wpack, ints, aux, prev, out, grad_res, grad_low, sums):
    res = residual[...]
    gain = small[C_GAIN2 : C_GAIN2 + 1]
    rstd, xhat, normed = norm_two(res, gain)
    low = normed.astype(BF)
    width = res.shape[1]
    heads = 2
    copies = recv.shape[0] // heads
    groups = []
    for h in range(heads):
        total = recv[h * copies].astype(F32)
        for r in range(1, copies):
            total = total + recv[h * copies + r].astype(F32)
        groups.append(total.astype(BF))
    rows = jnp.concatenate(groups, axis=0)
    valid = ints[:, 4:5].astype(F32)
    go = cot[...] * valid
    lane = lax.broadcasted_iota(jnp.int32, (res.shape[0], rows.shape[0]), 1)
    first = jnp.where(lane == ints[:, 2:3], 1.0, 0.0).astype(BF)
    second = jnp.where(lane == ints[:, 3:4], 1.0, 0.0).astype(BF)
    eo0 = dot(first, rows[:, :width])
    eo1 = dot(second, rows[:, :width])
    gin = dot(first + second, rows[:, width:])
    info = aux[...]
    p0, p1 = info[:, 0:1], info[:, 1:2]
    alpha = ((info[:, 2:3], info[:, 3:4]), (info[:, 4:5], info[:, 5:6]))
    r0, r1 = ints[:, 0:1], ints[:, 1:2]

    def at(route, which):
        return jnp.where(route == which, 1.0, 0.0)

    vec = (small[C_VEC : C_VEC + 1], small[C_VEC + 1 : C_VEC + 2])
    share0 = at(r0, NEXP + 1) + at(r0, NEXP + 2) * alpha[0][0] + at(r0, NEXP + 3) * alpha[1][0]
    share1 = at(r1, NEXP + 1) + at(r1, NEXP + 2) * alpha[0][0] + at(r1, NEXP + 3) * alpha[1][0]
    weight = [p0 * at(r0, NEXP + 2 + j) + p1 * at(r1, NEXP + 2 + j) for j in range(2)]
    mixed = (
        p0 * eo0
        + p1 * eo1
        + (p0 * share0 + p1 * share1) * normed
        + (weight[0] * alpha[0][1]) * vec[0]
        + (weight[1] * alpha[1][1]) * vec[1]
    )
    out[...] = valid * (res + mixed)

    def rowsum(v):
        return jnp.sum(v, axis=1, keepdims=True)

    s_norm = rowsum(go * normed)
    s_vec = [rowsum(go * vec[j]) for j in range(2)]
    gg0 = rowsum(go * eo0) + share0 * s_norm
    gg1 = rowsum(go * eo1) + share1 * s_norm
    for j in range(2):
        gg0 = gg0 + at(r0, NEXP + 2 + j) * alpha[j][1] * s_vec[j]
        gg1 = gg1 + at(r1, NEXP + 2 + j) * alpha[j][1] * s_vec[j]
    gsum = p0 * gg0 + p1 * gg1
    c0, c1 = p0 * (gg0 - gsum), p1 * (gg1 - gsum)
    wide = lax.broadcasted_iota(jnp.int32, (res.shape[0], 128), 1)
    dl = jnp.where(wide == r0, c0, 0.0) + jnp.where(wide == r1, c1, 0.0)
    coef = p0 * at(r0, NEXP + 1) + p1 * at(r1, NEXP + 1)
    vec_rows = []
    for j in range(2):
        ga0, ga1 = weight[j] * s_norm, weight[j] * s_vec[j]
        mean = alpha[j][0] * ga0 + alpha[j][1] * ga1
        dl = jnp.where(wide == C_CONST + 2 * j, alpha[j][0] * (ga0 - mean), dl)
        dl = jnp.where(wide == C_CONST + 2 * j + 1, alpha[j][1] * (ga1 - mean), dl)
        coef = coef + alpha[j][0] * weight[j]
        vec_rows.append(jnp.sum((alpha[j][1] * weight[j]) * go, axis=0, keepdims=True))
    dl = dl.astype(BF)
    dlt = jnp.transpose(dl)
    proj = dot(dlt, low)
    resid = lax.dot_general(
        jnp.transpose(prev[...]), jnp.where(wide < C_CONST, dl.astype(F32), 0.0), MM,
        precision=lax.Precision.HIGHEST, preferred_element_type=F32,
    )
    gn = gin + coef * go + dot(dl, wpack[...], ANY2)
    gain_row = jnp.sum(gn * xhat, axis=0, keepdims=True)
    row = lax.broadcasted_iota(jnp.int32, (24, 1), 0)
    table = jnp.where(row < C_VEC, proj[:24], 0.0)
    table = jnp.where(row == C_VEC, vec_rows[0], table)
    table = jnp.where(row == C_VEC + 1, vec_rows[1], table)
    sums[:24, :] = jnp.where(row == C_GAIN2, gain_row, table)
    sums[24:, :128] = resid[: sums.shape[0] - 24]
    sums[24:, 128:] = jnp.zeros((sums.shape[0] - 24, sums.shape[1] - 128), F32)
    ghat = gn * gain
    grad = go + rstd * (ghat - xhat * jnp.mean(ghat * xhat, axis=-1, keepdims=True))
    grad_res[...] = grad
    grad_low[...] = grad.astype(BF)


def grad_vec_kernel(idx, mine, other, attn, wos, sums, more_sums, send, keep, give, both, pay):
    h = idx[S_HEAD]
    rows = mine.shape[0]
    both[pl.ds(h * rows, rows), :] = mine[...]
    both[pl.ds((1 - h) * rows, rows), :] = other[...]
    part = attn.shape[1]
    g = both[...]
    gv = dot(g, wos[...]).astype(BF)
    slots = send.shape[1]
    n_seq = g.shape[0] // slots
    for p in range(part // 128):
        for q in range(n_seq):
            send[unit_at(q, p)] = gv[q * slots : (q + 1) * slots, p * 128 : (p + 1) * 128]
    for u in idle_units(send.shape[0], n_seq, part // 128):
        send[u] = jnp.zeros(send.shape[1:], BF)
    dw = dot(jnp.transpose(g), attn[...])
    total = sums[...] + more_sums[...]
    table = jnp.concatenate([total[:24], jnp.zeros((104, total.shape[1]), F32)], axis=0)
    columns = jnp.transpose(table)
    n, owned, _ = pay.shape
    resid = jnp.concatenate([total[24:, :128], jnp.zeros((88 + 24, 128), F32)], axis=0)
    block = pltpu.roll(resid[:owned, :], RESID, 1)
    for i in range(n):
        at = i * owned
        pay[i, :, :part] = dw[at : at + owned]
        pay[i, :, part:] = columns[at : at + owned] + block
    for k, offset in enumerate(halving_order(n)):
        value = pay[idx[S_BLOCK] ^ offset]
        if k < n // 2:
            keep[k] = value
        else:
            give[k - n // 2] = value.astype(BF)


def halve_kernel(mine, came, keep, give):
    half = keep.shape[0]
    keep[...] = mine[:half] + came[:half].astype(F32)
    give[...] = (mine[half:] + came[half:].astype(F32)).astype(BF)


def last_add_kernel(n_all, mine, came, dw, gain2, router, const, vec, resid):
    total = mine[0] + came[0].astype(F32)
    dw[...] = total[:, : dw.shape[1]]
    table = total[:, dw.shape[1] :]
    rows = jnp.transpose(table)
    router[...] = rows[:n_all]
    const[...] = rows[C_CONST:C_VEC]
    vec[...] = rows[C_VEC : C_VEC + 2]
    gain2[...] = rows[C_GAIN2 : C_GAIN2 + 1]
    resid[...] = table[:n_all, RESID : RESID + n_all]


def unit_back_kernel(idx, grad, w_pair, keep, give, full):
    slots = keep.shape[1]
    block = 256

    def step(start, _):
        at = pl.ds(start, block)
        full[at, :] = dot(grad[at, :], w_pair[...], ANY2)

    each_block(full.shape[0], block, step)
    for k in range(2):
        for n, (far, third, first) in enumerate((a, b, c) for a in (0, 4) for b in (0, 8) for c in (0, 2)):
            which = idx[S_BASE] ^ (k + far + third + first)
            rows = full[pl.ds(pl.multiple_of(which * slots, slots), slots), :]
            if k == 0:
                keep[n] = rows
            else:
                give[n] = rows.astype(BF)


def both_kernel(mine, came, first, second):
    total = mine[...] + came[...].astype(F32)
    half = first.shape[0]
    first[...] = total[:half].astype(BF)
    second[...] = total[half:].astype(BF)


def heads_kernel(a, b, own, away):
    total = a[...].astype(F32) + b[...].astype(F32)
    own[...] = total[0]
    away[...] = total[1].astype(BF)


def total_kernel(recv, w, gain, dw, gain_row):
    part = dw.shape[2]
    owned = dw.shape[1]
    column = jnp.transpose(jnp.broadcast_to(gain[...].astype(F32), (8, owned)))[:, 0:1]
    rowsum = jnp.zeros((owned, 1), F32)
    for p in range(part // 128):
        total = recv[unit_at(0, p)].astype(F32)
        for q in range(1, 4):
            total = total + recv[unit_at(q, p)].astype(F32)
        for k in range(3):
            piece = total[:, k * 128 : (k + 1) * 128]
            at = slice(p * 128, (p + 1) * 128)
            rowsum = rowsum + jnp.sum(piece * w[k, :, at].astype(F32), axis=1, keepdims=True)
            dw[k, :, at] = piece
    rowsum = rowsum / column
    gain_row[...] = jnp.transpose(jnp.broadcast_to(rowsum, (owned, 128)))[: gain_row.shape[0]]


def pair_add_kernel(n, *refs):
    for i in range(n):
        refs[2 * n + i][...] = (refs[i][...].astype(F32) + refs[n + i][...].astype(F32)).astype(BF)


def place_kernel(e_loc, idx, *refs):
    came, gin, gdown = refs[:e_loc], refs[e_loc], refs[e_loc + 1]
    width = gin.shape[0] // (2 * e_loc)
    strips = width // 256
    per = strips * 2 * e_loc
    for q in range(e_loc):

        @pl.when(idx[S_EXPERT] == q)
        def _():
            for d in range(e_loc):
                e = q ^ d
                for i in range(2):
                    lanes = slice(i * 128, (i + 1) * 128)
                    rows = came[d][0:width, lanes].astype(F32)
                    gin[pl.ds(2 * e + i, width, stride=2 * e_loc), :] = rows
                    for j in range(strips):
                        at = width + j * 128
                        rows = came[d][at : at + 128, lanes].astype(F32)
                        start = (2 * j + i) * e_loc + e
                        gdown[pl.ds(start, 128, stride=per), :] = rows


def pack_kernel(idx, w_qkv, w_out, router, const, vec, gain1, gain2, keep, swap, give, early, pairs):
    part = w_out.shape[1]
    owned = w_out.shape[0]
    rows = [r[...].astype(F32) for r in (router, const, vec, gain1, gain2)]
    rows.append(jnp.zeros((128 - 20, owned), F32))
    columns = jnp.transpose(jnp.concatenate(rows, axis=0))
    early[:, :part] = w_out[...]
    early[:, part:] = columns.astype(BF)
    for k in range(3):
        for p in range(4):
            if p < part // 128:
                pairs[p, :, k * 128 : (k + 1) * 128] = w_qkv[k, :, p * 128 : (p + 1) * 128]
            else:
                pairs[p, :, k * 128 : (k + 1) * 128] = jnp.zeros((owned, 128), BF)
    near, away = 2 * idx[0], 2 * (1 - idx[0])
    core = idx[1]
    keep[...] = pairs[near + core]
    swap[...] = pairs[away + core]
    give[:owned, :] = pairs[near + 1 - core]
    give[owned:, :] = pairs[away + 1 - core]


def final_kernel(idx, tokens, own, came, grad_res, small, grad, gn_rows):
    slots = own.shape[0]
    first = idx[S_BIT + 1]
    gn_rows[pl.ds(pl.multiple_of(first * slots, slots), slots), :] = own[...]
    gn_rows[pl.ds(pl.multiple_of((1 - first) * slots, slots), slots), :] = came[...].astype(F32)
    x = tokens[...].astype(F32)
    rstd = lax.rsqrt(jnp.mean(x * x, axis=-1, keepdims=True) + EPS)
    xhat = x * rstd
    ghat = gn_rows[...] * small[C_GAIN1 : C_GAIN1 + 1]
    grad[...] = grad_res[...] + rstd * (
        ghat - xhat * jnp.mean(ghat * xhat, axis=-1, keepdims=True)
    )


def per_device(
    tokens, previous_layer_logits, lengths, routes, pair_order, gain_attn, w_qkv, w_out, gain_ffn,
    w_router, w_residual, w_const, const_vec, w_in, w_down, cotangent,
):
    seq_dev, slot_dev, width = tokens.shape
    n_all = previous_layer_logits.shape[2]
    tok = seq_dev * slot_dev
    heads = lax.axis_size("head")
    ring = lax.axis_size("ring")
    n_blk = 2 * ring
    n_seq = seq_dev * heads
    n_slots = slot_dev * n_blk
    e_loc = w_in.shape[1]
    n_share = ring // e_loc
    unit = w_in.shape[3]
    rows_here = gain_attn.shape[0]
    part = w_qkv.shape[2]
    capacity = 9 * 2 * tok // (8 * n_all)
    h = lax.axis_index("head")
    ring_at = lax.axis_index("ring")
    core = lax.axis_index("core")
    b = ring_at * 2 + core
    q = ring_at % e_loc
    swap = [(0, 1), (1, 0)]
    blk = ("ring", "core")
    barrier = lax.optimization_barrier

    def across(x):
        return lax.ppermute(x, "head", swap)

    def partner(x):
        return lax.ppermute(x, "core", swap)

    def join(parts):
        total = unit * len(parts)
        cube = jnp.concatenate([p[:width].reshape(width, 2, unit) for p in parts], axis=2)
        down = [p[width:].reshape(strips, unit, 2 * unit) for p in parts]
        down = [jnp.transpose(p, (1, 0, 2)).reshape(unit, -1, 2 * total) for p in down]
        down = jnp.transpose(jnp.concatenate(down, axis=0), (1, 0, 2))
        return jnp.concatenate(
            [cube.reshape(width, 2 * total), down.reshape(-1, 2 * total)], axis=0)

    def divide(full):
        total = full.shape[1] // 2
        cube = full[:width].reshape(width, 2, total // unit, unit)
        down = jnp.transpose(full[width:].reshape(-1, total, 2 * total), (1, 0, 2))
        down = down.reshape(total // unit, unit, strips, 2 * unit)
        return [
            jnp.concatenate(
                [cube[:, :, d].reshape(width, 2 * unit),
                 jnp.transpose(down[d], (1, 0, 2)).reshape(-1, 2 * unit)], axis=0)
            for d in range(total // unit)]

    def hop(x, d):
        return lax.ppermute(x, "ring", [(i, i ^ d) for i in range(ring)]) if d else x

    bit = [(ring_at >> i) & 1 for i in range(3)]
    more = [1 << i for i in range(3, ring.bit_length() - 1)]
    both_axes = ("head", "ring")

    def to_head(same):
        pairs = []
        for i in range(heads):
            for r in range(ring):
                third = (r >> 2) & 1
                target = third if same else 1 - third
                pairs.append((i * ring + r, target * ring + ((r & ~4) | (i << 2))))
        return pairs

    def xor_blocks(ring_base, offsets):
        ring_off = np.array([d for d, _ in offsets], np.int32)
        core_off = np.array([k for _, k in offsets], np.int32)
        return (ring_base ^ ring_off) * 2 + (core ^ core_off)

    seq_base = (ring_at & ~4) | (h << 2)
    x_off = [(0, 0), (1, 0), (4, 0), (5, 0)]
    for d in more:
        x_off = x_off + [(r ^ d, k) for r, k in x_off]
    x_off = x_off + [(r ^ 2, k) for r, k in x_off]
    x_off = x_off + [(r, 1) for r, _ in x_off]
    w_off = [(0, 0), (0, 1), (2, 0), (2, 1)]
    w_off = w_off + [(r ^ 4, k) for r, k in w_off]
    w_off = w_off + [(r ^ 1, k) for r, k in w_off]
    p_off = [(0, 0)]
    for d in (4, 2, 1):
        p_off = p_off + [(r ^ d, 0) for r, _ in p_off]
    p_off = p_off + [(r, 1) for r, _ in p_off]
    direct = ring == 8
    flat_tokens = tokens.reshape(tok, width)
    near_rows = lax.dynamic_index_in_dim(tokens, bit[0], 0, keepdims=False)
    away_rows = lax.dynamic_index_in_dim(tokens, 1 - bit[0], 0, keepdims=False)
    w_phys = jnp.transpose(w_qkv, (1, 0, 2))
    gain_row_in = gain_attn[None, :]
    keep_w, swap_w, give_w, early = call(
        pack_kernel,
        [sds((rows_here, part), BF), sds((rows_here, part), BF), sds((2 * rows_here, part), BF),
         sds((rows_here, part + 128), BF)],
        [jnp.stack([bit[1], core]), w_phys, w_out, jnp.transpose(w_router), jnp.transpose(w_const),
         jnp.transpose(const_vec), gain_row_in, gain_ffn[None, :]], smem=1,
        scratch=[pltpu.VMEM((4, rows_here, part), BF)], name="pack", far_in=range(1, 8))

    def spread_to(x, d):
        return jnp.concatenate([x, hop(x, d)], axis=0)

    def gathered(x):
        return [lax.all_gather(x, blk, axis=0, tiled=True)]

    p_rows = rows_here if direct else width
    w_rows = rows_here if direct else width
    two_blocks = jnp.concatenate([near_rows, hop(away_rows, 1)], axis=0)
    if direct:
        came_w = partner(give_w)
        early = spread_to(early, 4)
        (two_blocks, routes, pair_order, cotangent, lengths, previous_layer_logits, w_in,
         w_down) = barrier((two_blocks, routes, pair_order, cotangent, lengths,
                            previous_layer_logits, w_in, w_down))
        swapped = [hop(swap_w, 2), hop(came_w[rows_here:], 2)]
    if direct:
        early = spread_to(early, 2)
    x_parts = [lax.ppermute(two_blocks, both_axes, to_head(same)) for same in (True, False)]

    seq = 2 * bit[2] + bit[0]
    seq_len = lax.dynamic_index_in_dim(lengths, seq, 0, keepdims=False)
    base = seq_base * 2 + core
    scalars = [jnp.stack([h, seq_len, base, q, b, bit[1], bit[0], h * 0]), xor_blocks(seq_base, x_off)]
    w_table = S_TABLE + len(x_off)
    if direct:
        scalars += [xor_blocks(ring_at, w_off), xor_blocks(ring_at, p_off)]
        p_table = w_table + len(w_off)
    else:
        scalars += [jnp.zeros((8,), jnp.int32)]
        p_table = w_table
    idx = jnp.concatenate(scalars)

    positions = b * slot_dev + jnp.arange(slot_dev, dtype=jnp.int32)
    own_len = lax.dynamic_slice_in_dim(lengths, h * seq_dev, seq_dev)
    valid = (positions[None, :] < own_len[:, None]).reshape(tok)
    route_rows = jnp.transpose(routes.reshape(tok, 2))
    order = jnp.transpose(pair_order.reshape(tok, 2)).reshape(2 * tok)
    route = route_rows.reshape(2 * tok)
    eligible = jnp.concatenate([valid, valid]) & (route < NEXP)
    before = (
        (route[:, None] == route[None, :]) & (order[None, :] < order[:, None]) & eligible[None, :]
    )
    rank = jnp.sum(before.astype(jnp.int32), axis=1)
    slot = jnp.where(eligible & (rank < capacity), route * capacity + rank, NEXP * capacity)
    slot = slot.reshape(2, tok)
    slot_rows = jnp.concatenate([slot, jnp.zeros((6, tok), jnp.int32)], axis=0)
    ints = jnp.concatenate(
        [routes.reshape(tok, 2), jnp.transpose(slot), valid[:, None].astype(jnp.int32),
         jnp.zeros((tok, 3), jnp.int32)], axis=1)

    strips = width // (2 * unit)
    bundle = jnp.concatenate(
        [jnp.transpose(w_in, (1, 0, 2, 3)).reshape(e_loc, width, 2 * unit),
         jnp.transpose(w_down.reshape(unit, e_loc, strips, 2 * unit), (1, 2, 0, 3)).reshape(
             e_loc, strips * unit, 2 * unit)], axis=1)
    shares = [lax.dynamic_index_in_dim(bundle, q ^ d, 0, keepdims=False) for d in range(e_loc)]

    if direct:
        x_parts, swapped, early, shares, ints, slot_rows, cotangent, lengths = barrier(
            (x_parts, swapped, early, shares, ints, slot_rows, cotangent, lengths))
    for d in more:
        x_parts = x_parts + [hop(a, d) for a in x_parts]
    x_parts = x_parts + [hop(a, 2) for a in x_parts]
    if direct:
        first = jnp.concatenate([keep_w, came_w[:rows_here], *swapped], axis=0)
        w_parts = [first, hop(first, 4), hop(first, 1)]
        early = spread_to(early, 1)
    cot = cotangent.reshape(tok, width)
    per_send = e_loc * capacity
    (send_g,) = call(
        send_grad_kernel, [sds((heads * n_share, per_send, width), BF)], [slot_rows, cot, ints],
        name="send_grad")

    def to_experts(rows):
        flat = rows.reshape(heads * ring * capacity, rows.shape[-1])
        return lax.all_to_all(flat, ("head", "ring"), 0, 0, tiled=True)

    frequency = 10000.0 ** (-(2.0 * jnp.arange(HD // 2, dtype=F32)) / HD)
    slots_here = jnp.arange(n_slots, dtype=jnp.int32) + jnp.minimum(lengths[0], 0)
    angles = slots_here.astype(F32)[:, None] * frequency[None, :]
    cos_all = jnp.concatenate([jnp.cos(angles)] * 4, axis=1)
    sin_all = jnp.concatenate([jnp.sin(angles)] * 4, axis=1)
    prev = previous_layer_logits.reshape(tok, n_all)
    prev_wide = jnp.pad(prev, ((0, 0), (0, 128 - n_all)))
    prev_logits = jnp.pad(
        jnp.dot(prev, w_residual, precision=lax.Precision.HIGHEST), ((0, 0), (0, 128 - n_all)))
    if direct:
        x_parts, w_parts, early, send_g, cos_all, sin_all = barrier(
            (x_parts, w_parts, early, send_g, cos_all, sin_all))
        w_parts = w_parts + [hop(w_parts[1], 1)]
        early_parts = [early, partner(early)]
    else:
        wide_w = jnp.pad(w_qkv, ((0, 0), (0, 0), (0, 512 - part))).reshape(rows_here, 3, 4, 128)
        wide_w = jnp.transpose(wide_w, (0, 2, 1, 3)).reshape(rows_here, -1)
        (whole_w,) = gathered(wide_w)
        w_parts = [lax.dynamic_slice_in_dim(whole_w, (2 * bit[1] + core) * part, part, 1)]
        early_parts = gathered(early)
    x_parts = x_parts + [partner(a) for a in x_parts]
    g_rows = to_experts(send_g)
    x_parts, w_parts, early_parts = barrier((x_parts, w_parts, early_parts))

    attn_unit, lse, xn, qkv, early_all, w_pair = call(
        functools.partial(
            attend_kernel, len(x_parts), len(w_parts), len(early_parts), w_rows, p_rows),
        [sds((n_slots, 128), BF), sds((8, n_slots), F32), sds((n_slots, width), BF),
         sds((n_slots, 384), BF), sds((width, part + 128), BF), sds((width, 384), BF)],
        [idx, *x_parts, *w_parts, *early_parts, cos_all, sin_all], smem=1,
        scratch=[pltpu.VMEM((128, n_slots), BF)],
        flops=2 * n_slots * n_slots * 512 + 2 * n_slots * width * 384, name="attend",
        far_in=range(1, 3 + len(x_parts) + len(w_parts) + len(early_parts)),
        far_out=(0, 1, 2, 3, 4, 5))
    attn_unit, g_rows, shares = barrier((attn_unit, g_rows, shares))

    pieces = [hop(shares[d], d) for d in range(e_loc)]

    def exchange(x):
        flat = x.reshape(n_blk * (x.size // x.shape[-1] // n_blk), x.shape[-1])
        return lax.all_to_all(flat, blk, 0, 0, tiled=True)

    attn_recv = exchange(attn_unit).reshape(n_blk, slot_dev, 128)
    attn_recv, pieces[:-1] = barrier((attn_recv, pieces[:-1]))
    w_out_all = Columns(early_all, part, 0)
    mine, other, attn_low = call(
        out_kernel,
        [sds((tok, width), F32), sds((tok, width), BF), sds((n_seq * slot_dev, part), BF)],
        [idx, attn_recv, w_out_all], smem=1,
        scratch=[pltpu.VMEM((n_seq * slot_dev, width), F32)],
        flops=2 * n_seq * slot_dev * width * part, name="out", far_in=(2,), far_out=(2,))
    w_small_all = Columns(early_all, 128, part)
    send_x, residual, aux, small = call(
        route_kernel,
        [sds((heads * n_share, per_send, width + 128), BF), sds((tok, width), F32),
         sds((tok, 128), F32), sds((24, width), F32)],
        [flat_tokens, mine, across(other), w_small_all, prev_logits, ints, slot_rows],
        flops=tok * width * 1000, name="route", far_in=(3, 4, 5), far_out=(1, 2, 3))
    send_x, pieces = barrier((send_x, pieces))
    pieces = pieces + [partner(p) for p in pieces]
    x_rows = to_experts(send_x)
    x_rows, pieces = barrier((x_rows, pieces))
    group = max(1, 128 // unit)
    if group > 1:
        pieces = [join(pieces[i : i + group]) for i in range(0, len(pieces), group)]
    back_rows, *grad_pieces = experts(x_rows, g_rows, pieces)
    back_recv = to_experts(back_rows)

    if group > 1:
        grad_pieces = [part_of for full in grad_pieces for part_of in divide(full)]
    ours = list(grad_pieces[:e_loc])
    theirs = [partner(p) for p in grad_pieces[e_loc:]]
    recv = back_recv.reshape(heads * n_share, per_send, 2 * width)
    added = call(
        functools.partial(pair_add_kernel, e_loc), [sds(p.shape, BF) for p in ours], ours + theirs,
        name="pair_add", far_in=range(2 * e_loc), far_out=range(e_loc))

    came = [added[0], hop(added[1], 1)]
    half_way = hop(added[3], 2)
    recv, added, came, half_way = barrier((recv, added, came, half_way))
    output, grad_res, grad_low, sums = call(
        combine_kernel,
        [sds((tok, width), F32), sds((tok, width), F32), sds((tok, width), BF), sds((40, width), F32)],
        [recv, residual, cot, small, w_small_all, ints, aux, prev_wide], flops=tok * width * 2000,
        name="combine", far_in=(1, 2, 3, 4, 5, 6, 7), far_out=(0, 1))

    came = came + [hop(added[2], 2), hop(half_way, 1)]
    pay = (n_blk // 2, rows_here, part + 128)
    send_gv, keep, give = call(
        grad_vec_kernel,
        [sds((n_blk, slot_dev, 128), BF), sds(pay, F32), sds(pay, BF)],
        [idx, grad_low, across(grad_low), attn_low, w_out_all, sums, across(sums)], smem=1,
        scratch=[pltpu.VMEM((n_seq * slot_dev, width), BF),
                 pltpu.VMEM((n_blk, rows_here, part + 128), F32)],
        flops=4 * n_seq * slot_dev * width * part, name="grad_vec", far_in=(3, 4), far_out=(1, 2))
    dout = exchange(send_gv)
    steps = [1 << (i - 1) for i in halving_bits(n_blk)[1:]]

    def halve(keep, came_sum, d):
        half = (keep.shape[0] // 2,) + keep.shape[1:]
        keep, give = call(
            halve_kernel, [sds(half, F32), sds(half, BF)], [keep, came_sum], name="halve")
        return keep, hop(give, d)

    came_sum = partner(give)
    dout, came, came_sum = barrier((dout, came, came_sum))

    keep, came_sum = halve(keep, came_sum, steps[0])
    (grad_unit,) = call(
        attend_back_kernel, [sds((n_slots, 384), BF)],
        [idx, qkv, dout, attn_unit, lse, cos_all, sin_all], smem=1,
        scratch=[pltpu.VMEM((128, n_slots), BF), pltpu.VMEM((n_slots, 128), F32),
                 pltpu.VMEM((n_slots, 128), F32)],
        flops=5 * n_slots * n_slots * 256, name="attend_back", far_in=(1, 3, 4, 5, 6), far_out=())
    grad_unit, came_sum = barrier((grad_unit, came_sum))
    rows8 = (8, slot_dev, width)
    gn_keep, gn_give = call(
        unit_back_kernel, [sds(rows8, F32), sds(rows8, BF)], [idx, grad_unit, w_pair], smem=1,
        scratch=[pltpu.VMEM((n_slots, width), F32)], flops=2 * n_slots * width * 384,
        name="unit_back", far_in=(2,), far_out=(0,))
    gn_came = partner(gn_give)
    (unit_dw,) = call(
        unit_dw_kernel, [sds((width, 384), BF)], [xn, grad_unit],
        flops=2 * n_slots * width * 384, name="unit_dw", far_in=(0,), room=20)
    gn_came, unit_dw, came_sum = barrier((gn_came, unit_dw, came_sum))
    gn_keep, gn_came = halve(gn_keep, gn_came, 2)
    keep, came_sum = halve(keep, came_sum, steps[1])
    dw_recv = exchange(unit_dw).reshape(n_blk, rows_here, 384)
    def by_source(parts):
        chosen = []
        for e in range(e_loc):
            value = parts[e_loc - 1]
            for d in range(e_loc - 1):
                value = jnp.where((q ^ d) == e, parts[d], value)
            chosen.append(value.astype(F32))
        return chosen

    if group == 1:
        in_sum, down_sum = call(
            functools.partial(place_kernel, e_loc),
            [sds((width * e_loc * 2, 128), F32), sds((width // 128 * e_loc * unit, 128), F32)],
            [idx, *came], smem=1, name="place", far_in=range(1, e_loc + 1), far_out=(0, 1))
        in_sum = in_sum.reshape(width, e_loc, 2, unit)
        down_sum = jnp.transpose(down_sum.reshape(unit, -1, e_loc, 128), (0, 2, 1, 3))
        down_sum = down_sum.reshape(unit, e_loc, width)
    else:
        in_sum = jnp.stack(by_source([p[:width].reshape(width, 2, unit) for p in came]), axis=1)
        down_sum = by_source([p[width:].reshape(strips, unit, 2 * unit) for p in came])
        down_sum = jnp.transpose(jnp.stack(down_sum, axis=0), (2, 0, 1, 3))
        down_sum = down_sum.reshape(unit, e_loc, width)
    gn_came, in_sum, down_sum, came_sum = barrier((gn_came, in_sum, down_sum, came_sum))
    rows2 = (2, slot_dev, width)
    gn_parts = call(
        both_kernel, [sds(rows2, BF), sds(rows2, BF)], [gn_keep, gn_came], name="both")
    gn_parts = [
        lax.ppermute(a, both_axes, [(t, f) for f, t in to_head(same)])
        for a, same in zip(gn_parts, (True, False))]
    for d in steps[2:]:
        keep, came_sum = halve(keep, came_sum, d)
    gn_parts, came_sum = barrier((gn_parts, came_sum))
    gn_own, gn_away = call(
        heads_kernel, [sds((slot_dev, width), F32), sds((slot_dev, width), BF)], list(gn_parts),
        name="heads")
    gn_near = hop(gn_away, 1)
    out_sum, gain2_sum, router_sum, const_sum, vec_sum, resid_sum = call(
        functools.partial(last_add_kernel, n_all),
        [sds((rows_here, part), F32), sds((1, rows_here), F32), sds((n_all, rows_here), F32),
         sds((4, rows_here), F32), sds((2, rows_here), F32), sds((n_all, n_all), F32)],
        [keep, came_sum], name="last_add")
    (grad_tokens,) = call(
        final_kernel, [sds((tok, width), F32)],
        [idx, flat_tokens, gn_own, gn_near, grad_res, small], smem=1,
        scratch=[pltpu.VMEM((tok, width), F32)], name="final", far_in=(1, 4, 5), far_out=(0,))
    dw_recv, grad_tokens, gain2_sum = barrier((dw_recv, grad_tokens, gain2_sum))
    qkv_sum, gain1_part = call(
        total_kernel, [sds((3, rows_here, part), F32), sds((8, rows_here), F32)],
        [dw_recv, w_phys, gain_row_in], name="total", far_in=(1, 2))
    gain1_sum = gain1_part[0] + across(gain1_part)[0]

    return (
        output.reshape(tokens.shape),
        grad_tokens.reshape(tokens.shape),
        gain1_sum,
        jnp.transpose(qkv_sum, (1, 0, 2)),
        out_sum,
        gain2_sum.reshape(rows_here),
        jnp.transpose(router_sum),
        resid_sum,
        jnp.transpose(const_sum),
        jnp.transpose(vec_sum),
        in_sum,
        down_sum,
    )


def solution(mesh):
    heads, blocks = mesh.devices.shape
    split = Mesh(mesh.devices.reshape(heads, blocks // 2, 2), ("head", "ring", "core"))
    blk = ("ring", "core")
    in_specs = (
        P("head", blk, None),
        P("head", blk, None),
        P(),
        P("head", blk, None),
        P("head", blk, None),
        P(blk),
        P(blk, None, "head"),
        P(blk, "head"),
        P(blk),
        P(blk, None),
        P(),
        P(blk, None),
        P(blk, None),
        P(None, "head", None, blk),
        P(blk, "head", None),
        P("head", blk, None),
    )
    out_specs = (
        P("head", blk, None),
        P("head", blk, None),
        P(blk),
        P(blk, None, "head"),
        P(blk, "head"),
        P(blk),
        P(blk, None),
        P(),
        P(blk, None),
        P(blk, None),
        P(None, "head", None, blk),
        P(blk, "head", None),
    )
    return jax.shard_map(
        per_device, mesh=split, in_specs=in_specs, out_specs=out_specs, check_vma=False
    )
```

```python
import functools
import math

import jax
import jax.numpy as jnp
import numpy as np
from jax import lax
from jax.experimental import pallas as pl
from jax.experimental.pallas import tpu as pltpu
from jax.sharding import Mesh
from jax.sharding import PartitionSpec as P

HD = 64
NEXP = 8
EPS = 1e-05
NEG = -1e30
BF = jnp.bfloat16
F32 = jnp.float32
MIB = 1 << 20
ANY2 = (((1,), (1,)), ((), ()))
MM = (((1,), (0,)), ((), ()))
C_CONST, C_VEC, C_GAIN1, C_GAIN2 = 12, 16, 18, 19
RESID = 32
S_HEAD, S_LEN, S_BASE, S_EXPERT, S_BLOCK, S_BIT, S_TABLE = 0, 1, 2, 3, 4, 5, 8


def dot(a, b, dims=MM):
    return lax.dot_general(a, b, dims, preferred_element_type=F32)


def whole_block(shape):
    return pl.BlockSpec(shape, lambda i: (0,) * len(shape), pipeline_mode=pl.Buffered(1))


def far(x):
    return pltpu.with_memory_space_constraint(x, pltpu.HBM)


class Columns:
    def __init__(self, array, count, at):
        self.array, self.at, self.window = array, (0, at // count), (array.shape[0], count)
        self.shape, self.dtype = self.window, array.dtype


def call(kernel, outs, args, smem=0, scratch=(), room=12, flops=0, name=None,
         far_in=(), far_out=()):
    sm = pl.BlockSpec(memory_space=pltpu.SMEM)
    total = sum(math.prod(a.shape) * a.dtype.itemsize for a in list(args) + list(outs))
    limit = total + sum(math.prod(a.shape) * a.dtype.itemsize for a in scratch) + room * MIB
    specs = [
        pl.BlockSpec(a.window, functools.partial(lambda at, i: at, a.at), pipeline_mode=pl.Buffered(1))
        if isinstance(a, Columns) else whole_block(a.shape) for a in args[smem:]]
    args = [a.array if isinstance(a, Columns) else a for a in args]
    args = [far(a) if i in far_in else a for i, a in enumerate(args)]
    shapes = tuple(pltpu.HBM(o.shape, o.dtype) if i in far_out else o for i, o in enumerate(outs))
    return pl.pallas_call(
        kernel,
        grid=(1,),
        out_shape=shapes,
        in_specs=[sm] * smem + specs,
        out_specs=tuple(whole_block(o.shape) for o in outs),
        scratch_shapes=list(scratch),
        compiler_params=pltpu.CompilerParams(vmem_limit_bytes=min(limit, 60 * MIB)),
        cost_estimate=pl.CostEstimate(flops=flops, bytes_accessed=total, transcendentals=0),
        name=name,
    )(*args)


def sds(shape, dtype):
    return jax.ShapeDtypeStruct(shape, dtype)


def unit_at(seq, pair):
    ring = (seq >> 1) * 4 + (pair >> 1) * 2 + (seq & 1)
    return ring * 2 + (pair & 1)


def idle_units(n_blk, n_seq, pairs):
    busy = {unit_at(q, p) for q in range(n_seq) for p in range(pairs)}
    return [u for u in range(n_blk) if u not in busy]


def halving_bits(n):
    return [0, 1, 3, 2] + list(range(4, n.bit_length() - 1))


def halving_order(n):
    bits = halving_bits(n)
    last = len(bits) - 1
    return [sum(((k >> (last - i)) & 1) << b for i, b in enumerate(bits)) for k in range(n)]


def gather_rows(dst, arrays, idx, base, rows):
    j = base
    for a in arrays:
        for i in range(a.shape[0] // rows):
            at = idx[j] * rows
            if rows % 16 == 0:
                at = pl.multiple_of(at, 16)
            dst[pl.ds(at, rows), :] = a[i * rows : (i + 1) * rows, :]
            j += 1


def lower_lanes(shape):
    return (lax.broadcasted_iota(jnp.int32, shape, 1) & 63) < 32


def turned(values):
    return jnp.where(
        lower_lanes(values.shape), -pltpu.roll(values, 96, 1), pltpu.roll(values, 32, 1)
    )


def head_mask(shape, which):
    lane = lax.broadcasted_iota(jnp.int32, shape, 1)
    return (lane >= 64) if which else (lane < 64)


def only(values, which):
    return jnp.where(head_mask(values.shape, which), values, jnp.zeros_like(values))


def scores_of(k_rows, q_head, first_query, limit_len):
    s = dot(k_rows, q_head, ANY2)
    key = lax.broadcasted_iota(jnp.int32, s.shape, 0)
    query = lax.broadcasted_iota(jnp.int32, (1, s.shape[1]), 1) + first_query
    last = jnp.minimum(query, limit_len - 1)
    return jnp.where(key <= last, s, NEG)


def each_block(total, block, fn):
    if total // block <= 4:
        for i in range(total // block):
            fn(i * block, (i + 1) * block)
    else:

        @pl.loop(0, total // block)
        def _(i):
            fn(pl.multiple_of(i * block, block), total)


def attend_kernel(n_x, n_w, n_p, w_rows, p_rows, idx, *refs):
    xs, ws, ps = refs[:n_x], refs[n_x : n_x + n_w], refs[n_x + n_w : n_x + n_w + n_p]
    cos, sin, out, lse, xn, qkv, early, wg, vt = refs[n_x + n_w + n_p :]
    total = qkv.shape[0]
    block = 256
    slots = 64
    limit_len = idx[S_LEN]
    j = S_TABLE + sum(a.shape[0] // slots for a in xs)
    gather_rows(wg, ws, idx, j, w_rows)
    gather_rows(early, ps, idx, j + sum(a.shape[0] // w_rows for a in ws), p_rows)
    columns = early[:, early.shape[1] - 128 :].astype(F32)
    gain = jnp.transpose(columns)[C_GAIN1 : C_GAIN1 + 1]
    j = S_TABLE
    for a in xs:
        for i in range(a.shape[0] // slots):
            x = a[i * slots : (i + 1) * slots, :].astype(F32)
            rstd = lax.rsqrt(jnp.mean(x * x, axis=-1, keepdims=True) + EPS)
            at = pl.ds(pl.multiple_of(idx[j] * slots, slots), slots)
            xn[at, :] = (x * rstd * gain).astype(BF)
            j += 1

    def project(start, _):
        at = pl.ds(start, block)
        y = dot(xn[at, :], wg[...])
        c, s = cos[at, :], sin[at, :]
        q, k = y[:, 0:128], y[:, 128:256]
        q = (q * c + turned(q) * s) * (1.0 / math.sqrt(HD))
        qkv[at, 0:128] = q.astype(BF)
        qkv[at, 128:256] = (k * c + turned(k) * s).astype(BF)
        qkv[at, 256:384] = y[:, 256:384].astype(BF)

    each_block(total, block, project)
    vt[...] = jnp.transpose(qkv[:, 256:384])

    def step(start, n_keys):
        q = qkv[pl.ds(start, block), 0:128]
        parts = []
        for h in range(2):
            s = scores_of(qkv[0:n_keys, 128:256], only(q, h), start, limit_len)
            m = jnp.max(s, axis=0, keepdims=True)
            p = jnp.exp(s - m)
            total_p = jnp.sum(p, axis=0, keepdims=True)
            o = dot(vt[h * 64 : (h + 1) * 64, 0:n_keys], p.astype(BF))
            parts.append(o / total_p)
            lse[h : h + 1, pl.ds(start, block)] = m + jnp.log(total_p)
        out[pl.ds(start, block), :] = jnp.transpose(jnp.concatenate(parts, axis=0)).astype(BF)

    each_block(total, block, step)


def unit_dw_kernel(xn, grad, dw):
    dw[...] = dot(jnp.transpose(xn[...]), grad[...]).astype(BF)


def attend_back_kernel(idx, qkv, dout, out, lse, cos, sin, grad, kt, dk, dv):
    total = qkv.shape[0]
    block = 256
    limit_len = idx[S_LEN]
    kt[...] = jnp.transpose(qkv[:, 128:256])
    dk[...] = jnp.zeros_like(dk)
    dv[...] = jnp.zeros_like(dv)

    def unrotate(values, at, size):
        c, s = cos[pl.ds(at, size), :], sin[pl.ds(at, size), :]
        return values * c - turned(values) * s

    def step(start, n_keys):
        q = qkv[pl.ds(start, block), 0:128]
        do = dout[pl.ds(start, block), :]
        prod_t = jnp.transpose(do.astype(F32) * out[pl.ds(start, block), :].astype(F32))
        probs, ds, dq = [], [], []
        for h in range(2):
            q_head, do_head = only(q, h), only(do, h)
            s = scores_of(qkv[0:n_keys, 128:256], q_head, start, limit_len)
            p = jnp.exp(s - lse[h : h + 1, pl.ds(start, block)])
            delta = jnp.sum(prod_t[h * 64 : (h + 1) * 64], axis=0, keepdims=True)
            dp = dot(qkv[0:n_keys, 256:384], do_head, ANY2)
            d = (p * (dp - delta)).astype(BF)
            probs.append(p.astype(BF))
            ds.append(d)
            dq.append(dot(kt[h * 64 : (h + 1) * 64, 0:n_keys], d))
        both_q = jnp.concatenate([only(q, 0), only(q, 1)], axis=0)
        both_do = jnp.concatenate([only(do, 0), only(do, 1)], axis=0)
        dv[0:n_keys, :] += dot(jnp.concatenate(probs, axis=1), both_do)
        dk[0:n_keys, :] += dot(jnp.concatenate(ds, axis=1), both_q)
        gq = jnp.transpose(jnp.concatenate(dq, axis=0)) * (1.0 / math.sqrt(HD))
        grad[pl.ds(start, block), 0:128] = unrotate(gq, start, block).astype(BF)

    each_block(total, block, step)

    def finish(start, _):
        at = pl.ds(start, block)
        grad[at, 128:256] = unrotate(dk[at, :], start, block).astype(BF)
        grad[at, 256:384] = dv[at, :].astype(BF)

    each_block(total, block, finish)


def out_kernel(idx, recv, wos, mine, other, attn, full):
    h = idx[S_HEAD]
    part = attn.shape[1]
    slots = recv.shape[1]
    n_seq = attn.shape[0] // slots
    for p in range(part // 128):
        for q in range(n_seq):
            attn[q * slots : (q + 1) * slots, p * 128 : (p + 1) * 128] = recv[unit_at(q, p)]
    full[...] = dot(attn[...], wos[...], ANY2)
    rows = mine.shape[0]
    mine[...] = full[pl.ds(h * rows, rows), :]
    other[...] = full[pl.ds((1 - h) * rows, rows), :].astype(BF)


def onehot_rows(slots, n_rows):
    at = lax.broadcasted_iota(jnp.int32, (n_rows, slots.shape[1]), 0)
    return jnp.where((at == slots[0:1]) | (at == slots[1:2]), 1.0, 0.0).astype(BF)


def spread(rows, send):
    per = send.shape[1]
    copies = send.shape[0] * per // rows.shape[0]
    for i in range(send.shape[0]):
        at = (i // copies) * per
        send[i] = rows[at : at + per]


def send_grad_kernel(slots, cot, ints, send):
    g = (cot[...] * ints[:, 4:5].astype(F32)).astype(BF)
    n_rows = send.shape[1] * 2
    spread(dot(onehot_rows(slots[...], n_rows), g).astype(BF), send)


def norm_two(residual, gain):
    rstd = lax.rsqrt(jnp.mean(residual * residual, axis=-1, keepdims=True) + EPS)
    xhat = residual * rstd
    return rstd, xhat, xhat * gain


def route_kernel(tokens, mine, other, wpack, prev_logits, ints, slots, send, residual, aux, small):
    res = tokens[...].astype(F32) + mine[...] + other[...].astype(F32)
    residual[...] = res
    small[...] = jnp.transpose(wpack[...].astype(F32))[: small.shape[0]]
    _, _, normed = norm_two(res, small[C_GAIN2 : C_GAIN2 + 1])
    low = normed.astype(BF)
    logits = dot(low, wpack[...]) + prev_logits[...]
    lane = lax.broadcasted_iota(jnp.int32, logits.shape, 1)

    def pick(which):
        return jnp.sum(jnp.where(lane == which, logits, 0.0), axis=1, keepdims=True)

    def pair_softmax(a, b):
        top = jnp.maximum(a, b)
        ea, eb = jnp.exp(a - top), jnp.exp(b - top)
        return ea / (ea + eb), eb / (ea + eb)

    p0, p1 = pair_softmax(pick(ints[:, 0:1]), pick(ints[:, 1:2]))
    a00, a01 = pair_softmax(pick(C_CONST), pick(C_CONST + 1))
    a10, a11 = pair_softmax(pick(C_CONST + 2), pick(C_CONST + 3))
    info = jnp.zeros_like(logits)
    for i, v in enumerate((p0, p1, a00, a01, a10, a11)):
        info = jnp.where(lane == i, v, info)
    aux[...] = info
    n_rows = send.shape[1] * 2
    tok = slots.shape[1]
    at = lax.broadcasted_iota(jnp.int32, (n_rows, tok), 0)
    first = jnp.where(at == slots[0:1], 1.0, 0.0).astype(BF)
    second = jnp.where(at == slots[1:2], 1.0, 0.0).astype(BF)

    def split(v, base):
        high = v.astype(BF).astype(F32)
        return jnp.where(lane == 0, high, jnp.where(lane == 1, v - high, base))

    extra = dot(first, split(p0, 0.0).astype(BF)) + dot(second, split(p1, 0.0).astype(BF))
    rows = jnp.concatenate([dot(first + second, low), extra], axis=1)
    spread(rows.astype(BF), send)


def expert_kernel(n_pieces, n_steps, x_ref, g_ref, *refs):
    w, back, grads = refs[:n_pieces], refs[n_pieces], refs[n_pieces + 1 : 2 * n_pieces + 1]
    wd_all = refs[2 * n_pieces + 1]
    acc = refs[2 * n_pieces + 2] if n_steps > 1 else None
    step = pl.program_id(0)
    width = g_ref.shape[1]
    two = w[0].shape[1]
    unit = two // 2
    strips = width // two

    @pl.when(step == 0)
    def _():
        for d in range(n_pieces):
            for j in range(strips):
                at = width + j * unit
                wd_all[d * unit : (d + 1) * unit, j * two : (j + 1) * two] = w[d][at : at + unit, :]

    x = x_ref[:, :width]
    g = g_ref[...]
    prob = jnp.sum(x_ref[:, width:].astype(F32), axis=1, keepdims=True)
    xt = jnp.transpose(x)
    g_scaled = (g.astype(F32) * prob).astype(BF)
    up_grad = dot(g, wd_all[...], ANY2) * prob
    hiddens = []
    grad_in = jnp.zeros((x.shape[0], width), F32)

    def keep(d, start, value):
        at = slice(start, start + value.shape[0])
        if n_steps == 1:
            grads[d][at, :] = value.astype(BF)
            return

        @pl.when(step == 0)
        def _():
            acc[d, at, :] = value

        @pl.when(step > 0)
        def _():
            acc[d, at, :] += value

        @pl.when(step == n_steps - 1)
        def _():
            grads[d][at, :] = acc[d, at, :].astype(BF)

    for d in range(n_pieces):
        both = dot(x, w[d][:width, :])
        gate, up = both[:, :unit], both[:, unit:]
        sig = 1.0 / (1.0 + jnp.exp(-gate))
        act = gate * sig
        hidden = (act * up).astype(BF)
        hiddens.append(hidden)
        gh = up_grad[:, d * unit : (d + 1) * unit]
        g_gate = gh * up * sig * (1.0 + gate * (1.0 - sig))
        g_both = jnp.concatenate([g_gate, gh * act], axis=1).astype(BF)
        grad_in += dot(g_both, w[d][:width, :], ANY2)
        keep(d, 0, dot(xt, g_both))
        gd = dot(jnp.transpose(hidden), g_scaled)
        for j in range(strips):
            keep(d, width + j * unit, gd[:, j * two : (j + 1) * two])
    back[:, :width] = dot(jnp.concatenate(hiddens, axis=1), wd_all[...]).astype(BF)
    back[:, width:] = grad_in.astype(BF)


def experts(x_rows, g_rows, pieces):
    n = len(pieces)
    rows, wide = x_rows.shape
    width = g_rows.shape[1]
    deep, two = pieces[0].shape
    unit = two // 2
    block = 384 if rows % 384 == 0 else rows
    steps = rows // block
    outs = [sds((rows, 2 * width), BF)] + [sds((deep, two), BF)] * n
    scratch = [pltpu.VMEM((n * unit, width), BF)]
    if steps > 1:
        scratch.append(pltpu.VMEM((n, deep, two), F32))
    return pl.pallas_call(
        functools.partial(expert_kernel, n, steps),
        grid=(steps,),
        in_specs=[
            pl.BlockSpec((block, wide), lambda i: (i, 0)),
            pl.BlockSpec((block, width), lambda i: (i, 0)),
        ]
        + [whole_block(a.shape) for a in pieces],
        out_specs=tuple(
            [pl.BlockSpec((block, 2 * width), lambda i: (i, 0))]
            + [whole_block(o.shape) for o in outs[1:]]
        ),
        out_shape=tuple(outs[:1] + [pltpu.HBM(o.shape, o.dtype) for o in outs[1:]]),
        scratch_shapes=scratch,
        compiler_params=pltpu.CompilerParams(vmem_limit_bytes=(30 if steps == 1 else 48) * MIB),
        cost_estimate=pl.CostEstimate(
            flops=18 * rows * width * unit * n,
            bytes_accessed=8 * rows * width + 12 * width * unit * n,
            transcendentals=0,
        ),
        name="experts",
    )(x_rows, far(g_rows), *[far(p) for p in pieces])


def combine_kernel(recv, residual, cot, small, wpack, ints, aux, prev, out, grad_res, grad_low, sums):
    res = residual[...]
    gain = small[C_GAIN2 : C_GAIN2 + 1]
    rstd, xhat, normed = norm_two(res, gain)
    low = normed.astype(BF)
    width = res.shape[1]
    heads = 2
    copies = recv.shape[0] // heads
    groups = []
    for h in range(heads):
        total = recv[h * copies].astype(F32)
        for r in range(1, copies):
            total = total + recv[h * copies + r].astype(F32)
        groups.append(total.astype(BF))
    rows = jnp.concatenate(groups, axis=0)
    valid = ints[:, 4:5].astype(F32)
    go = cot[...] * valid
    lane = lax.broadcasted_iota(jnp.int32, (res.shape[0], rows.shape[0]), 1)
    first = jnp.where(lane == ints[:, 2:3], 1.0, 0.0).astype(BF)
    second = jnp.where(lane == ints[:, 3:4], 1.0, 0.0).astype(BF)
    eo0 = dot(first, rows[:, :width])
    eo1 = dot(second, rows[:, :width])
    gin = dot(first + second, rows[:, width:])
    info = aux[...]
    p0, p1 = info[:, 0:1], info[:, 1:2]
    alpha = ((info[:, 2:3], info[:, 3:4]), (info[:, 4:5], info[:, 5:6]))
    r0, r1 = ints[:, 0:1], ints[:, 1:2]

    def at(route, which):
        return jnp.where(route == which, 1.0, 0.0)

    vec = (small[C_VEC : C_VEC + 1], small[C_VEC + 1 : C_VEC + 2])
    share0 = at(r0, NEXP + 1) + at(r0, NEXP + 2) * alpha[0][0] + at(r0, NEXP + 3) * alpha[1][0]
    share1 = at(r1, NEXP + 1) + at(r1, NEXP + 2) * alpha[0][0] + at(r1, NEXP + 3) * alpha[1][0]
    weight = [p0 * at(r0, NEXP + 2 + j) + p1 * at(r1, NEXP + 2 + j) for j in range(2)]
    mixed = (
        p0 * eo0
        + p1 * eo1
        + (p0 * share0 + p1 * share1) * normed
        + (weight[0] * alpha[0][1]) * vec[0]
        + (weight[1] * alpha[1][1]) * vec[1]
    )
    out[...] = valid * (res + mixed)

    def rowsum(v):
        return jnp.sum(v, axis=1, keepdims=True)

    s_norm = rowsum(go * normed)
    s_vec = [rowsum(go * vec[j]) for j in range(2)]
    gg0 = rowsum(go * eo0) + share0 * s_norm
    gg1 = rowsum(go * eo1) + share1 * s_norm
    for j in range(2):
        gg0 = gg0 + at(r0, NEXP + 2 + j) * alpha[j][1] * s_vec[j]
        gg1 = gg1 + at(r1, NEXP + 2 + j) * alpha[j][1] * s_vec[j]
    gsum = p0 * gg0 + p1 * gg1
    c0, c1 = p0 * (gg0 - gsum), p1 * (gg1 - gsum)
    wide = lax.broadcasted_iota(jnp.int32, (res.shape[0], 128), 1)
    dl = jnp.where(wide == r0, c0, 0.0) + jnp.where(wide == r1, c1, 0.0)
    coef = p0 * at(r0, NEXP + 1) + p1 * at(r1, NEXP + 1)
    vec_rows = []
    for j in range(2):
        ga0, ga1 = weight[j] * s_norm, weight[j] * s_vec[j]
        mean = alpha[j][0] * ga0 + alpha[j][1] * ga1
        dl = jnp.where(wide == C_CONST + 2 * j, alpha[j][0] * (ga0 - mean), dl)
        dl = jnp.where(wide == C_CONST + 2 * j + 1, alpha[j][1] * (ga1 - mean), dl)
        coef = coef + alpha[j][0] * weight[j]
        vec_rows.append(jnp.sum((alpha[j][1] * weight[j]) * go, axis=0, keepdims=True))
    dl = dl.astype(BF)
    dlt = jnp.transpose(dl)
    proj = dot(dlt, low)
    resid = lax.dot_general(
        jnp.transpose(prev[...]), jnp.where(wide < C_CONST, dl.astype(F32), 0.0), MM,
        precision=lax.Precision.HIGHEST, preferred_element_type=F32,
    )
    gn = gin + coef * go + dot(dl, wpack[...], ANY2)
    gain_row = jnp.sum(gn * xhat, axis=0, keepdims=True)
    row = lax.broadcasted_iota(jnp.int32, (24, 1), 0)
    table = jnp.where(row < C_VEC, proj[:24], 0.0)
    table = jnp.where(row == C_VEC, vec_rows[0], table)
    table = jnp.where(row == C_VEC + 1, vec_rows[1], table)
    sums[:24, :] = jnp.where(row == C_GAIN2, gain_row, table)
    sums[24:, :128] = resid[: sums.shape[0] - 24]
    sums[24:, 128:] = jnp.zeros((sums.shape[0] - 24, sums.shape[1] - 128), F32)
    ghat = gn * gain
    grad = go + rstd * (ghat - xhat * jnp.mean(ghat * xhat, axis=-1, keepdims=True))
    grad_res[...] = grad
    grad_low[...] = grad.astype(BF)


def grad_vec_kernel(idx, mine, other, wos, send, both):
    h = idx[S_HEAD]
    rows = mine.shape[0]
    both[pl.ds(h * rows, rows), :] = mine[...]
    both[pl.ds((1 - h) * rows, rows), :] = other[...]
    part = wos.shape[1]
    g = both[...]
    gv = dot(g, wos[...]).astype(BF)
    slots = send.shape[1]
    n_seq = g.shape[0] // slots
    for p in range(part // 128):
        for q in range(n_seq):
            send[unit_at(q, p)] = gv[q * slots : (q + 1) * slots, p * 128 : (p + 1) * 128]
    for u in idle_units(send.shape[0], n_seq, part // 128):
        send[u] = jnp.zeros(send.shape[1:], BF)


def pay_kernel(idx, both, attn, sums, more_sums, keep, give, pay):
    part = attn.shape[1]
    dw = dot(jnp.transpose(both[...]), attn[...])
    total = sums[...] + more_sums[...]
    table = jnp.concatenate([total[:24], jnp.zeros((104, total.shape[1]), F32)], axis=0)
    columns = jnp.transpose(table)
    n, owned, _ = pay.shape
    resid = jnp.concatenate([total[24:, :128], jnp.zeros((88 + 24, 128), F32)], axis=0)
    block = pltpu.roll(resid[:owned, :], RESID, 1)
    for i in range(n):
        at = i * owned
        pay[i, :, :part] = dw[at : at + owned]
        pay[i, :, part:] = columns[at : at + owned] + block
    for k, offset in enumerate(halving_order(n)):
        value = pay[idx[S_BLOCK] ^ offset]
        if k < n // 2:
            keep[k] = value
        else:
            give[k - n // 2] = value.astype(BF)


def halve_kernel(mine, came, keep, give):
    half = keep.shape[0]
    keep[...] = mine[:half] + came[:half].astype(F32)
    give[...] = (mine[half:] + came[half:].astype(F32)).astype(BF)


def last_add_kernel(n_all, mine, came, dw, gain2, router, const, vec, resid):
    total = mine[0] + came[0].astype(F32)
    dw[...] = total[:, : dw.shape[1]]
    table = total[:, dw.shape[1] :]
    rows = jnp.transpose(table)
    router[...] = rows[:n_all]
    const[...] = rows[C_CONST:C_VEC]
    vec[...] = rows[C_VEC : C_VEC + 2]
    gain2[...] = rows[C_GAIN2 : C_GAIN2 + 1]
    resid[...] = table[:n_all, RESID : RESID + n_all]


def unit_back_kernel(idx, grad, w_pair, keep, give, full):
    slots = keep.shape[1]
    block = 256

    def step(start, _):
        at = pl.ds(start, block)
        full[at, :] = dot(grad[at, :], w_pair[...], ANY2)

    each_block(full.shape[0], block, step)
    for k in range(2):
        for n, (far, third, first) in enumerate((a, b, c) for a in (0, 4) for b in (0, 8) for c in (0, 2)):
            which = idx[S_BASE] ^ (k + far + third + first)
            rows = full[pl.ds(pl.multiple_of(which * slots, slots), slots), :]
            if k == 0:
                keep[n] = rows
            else:
                give[n] = rows.astype(BF)


def both_kernel(mine, came, first, second):
    total = mine[...] + came[...].astype(F32)
    half = first.shape[0]
    first[...] = total[:half].astype(BF)
    second[...] = total[half:].astype(BF)


def heads_kernel(a, b, own, away):
    total = a[...].astype(F32) + b[...].astype(F32)
    own[...] = total[0]
    away[...] = total[1].astype(BF)


def total_kernel(recv, w, gain, dw, gain_row):
    part = dw.shape[2]
    owned = dw.shape[1]
    column = jnp.transpose(jnp.broadcast_to(gain[...].astype(F32), (8, owned)))[:, 0:1]
    rowsum = jnp.zeros((owned, 1), F32)
    for p in range(part // 128):
        total = recv[unit_at(0, p)].astype(F32)
        for q in range(1, 4):
            total = total + recv[unit_at(q, p)].astype(F32)
        for k in range(3):
            piece = total[:, k * 128 : (k + 1) * 128]
            at = slice(p * 128, (p + 1) * 128)
            rowsum = rowsum + jnp.sum(piece * w[k, :, at].astype(F32), axis=1, keepdims=True)
            dw[k, :, at] = piece
    rowsum = rowsum / column
    gain_row[...] = jnp.transpose(jnp.broadcast_to(rowsum, (owned, 128)))[: gain_row.shape[0]]


def pair_add_kernel(n, *refs):
    for i in range(n):
        refs[2 * n + i][...] = (refs[i][...].astype(F32) + refs[n + i][...].astype(F32)).astype(BF)


def place_kernel(e_loc, idx, *refs):
    came, gin, gdown = refs[:e_loc], refs[e_loc], refs[e_loc + 1]
    width = gin.shape[0] // (2 * e_loc)
    strips = width // 256
    for q in range(e_loc):

        @pl.when(idx[S_EXPERT] == q)
        def _():
            for d in range(e_loc):
                e = q ^ d
                for i in range(2):
                    lanes = slice(i * 128, (i + 1) * 128)
                    rows = came[d][0:width, lanes].astype(F32)
                    gin[pl.ds(2 * e + i, width, stride=2 * e_loc), :] = rows
                    for j in range(strips):
                        at = width + j * 128
                        rows = came[d][at : at + 128, lanes].astype(F32)
                        at = (2 * j + i) * 128
                        gdown[:, e, at : at + 128] = rows


def pack_kernel(idx, w_qkv, w_out, router, const, vec, gain1, gain2, keep, swap, give, early, pairs):
    part = w_out.shape[1]
    owned = w_out.shape[0]
    rows = [r[...].astype(F32) for r in (router, const, vec, gain1, gain2)]
    rows.append(jnp.zeros((128 - 20, owned), F32))
    columns = jnp.transpose(jnp.concatenate(rows, axis=0))
    early[:, :part] = w_out[...]
    early[:, part:] = columns.astype(BF)
    for k in range(3):
        for p in range(4):
            if p < part // 128:
                pairs[p, :, k * 128 : (k + 1) * 128] = w_qkv[k, :, p * 128 : (p + 1) * 128]
            else:
                pairs[p, :, k * 128 : (k + 1) * 128] = jnp.zeros((owned, 128), BF)
    near, away = 2 * idx[0], 2 * (1 - idx[0])
    core = idx[1]
    keep[...] = pairs[near + core]
    swap[...] = pairs[away + core]
    give[:owned, :] = pairs[near + 1 - core]
    give[owned:, :] = pairs[away + 1 - core]


def final_kernel(idx, tokens, own, came, grad_res, small, grad, gn_rows):
    slots = own.shape[0]
    first = idx[S_BIT + 1]
    gn_rows[pl.ds(pl.multiple_of(first * slots, slots), slots), :] = own[...]
    gn_rows[pl.ds(pl.multiple_of((1 - first) * slots, slots), slots), :] = came[...].astype(F32)
    x = tokens[...].astype(F32)
    rstd = lax.rsqrt(jnp.mean(x * x, axis=-1, keepdims=True) + EPS)
    xhat = x * rstd
    ghat = gn_rows[...] * small[C_GAIN1 : C_GAIN1 + 1]
    grad[...] = grad_res[...] + rstd * (
        ghat - xhat * jnp.mean(ghat * xhat, axis=-1, keepdims=True)
    )


def per_device(
    tokens, previous_layer_logits, lengths, routes, pair_order, gain_attn, w_qkv, w_out, gain_ffn,
    w_router, w_residual, w_const, const_vec, w_in, w_down, cotangent,
):
    seq_dev, slot_dev, width = tokens.shape
    n_all = previous_layer_logits.shape[2]
    tok = seq_dev * slot_dev
    heads = lax.axis_size("head")
    ring = lax.axis_size("ring")
    n_blk = 2 * ring
    n_seq = seq_dev * heads
    n_slots = slot_dev * n_blk
    e_loc = w_in.shape[1]
    n_share = ring // e_loc
    unit = w_in.shape[3]
    rows_here = gain_attn.shape[0]
    part = w_qkv.shape[2]
    capacity = 9 * 2 * tok // (8 * n_all)
    h = lax.axis_index("head")
    ring_at = lax.axis_index("ring")
    core = lax.axis_index("core")
    b = ring_at * 2 + core
    q = ring_at % e_loc
    swap = [(0, 1), (1, 0)]
    blk = ("ring", "core")
    barrier = lax.optimization_barrier

    def across(x):
        return lax.ppermute(x, "head", swap)

    def partner(x):
        return lax.ppermute(x, "core", swap)

    def join(parts):
        total = unit * len(parts)
        cube = jnp.concatenate([p[:width].reshape(width, 2, unit) for p in parts], axis=2)
        down = [p[width:].reshape(strips, unit, 2 * unit) for p in parts]
        down = [jnp.transpose(p, (1, 0, 2)).reshape(unit, -1, 2 * total) for p in down]
        down = jnp.transpose(jnp.concatenate(down, axis=0), (1, 0, 2))
        return jnp.concatenate(
            [cube.reshape(width, 2 * total), down.reshape(-1, 2 * total)], axis=0)

    def divide(full):
        total = full.shape[1] // 2
        cube = full[:width].reshape(width, 2, total // unit, unit)
        down = jnp.transpose(full[width:].reshape(-1, total, 2 * total), (1, 0, 2))
        down = down.reshape(total // unit, unit, strips, 2 * unit)
        return [
            jnp.concatenate(
                [cube[:, :, d].reshape(width, 2 * unit),
                 jnp.transpose(down[d], (1, 0, 2)).reshape(-1, 2 * unit)], axis=0)
            for d in range(total // unit)]

    def hop(x, d):
        return lax.ppermute(x, "ring", [(i, i ^ d) for i in range(ring)]) if d else x

    bit = [(ring_at >> i) & 1 for i in range(3)]
    more = [1 << i for i in range(3, ring.bit_length() - 1)]
    both_axes = ("head", "ring")

    def to_head(same):
        pairs = []
        for i in range(heads):
            for r in range(ring):
                third = (r >> 2) & 1
                target = third if same else 1 - third
                pairs.append((i * ring + r, target * ring + ((r & ~4) | (i << 2))))
        return pairs

    def xor_blocks(ring_base, offsets):
        ring_off = np.array([d for d, _ in offsets], np.int32)
        core_off = np.array([k for _, k in offsets], np.int32)
        return (ring_base ^ ring_off) * 2 + (core ^ core_off)

    seq_base = (ring_at & ~4) | (h << 2)
    x_off = [(0, 0), (1, 0), (4, 0), (5, 0)]
    for d in more:
        x_off = x_off + [(r ^ d, k) for r, k in x_off]
    x_off = x_off + [(r ^ 2, k) for r, k in x_off]
    x_off = x_off + [(r, 1) for r, _ in x_off]
    w_off = [(0, 0), (0, 1), (2, 0), (2, 1)]
    w_off = w_off + [(r ^ 4, k) for r, k in w_off]
    w_off = w_off + [(r ^ 1, k) for r, k in w_off]
    p_off = [(0, 0)]
    for d in (4, 2, 1):
        p_off = p_off + [(r ^ d, 0) for r, _ in p_off]
    p_off = p_off + [(r, 1) for r, _ in p_off]
    direct = ring == 8
    flat_tokens = tokens.reshape(tok, width)
    near_rows = lax.dynamic_index_in_dim(tokens, bit[0], 0, keepdims=False)
    away_rows = lax.dynamic_index_in_dim(tokens, 1 - bit[0], 0, keepdims=False)
    w_phys = jnp.transpose(w_qkv, (1, 0, 2))
    gain_row_in = gain_attn[None, :]
    keep_w, swap_w, give_w, early = call(
        pack_kernel,
        [sds((rows_here, part), BF), sds((rows_here, part), BF), sds((2 * rows_here, part), BF),
         sds((rows_here, part + 128), BF)],
        [jnp.stack([bit[1], core]), w_phys, w_out, jnp.transpose(w_router), jnp.transpose(w_const),
         jnp.transpose(const_vec), gain_row_in, gain_ffn[None, :]], smem=1,
        scratch=[pltpu.VMEM((4, rows_here, part), BF)], name="pack", far_in=range(1, 8))

    def spread_to(x, d):
        return jnp.concatenate([x, hop(x, d)], axis=0)

    def gathered(x):
        return [lax.all_gather(x, blk, axis=0, tiled=True)]

    p_rows = rows_here if direct else width
    w_rows = rows_here if direct else width
    two_blocks = jnp.concatenate([near_rows, hop(away_rows, 1)], axis=0)
    if direct:
        came_w = partner(give_w)
        early = spread_to(early, 4)
        (two_blocks, routes, pair_order, cotangent, lengths, previous_layer_logits, w_in,
         w_down) = barrier((two_blocks, routes, pair_order, cotangent, lengths,
                            previous_layer_logits, w_in, w_down))
        swapped = [hop(swap_w, 2), hop(came_w[rows_here:], 2)]
    if direct:
        early = spread_to(early, 2)
    x_parts = [lax.ppermute(two_blocks, both_axes, to_head(same)) for same in (True, False)]

    seq = 2 * bit[2] + bit[0]
    seq_len = lax.dynamic_index_in_dim(lengths, seq, 0, keepdims=False)
    base = seq_base * 2 + core
    scalars = [jnp.stack([h, seq_len, base, q, b, bit[1], bit[0], h * 0]), xor_blocks(seq_base, x_off)]
    w_table = S_TABLE + len(x_off)
    if direct:
        scalars += [xor_blocks(ring_at, w_off), xor_blocks(ring_at, p_off)]
        p_table = w_table + len(w_off)
    else:
        scalars += [jnp.zeros((8,), jnp.int32)]
        p_table = w_table
    idx = jnp.concatenate(scalars)

    positions = b * slot_dev + jnp.arange(slot_dev, dtype=jnp.int32)
    own_len = lax.dynamic_slice_in_dim(lengths, h * seq_dev, seq_dev)
    valid = (positions[None, :] < own_len[:, None]).reshape(tok)
    route_rows = jnp.transpose(routes.reshape(tok, 2))
    order = jnp.transpose(pair_order.reshape(tok, 2)).reshape(2 * tok)
    route = route_rows.reshape(2 * tok)
    eligible = jnp.concatenate([valid, valid]) & (route < NEXP)
    before = (
        (route[:, None] == route[None, :]) & (order[None, :] < order[:, None]) & eligible[None, :]
    )
    rank = jnp.sum(before.astype(jnp.int32), axis=1)
    slot = jnp.where(eligible & (rank < capacity), route * capacity + rank, NEXP * capacity)
    slot = slot.reshape(2, tok)
    slot_rows = jnp.concatenate([slot, jnp.zeros((6, tok), jnp.int32)], axis=0)
    ints = jnp.concatenate(
        [routes.reshape(tok, 2), jnp.transpose(slot), valid[:, None].astype(jnp.int32),
         jnp.zeros((tok, 3), jnp.int32)], axis=1)

    strips = width // (2 * unit)
    bundle = jnp.concatenate(
        [jnp.transpose(w_in, (1, 0, 2, 3)).reshape(e_loc, width, 2 * unit),
         jnp.transpose(w_down.reshape(unit, e_loc, strips, 2 * unit), (1, 2, 0, 3)).reshape(
             e_loc, strips * unit, 2 * unit)], axis=1)
    shares = [lax.dynamic_index_in_dim(bundle, q ^ d, 0, keepdims=False) for d in range(e_loc)]

    if direct:
        x_parts, swapped, early, shares, ints, slot_rows, cotangent, lengths = barrier(
            (x_parts, swapped, early, shares, ints, slot_rows, cotangent, lengths))
    for d in more:
        x_parts = x_parts + [hop(a, d) for a in x_parts]
    x_parts = x_parts + [hop(a, 2) for a in x_parts]
    if direct:
        first = jnp.concatenate([keep_w, came_w[:rows_here], *swapped], axis=0)
        w_parts = [first, hop(first, 4), hop(first, 1)]
        early = spread_to(early, 1)
    cot = cotangent.reshape(tok, width)
    per_send = e_loc * capacity
    (send_g,) = call(
        send_grad_kernel, [sds((heads * n_share, per_send, width), BF)], [slot_rows, cot, ints],
        name="send_grad")

    def to_experts(rows):
        flat = rows.reshape(heads * ring * capacity, rows.shape[-1])
        return lax.all_to_all(flat, ("head", "ring"), 0, 0, tiled=True)

    frequency = 10000.0 ** (-(2.0 * jnp.arange(HD // 2, dtype=F32)) / HD)
    slots_here = jnp.arange(n_slots, dtype=jnp.int32) + jnp.minimum(lengths[0], 0)
    angles = slots_here.astype(F32)[:, None] * frequency[None, :]
    cos_all = jnp.concatenate([jnp.cos(angles)] * 4, axis=1)
    sin_all = jnp.concatenate([jnp.sin(angles)] * 4, axis=1)
    prev = previous_layer_logits.reshape(tok, n_all)
    prev_wide = jnp.pad(prev, ((0, 0), (0, 128 - n_all)))
    prev_logits = jnp.pad(
        jnp.dot(prev, w_residual, precision=lax.Precision.HIGHEST), ((0, 0), (0, 128 - n_all)))
    if direct:
        x_parts, w_parts, early, send_g, cos_all, sin_all = barrier(
            (x_parts, w_parts, early, send_g, cos_all, sin_all))
        w_parts = w_parts + [hop(w_parts[1], 1)]
        early_parts = [early, partner(early)]
    else:
        wide_w = jnp.pad(w_qkv, ((0, 0), (0, 0), (0, 512 - part))).reshape(rows_here, 3, 4, 128)
        wide_w = jnp.transpose(wide_w, (0, 2, 1, 3)).reshape(rows_here, -1)
        (whole_w,) = gathered(wide_w)
        w_parts = [lax.dynamic_slice_in_dim(whole_w, (2 * bit[1] + core) * part, part, 1)]
        early_parts = gathered(early)
    x_parts = x_parts + [partner(a) for a in x_parts]
    g_rows = to_experts(send_g)
    x_parts, w_parts, early_parts = barrier((x_parts, w_parts, early_parts))

    attn_unit, lse, xn, qkv, early_all, w_pair = call(
        functools.partial(
            attend_kernel, len(x_parts), len(w_parts), len(early_parts), w_rows, p_rows),
        [sds((n_slots, 128), BF), sds((8, n_slots), F32), sds((n_slots, width), BF),
         sds((n_slots, 384), BF), sds((width, part + 128), BF), sds((width, 384), BF)],
        [idx, *x_parts, *w_parts, *early_parts, cos_all, sin_all], smem=1,
        scratch=[pltpu.VMEM((128, n_slots), BF)],
        flops=2 * n_slots * n_slots * 512 + 2 * n_slots * width * 384, name="attend",
        far_in=range(1, 3 + len(x_parts) + len(w_parts) + len(early_parts)),
        far_out=(0, 1, 2, 3, 4, 5))
    attn_unit, g_rows, shares = barrier((attn_unit, g_rows, shares))

    pieces = [hop(shares[d], d) for d in range(e_loc)]

    def exchange(x):
        flat = x.reshape(n_blk * (x.size // x.shape[-1] // n_blk), x.shape[-1])
        return lax.all_to_all(flat, blk, 0, 0, tiled=True)

    attn_recv = exchange(attn_unit).reshape(n_blk, slot_dev, 128)
    attn_recv, pieces[:-1] = barrier((attn_recv, pieces[:-1]))
    w_out_all = Columns(early_all, part, 0)
    mine, other, attn_low = call(
        out_kernel,
        [sds((tok, width), F32), sds((tok, width), BF), sds((n_seq * slot_dev, part), BF)],
        [idx, attn_recv, w_out_all], smem=1,
        scratch=[pltpu.VMEM((n_seq * slot_dev, width), F32)],
        flops=2 * n_seq * slot_dev * width * part, name="out", far_in=(2,), far_out=(2,))
    w_small_all = Columns(early_all, 128, part)
    send_x, residual, aux, small = call(
        route_kernel,
        [sds((heads * n_share, per_send, width + 128), BF), sds((tok, width), F32),
         sds((tok, 128), F32), sds((24, width), F32)],
        [flat_tokens, mine, across(other), w_small_all, prev_logits, ints, slot_rows],
        flops=tok * width * 1000, name="route", far_in=(3, 4, 5), far_out=(1, 2, 3))
    send_x, pieces = barrier((send_x, pieces))
    pieces = pieces + [partner(p) for p in pieces]
    x_rows = to_experts(send_x)
    x_rows, pieces = barrier((x_rows, pieces))
    group = max(1, 128 // unit)
    if group > 1:
        pieces = [join(pieces[i : i + group]) for i in range(0, len(pieces), group)]
    back_rows, *grad_pieces = experts(x_rows, g_rows, pieces)
    back_recv = to_experts(back_rows)

    if group > 1:
        grad_pieces = [part_of for full in grad_pieces for part_of in divide(full)]
    ours = list(grad_pieces[:e_loc])
    theirs = [partner(p) for p in grad_pieces[e_loc:]]
    recv = back_recv.reshape(heads * n_share, per_send, 2 * width)
    added = call(
        functools.partial(pair_add_kernel, e_loc), [sds(p.shape, BF) for p in ours], ours + theirs,
        name="pair_add", far_in=range(2 * e_loc), far_out=range(e_loc))

    came = [added[0], hop(added[1], 1)]
    half_way = hop(added[3], 2)
    recv, added, came, half_way = barrier((recv, added, came, half_way))
    output, grad_res, grad_low, sums = call(
        combine_kernel,
        [sds((tok, width), F32), sds((tok, width), F32), sds((tok, width), BF), sds((40, width), F32)],
        [recv, residual, cot, small, w_small_all, ints, aux, prev_wide], flops=tok * width * 2000,
        name="combine", far_in=(1, 2, 3, 4, 5, 6, 7), far_out=(0, 1))

    came = came + [hop(added[2], 2), hop(half_way, 1)]
    pay = (n_blk // 2, rows_here, part + 128)
    send_gv, grad_both = call(
        grad_vec_kernel,
        [sds((n_blk, slot_dev, 128), BF), sds((n_seq * slot_dev, width), BF)],
        [idx, grad_low, across(grad_low), w_out_all], smem=1,
        flops=2 * n_seq * slot_dev * width * part, name="grad_vec", far_in=(3,), far_out=(1,))
    dout = exchange(send_gv)
    keep, give = call(
        pay_kernel, [sds(pay, F32), sds(pay, BF)],
        [idx, grad_both, attn_low, sums, across(sums)], smem=1,
        scratch=[pltpu.VMEM((n_blk, rows_here, part + 128), F32)],
        flops=2 * n_seq * slot_dev * width * part, name="pay", far_in=(1, 2, 3), far_out=(0, 1))
    steps = [1 << (i - 1) for i in halving_bits(n_blk)[1:]]

    def halve(keep, came_sum, d):
        half = (keep.shape[0] // 2,) + keep.shape[1:]
        keep, give = call(
            halve_kernel, [sds(half, F32), sds(half, BF)], [keep, came_sum], name="halve")
        return keep, hop(give, d)

    came_sum = partner(give)
    dout, came, came_sum = barrier((dout, came, came_sum))

    keep, came_sum = halve(keep, came_sum, steps[0])
    (grad_unit,) = call(
        attend_back_kernel, [sds((n_slots, 384), BF)],
        [idx, qkv, dout, attn_unit, lse, cos_all, sin_all], smem=1,
        scratch=[pltpu.VMEM((128, n_slots), BF), pltpu.VMEM((n_slots, 128), F32),
                 pltpu.VMEM((n_slots, 128), F32)],
        flops=5 * n_slots * n_slots * 256, name="attend_back", far_in=(1, 3, 4, 5, 6), far_out=())
    grad_unit, came_sum = barrier((grad_unit, came_sum))
    rows8 = (8, slot_dev, width)
    gn_keep, gn_give = call(
        unit_back_kernel, [sds(rows8, F32), sds(rows8, BF)], [idx, grad_unit, w_pair], smem=1,
        scratch=[pltpu.VMEM((n_slots, width), F32)], flops=2 * n_slots * width * 384,
        name="unit_back", far_in=(2,), far_out=(0,))
    gn_came = partner(gn_give)
    (unit_dw,) = call(
        unit_dw_kernel, [sds((width, 384), BF)], [xn, grad_unit],
        flops=2 * n_slots * width * 384, name="unit_dw", far_in=(0,), room=20)
    gn_came, unit_dw, came_sum = barrier((gn_came, unit_dw, came_sum))
    gn_keep, gn_came = halve(gn_keep, gn_came, 2)
    keep, came_sum = halve(keep, came_sum, steps[1])
    dw_recv = exchange(unit_dw).reshape(n_blk, rows_here, 384)
    def by_source(parts):
        chosen = []
        for e in range(e_loc):
            value = parts[e_loc - 1]
            for d in range(e_loc - 1):
                value = jnp.where((q ^ d) == e, parts[d], value)
            chosen.append(value.astype(F32))
        return chosen

    if group == 1:
        in_sum, down_sum = call(
            functools.partial(place_kernel, e_loc),
            [sds((width * e_loc * 2, 128), F32), sds((unit, e_loc, width), F32)],
            [idx, *came], smem=1, name="place", far_in=range(1, e_loc + 1), far_out=(0, 1))
        in_sum = in_sum.reshape(width, e_loc, 2, unit)
    else:
        in_sum = jnp.stack(by_source([p[:width].reshape(width, 2, unit) for p in came]), axis=1)
        down_sum = by_source([p[width:].reshape(strips, unit, 2 * unit) for p in came])
        down_sum = jnp.transpose(jnp.stack(down_sum, axis=0), (2, 0, 1, 3))
        down_sum = down_sum.reshape(unit, e_loc, width)
    gn_came, in_sum, down_sum, came_sum = barrier((gn_came, in_sum, down_sum, came_sum))
    rows2 = (2, slot_dev, width)
    gn_parts = call(
        both_kernel, [sds(rows2, BF), sds(rows2, BF)], [gn_keep, gn_came], name="both")
    gn_parts = [
        lax.ppermute(a, both_axes, [(t, f) for f, t in to_head(same)])
        for a, same in zip(gn_parts, (True, False))]
    for d in steps[2:]:
        keep, came_sum = halve(keep, came_sum, d)
    gn_own, gn_away = call(
        heads_kernel, [sds((slot_dev, width), F32), sds((slot_dev, width), BF)], list(gn_parts),
        name="heads")
    gn_near = hop(gn_away, 1)
    gn_near, dw_recv = barrier((gn_near, dw_recv))
    qkv_sum, gain1_part = call(
        total_kernel, [sds((3, rows_here, part), F32), sds((8, rows_here), F32)],
        [dw_recv, w_phys, gain_row_in], name="total", far_in=(1, 2))
    gain1_sum = gain1_part[0] + across(gain1_part)[0]

    out_sum, gain2_sum, router_sum, const_sum, vec_sum, resid_sum = call(
        functools.partial(last_add_kernel, n_all),
        [sds((rows_here, part), F32), sds((1, rows_here), F32), sds((n_all, rows_here), F32),
         sds((4, rows_here), F32), sds((2, rows_here), F32), sds((n_all, n_all), F32)],
        [keep, came_sum], name="last_add")
    (grad_tokens,) = call(
        final_kernel, [sds((tok, width), F32)],
        [idx, flat_tokens, gn_own, gn_near, grad_res, small], smem=1,
        scratch=[pltpu.VMEM((tok, width), F32)], name="final", far_in=(1, 4, 5), far_out=(0,))
    return (
        output.reshape(tokens.shape),
        grad_tokens.reshape(tokens.shape),
        gain1_sum,
        jnp.transpose(qkv_sum, (1, 0, 2)),
        out_sum,
        gain2_sum.reshape(rows_here),
        jnp.transpose(router_sum),
        resid_sum,
        jnp.transpose(const_sum),
        jnp.transpose(vec_sum),
        in_sum,
        down_sum,
    )


def solution(mesh):
    heads, blocks = mesh.devices.shape
    split = Mesh(mesh.devices.reshape(heads, blocks // 2, 2), ("head", "ring", "core"))
    blk = ("ring", "core")
    in_specs = (
        P("head", blk, None),
        P("head", blk, None),
        P(),
        P("head", blk, None),
        P("head", blk, None),
        P(blk),
        P(blk, None, "head"),
        P(blk, "head"),
        P(blk),
        P(blk, None),
        P(),
        P(blk, None),
        P(blk, None),
        P(None, "head", None, blk),
        P(blk, "head", None),
        P("head", blk, None),
    )
    out_specs = (
        P("head", blk, None),
        P("head", blk, None),
        P(blk),
        P(blk, None, "head"),
        P(blk, "head"),
        P(blk),
        P(blk, None),
        P(),
        P(blk, None),
        P(blk, None),
        P(None, "head", None, blk),
        P(blk, "head", None),
    )
    return jax.shard_map(
        per_device, mesh=split, in_specs=in_specs, out_specs=out_specs, check_vma=False
    )
```

```python
import functools
import math

import jax
import jax.numpy as jnp
import numpy as np
from jax import lax
from jax.experimental import pallas as pl
from jax.experimental.pallas import tpu as pltpu
from jax.sharding import Mesh
from jax.sharding import PartitionSpec as P

HD = 64
NEXP = 8
EPS = 1e-05
NEG = -1e30
BF = jnp.bfloat16
F32 = jnp.float32
MIB = 1 << 20
ANY2 = (((1,), (1,)), ((), ()))
MM = (((1,), (0,)), ((), ()))
C_CONST, C_VEC, C_GAIN1, C_GAIN2 = 12, 16, 18, 19
RESID = 32
S_HEAD, S_LEN, S_BASE, S_EXPERT, S_BLOCK, S_BIT, S_TABLE = 0, 1, 2, 3, 4, 5, 8


def dot(a, b, dims=MM):
    return lax.dot_general(a, b, dims, preferred_element_type=F32)


def whole_block(shape):
    return pl.BlockSpec(shape, lambda i: (0,) * len(shape), pipeline_mode=pl.Buffered(1))


def far(x):
    return pltpu.with_memory_space_constraint(x, pltpu.HBM)


class Columns:
    def __init__(self, array, count, at):
        self.array, self.at, self.window = array, (0, at // count), (array.shape[0], count)
        self.shape, self.dtype = self.window, array.dtype


def call(kernel, outs, args, smem=0, scratch=(), room=12, flops=0, name=None,
         far_in=(), far_out=()):
    sm = pl.BlockSpec(memory_space=pltpu.SMEM)
    total = sum(math.prod(a.shape) * a.dtype.itemsize for a in list(args) + list(outs))
    limit = total + sum(math.prod(a.shape) * a.dtype.itemsize for a in scratch) + room * MIB
    specs = [
        pl.BlockSpec(a.window, functools.partial(lambda at, i: at, a.at), pipeline_mode=pl.Buffered(1))
        if isinstance(a, Columns) else whole_block(a.shape) for a in args[smem:]]
    args = [a.array if isinstance(a, Columns) else a for a in args]
    args = [far(a) if i in far_in else a for i, a in enumerate(args)]
    shapes = tuple(pltpu.HBM(o.shape, o.dtype) if i in far_out else o for i, o in enumerate(outs))
    return pl.pallas_call(
        kernel,
        grid=(1,),
        out_shape=shapes,
        in_specs=[sm] * smem + specs,
        out_specs=tuple(whole_block(o.shape) for o in outs),
        scratch_shapes=list(scratch),
        compiler_params=pltpu.CompilerParams(vmem_limit_bytes=min(limit, 60 * MIB)),
        cost_estimate=pl.CostEstimate(flops=flops, bytes_accessed=total, transcendentals=0),
        name=name,
    )(*args)


def sds(shape, dtype):
    return jax.ShapeDtypeStruct(shape, dtype)


def unit_at(seq, pair):
    ring = (seq >> 1) * 4 + (pair >> 1) * 2 + (seq & 1)
    return ring * 2 + (pair & 1)


def idle_units(n_blk, n_seq, pairs):
    busy = {unit_at(q, p) for q in range(n_seq) for p in range(pairs)}
    return [u for u in range(n_blk) if u not in busy]


def halving_bits(n):
    return [0, 1, 3, 2] + list(range(4, n.bit_length() - 1))


def halving_order(n):
    bits = halving_bits(n)
    last = len(bits) - 1
    return [sum(((k >> (last - i)) & 1) << b for i, b in enumerate(bits)) for k in range(n)]


def gather_rows(dst, arrays, idx, base, rows):
    j = base
    for a in arrays:
        for i in range(a.shape[0] // rows):
            at = idx[j] * rows
            if rows % 16 == 0:
                at = pl.multiple_of(at, 16)
            dst[pl.ds(at, rows), :] = a[i * rows : (i + 1) * rows, :]
            j += 1


def lower_lanes(shape):
    return (lax.broadcasted_iota(jnp.int32, shape, 1) & 63) < 32


def turned(values):
    return jnp.where(
        lower_lanes(values.shape), -pltpu.roll(values, 96, 1), pltpu.roll(values, 32, 1)
    )


def head_mask(shape, which):
    lane = lax.broadcasted_iota(jnp.int32, shape, 1)
    return (lane >= 64) if which else (lane < 64)


def only(values, which):
    return jnp.where(head_mask(values.shape, which), values, jnp.zeros_like(values))


def scores_of(k_rows, q_head, first_query, limit_len):
    s = dot(k_rows, q_head, ANY2)
    key = lax.broadcasted_iota(jnp.int32, s.shape, 0)
    query = lax.broadcasted_iota(jnp.int32, (1, s.shape[1]), 1) + first_query
    last = jnp.minimum(query, limit_len - 1)
    return jnp.where(key <= last, s, NEG)


def each_block(total, block, fn):
    if total // block <= 4:
        for i in range(total // block):
            fn(i * block, (i + 1) * block)
    else:

        @pl.loop(0, total // block)
        def _(i):
            fn(pl.multiple_of(i * block, block), total)


def attend_kernel(n_x, n_w, n_p, w_rows, p_rows, idx, *refs):
    xs, ws, ps = refs[:n_x], refs[n_x : n_x + n_w], refs[n_x + n_w : n_x + n_w + n_p]
    cos, sin, out, lse, xn, qkv, early, wg, vt = refs[n_x + n_w + n_p :]
    total = qkv.shape[0]
    block = 256
    slots = 64
    limit_len = idx[S_LEN]
    j = S_TABLE + sum(a.shape[0] // slots for a in xs)
    gather_rows(wg, ws, idx, j, w_rows)
    gather_rows(early, ps, idx, j + sum(a.shape[0] // w_rows for a in ws), p_rows)
    columns = early[:, early.shape[1] - 128 :].astype(F32)
    gain = jnp.transpose(columns)[C_GAIN1 : C_GAIN1 + 1]
    j = S_TABLE
    for a in xs:
        for i in range(a.shape[0] // slots):
            x = a[i * slots : (i + 1) * slots, :].astype(F32)
            rstd = lax.rsqrt(jnp.mean(x * x, axis=-1, keepdims=True) + EPS)
            at = pl.ds(pl.multiple_of(idx[j] * slots, slots), slots)
            xn[at, :] = (x * rstd * gain).astype(BF)
            j += 1

    def project(start, _):
        at = pl.ds(start, block)
        y = dot(xn[at, :], wg[...])
        c, s = cos[at, :], sin[at, :]
        q, k = y[:, 0:128], y[:, 128:256]
        q = (q * c + turned(q) * s) * (1.0 / math.sqrt(HD))
        qkv[at, 0:128] = q.astype(BF)
        qkv[at, 128:256] = (k * c + turned(k) * s).astype(BF)
        qkv[at, 256:384] = y[:, 256:384].astype(BF)

    each_block(total, block, project)
    vt[...] = jnp.transpose(qkv[:, 256:384])

    def step(start, n_keys):
        q = qkv[pl.ds(start, block), 0:128]
        parts = []
        for h in range(2):
            s = scores_of(qkv[0:n_keys, 128:256], only(q, h), start, limit_len)
            m = jnp.max(s, axis=0, keepdims=True)
            p = jnp.exp(s - m)
            total_p = jnp.sum(p, axis=0, keepdims=True)
            o = dot(vt[h * 64 : (h + 1) * 64, 0:n_keys], p.astype(BF))
            parts.append(o / total_p)
            lse[h : h + 1, pl.ds(start, block)] = m + jnp.log(total_p)
        out[pl.ds(start, block), :] = jnp.transpose(jnp.concatenate(parts, axis=0)).astype(BF)

    each_block(total, block, step)


def unit_dw_kernel(idx, xn, grad, keep, give, full):
    dw = dot(jnp.transpose(xn[...]), grad[...])
    owned = full.shape[1]
    for i in range(full.shape[0]):
        full[i] = dw[i * owned : (i + 1) * owned]
    for n, offset in enumerate(a + b + c for a in (0, 8) for b in (0, 4) for c in (0, 1)):
        keep[n] = full[idx[S_BLOCK] ^ offset]
        give[n] = full[idx[S_BLOCK] ^ (offset + 2)].astype(BF)


def attend_back_kernel(idx, qkv, dout, out, lse, cos, sin, grad, kt, dk, dv):
    total = qkv.shape[0]
    block = 256
    limit_len = idx[S_LEN]
    kt[...] = jnp.transpose(qkv[:, 128:256])
    dk[...] = jnp.zeros_like(dk)
    dv[...] = jnp.zeros_like(dv)

    def unrotate(values, at, size):
        c, s = cos[pl.ds(at, size), :], sin[pl.ds(at, size), :]
        return values * c - turned(values) * s

    def step(start, n_keys):
        q = qkv[pl.ds(start, block), 0:128]
        do = dout[pl.ds(start, block), :]
        prod_t = jnp.transpose(do.astype(F32) * out[pl.ds(start, block), :].astype(F32))
        probs, ds, dq = [], [], []
        for h in range(2):
            q_head, do_head = only(q, h), only(do, h)
            s = scores_of(qkv[0:n_keys, 128:256], q_head, start, limit_len)
            p = jnp.exp(s - lse[h : h + 1, pl.ds(start, block)])
            delta = jnp.sum(prod_t[h * 64 : (h + 1) * 64], axis=0, keepdims=True)
            dp = dot(qkv[0:n_keys, 256:384], do_head, ANY2)
            d = (p * (dp - delta)).astype(BF)
            probs.append(p.astype(BF))
            ds.append(d)
            dq.append(dot(kt[h * 64 : (h + 1) * 64, 0:n_keys], d))
        both_q = jnp.concatenate([only(q, 0), only(q, 1)], axis=0)
        both_do = jnp.concatenate([only(do, 0), only(do, 1)], axis=0)
        dv[0:n_keys, :] += dot(jnp.concatenate(probs, axis=1), both_do)
        dk[0:n_keys, :] += dot(jnp.concatenate(ds, axis=1), both_q)
        gq = jnp.transpose(jnp.concatenate(dq, axis=0)) * (1.0 / math.sqrt(HD))
        grad[pl.ds(start, block), 0:128] = unrotate(gq, start, block).astype(BF)

    each_block(total, block, step)

    def finish(start, _):
        at = pl.ds(start, block)
        grad[at, 128:256] = unrotate(dk[at, :], start, block).astype(BF)
        grad[at, 256:384] = dv[at, :].astype(BF)

    each_block(total, block, finish)


def out_kernel(idx, recv, wos, mine, other, attn, full):
    h = idx[S_HEAD]
    part = attn.shape[1]
    slots = recv.shape[1]
    n_seq = attn.shape[0] // slots
    for p in range(part // 128):
        for q in range(n_seq):
            attn[q * slots : (q + 1) * slots, p * 128 : (p + 1) * 128] = recv[unit_at(q, p)]
    full[...] = dot(attn[...], wos[...], ANY2)
    rows = mine.shape[0]
    mine[...] = full[pl.ds(h * rows, rows), :]
    other[...] = full[pl.ds((1 - h) * rows, rows), :].astype(BF)


def onehot_rows(slots, n_rows):
    at = lax.broadcasted_iota(jnp.int32, (n_rows, slots.shape[1]), 0)
    return jnp.where((at == slots[0:1]) | (at == slots[1:2]), 1.0, 0.0).astype(BF)


def spread(rows, send):
    per = send.shape[1]
    copies = send.shape[0] * per // rows.shape[0]
    for i in range(send.shape[0]):
        at = (i // copies) * per
        send[i] = rows[at : at + per]


def send_grad_kernel(slots, cot, ints, send):
    g = (cot[...] * ints[:, 4:5].astype(F32)).astype(BF)
    n_rows = send.shape[1] * 2
    spread(dot(onehot_rows(slots[...], n_rows), g).astype(BF), send)


def norm_two(residual, gain):
    rstd = lax.rsqrt(jnp.mean(residual * residual, axis=-1, keepdims=True) + EPS)
    xhat = residual * rstd
    return rstd, xhat, xhat * gain


def route_kernel(tokens, mine, other, wpack, prev_logits, ints, slots, send, residual, aux, small):
    res = tokens[...].astype(F32) + mine[...] + other[...].astype(F32)
    residual[...] = res
    small[...] = jnp.transpose(wpack[...].astype(F32))[: small.shape[0]]
    _, _, normed = norm_two(res, small[C_GAIN2 : C_GAIN2 + 1])
    low = normed.astype(BF)
    logits = dot(low, wpack[...]) + prev_logits[...]
    lane = lax.broadcasted_iota(jnp.int32, logits.shape, 1)

    def pick(which):
        return jnp.sum(jnp.where(lane == which, logits, 0.0), axis=1, keepdims=True)

    def pair_softmax(a, b):
        top = jnp.maximum(a, b)
        ea, eb = jnp.exp(a - top), jnp.exp(b - top)
        return ea / (ea + eb), eb / (ea + eb)

    p0, p1 = pair_softmax(pick(ints[:, 0:1]), pick(ints[:, 1:2]))
    a00, a01 = pair_softmax(pick(C_CONST), pick(C_CONST + 1))
    a10, a11 = pair_softmax(pick(C_CONST + 2), pick(C_CONST + 3))
    info = jnp.zeros_like(logits)
    for i, v in enumerate((p0, p1, a00, a01, a10, a11)):
        info = jnp.where(lane == i, v, info)
    aux[...] = info
    n_rows = send.shape[1] * 2
    tok = slots.shape[1]
    at = lax.broadcasted_iota(jnp.int32, (n_rows, tok), 0)
    first = jnp.where(at == slots[0:1], 1.0, 0.0).astype(BF)
    second = jnp.where(at == slots[1:2], 1.0, 0.0).astype(BF)

    def split(v, base):
        high = v.astype(BF).astype(F32)
        return jnp.where(lane == 0, high, jnp.where(lane == 1, v - high, base))

    extra = dot(first, split(p0, 0.0).astype(BF)) + dot(second, split(p1, 0.0).astype(BF))
    rows = jnp.concatenate([dot(first + second, low), extra], axis=1)
    spread(rows.astype(BF), send)


def expert_kernel(n_pieces, n_steps, x_ref, g_ref, *refs):
    w, back, grads = refs[:n_pieces], refs[n_pieces], refs[n_pieces + 1 : 2 * n_pieces + 1]
    wd_all = refs[2 * n_pieces + 1]
    acc = refs[2 * n_pieces + 2] if n_steps > 1 else None
    step = pl.program_id(0)
    width = g_ref.shape[1]
    two = w[0].shape[1]
    unit = two // 2
    strips = width // two

    @pl.when(step == 0)
    def _():
        for d in range(n_pieces):
            for j in range(strips):
                at = width + j * unit
                wd_all[d * unit : (d + 1) * unit, j * two : (j + 1) * two] = w[d][at : at + unit, :]

    x = x_ref[:, :width]
    g = g_ref[...]
    prob = jnp.sum(x_ref[:, width:].astype(F32), axis=1, keepdims=True)
    xt = jnp.transpose(x)
    g_scaled = (g.astype(F32) * prob).astype(BF)
    up_grad = dot(g, wd_all[...], ANY2) * prob
    hiddens = []
    grad_in = jnp.zeros((x.shape[0], width), F32)

    def keep(d, start, value):
        at = slice(start, start + value.shape[0])
        if n_steps == 1:
            grads[d][at, :] = value.astype(BF)
            return

        @pl.when(step == 0)
        def _():
            acc[d, at, :] = value

        @pl.when(step > 0)
        def _():
            acc[d, at, :] += value

        @pl.when(step == n_steps - 1)
        def _():
            grads[d][at, :] = acc[d, at, :].astype(BF)

    for d in range(n_pieces):
        both = dot(x, w[d][:width, :])
        gate, up = both[:, :unit], both[:, unit:]
        sig = 1.0 / (1.0 + jnp.exp(-gate))
        act = gate * sig
        hidden = (act * up).astype(BF)
        hiddens.append(hidden)
        gh = up_grad[:, d * unit : (d + 1) * unit]
        g_gate = gh * up * sig * (1.0 + gate * (1.0 - sig))
        g_both = jnp.concatenate([g_gate, gh * act], axis=1).astype(BF)
        grad_in += dot(g_both, w[d][:width, :], ANY2)
        keep(d, 0, dot(xt, g_both))
        gd = dot(jnp.transpose(hidden), g_scaled)
        for j in range(strips):
            keep(d, width + j * unit, gd[:, j * two : (j + 1) * two])
    back[:, :width] = dot(jnp.concatenate(hiddens, axis=1), wd_all[...]).astype(BF)
    back[:, width:] = grad_in.astype(BF)


def experts(x_rows, g_rows, pieces):
    n = len(pieces)
    rows, wide = x_rows.shape
    width = g_rows.shape[1]
    deep, two = pieces[0].shape
    unit = two // 2
    block = 384 if rows % 384 == 0 else rows
    steps = rows // block
    outs = [sds((rows, 2 * width), BF)] + [sds((deep, two), BF)] * n
    scratch = [pltpu.VMEM((n * unit, width), BF)]
    if steps > 1:
        scratch.append(pltpu.VMEM((n, deep, two), F32))
    return pl.pallas_call(
        functools.partial(expert_kernel, n, steps),
        grid=(steps,),
        in_specs=[
            pl.BlockSpec((block, wide), lambda i: (i, 0)),
            pl.BlockSpec((block, width), lambda i: (i, 0)),
        ]
        + [whole_block(a.shape) for a in pieces],
        out_specs=tuple(
            [pl.BlockSpec((block, 2 * width), lambda i: (i, 0))]
            + [whole_block(o.shape) for o in outs[1:]]
        ),
        out_shape=tuple(outs[:1] + [pltpu.HBM(o.shape, o.dtype) for o in outs[1:]]),
        scratch_shapes=scratch,
        compiler_params=pltpu.CompilerParams(vmem_limit_bytes=(30 if steps == 1 else 48) * MIB),
        cost_estimate=pl.CostEstimate(
            flops=18 * rows * width * unit * n,
            bytes_accessed=8 * rows * width + 12 * width * unit * n,
            transcendentals=0,
        ),
        name="experts",
    )(x_rows, far(g_rows), *[far(p) for p in pieces])


def combine_kernel(recv, residual, cot, small, wpack, ints, aux, prev, out, grad_res, grad_low, sums):
    res = residual[...]
    gain = small[C_GAIN2 : C_GAIN2 + 1]
    rstd, xhat, normed = norm_two(res, gain)
    low = normed.astype(BF)
    width = res.shape[1]
    heads = 2
    copies = recv.shape[0] // heads
    groups = []
    for h in range(heads):
        total = recv[h * copies].astype(F32)
        for r in range(1, copies):
            total = total + recv[h * copies + r].astype(F32)
        groups.append(total.astype(BF))
    rows = jnp.concatenate(groups, axis=0)
    valid = ints[:, 4:5].astype(F32)
    go = cot[...] * valid
    lane = lax.broadcasted_iota(jnp.int32, (res.shape[0], rows.shape[0]), 1)
    first = jnp.where(lane == ints[:, 2:3], 1.0, 0.0).astype(BF)
    second = jnp.where(lane == ints[:, 3:4], 1.0, 0.0).astype(BF)
    eo0 = dot(first, rows[:, :width])
    eo1 = dot(second, rows[:, :width])
    gin = dot(first + second, rows[:, width:])
    info = aux[...]
    p0, p1 = info[:, 0:1], info[:, 1:2]
    alpha = ((info[:, 2:3], info[:, 3:4]), (info[:, 4:5], info[:, 5:6]))
    r0, r1 = ints[:, 0:1], ints[:, 1:2]

    def at(route, which):
        return jnp.where(route == which, 1.0, 0.0)

    vec = (small[C_VEC : C_VEC + 1], small[C_VEC + 1 : C_VEC + 2])
    share0 = at(r0, NEXP + 1) + at(r0, NEXP + 2) * alpha[0][0] + at(r0, NEXP + 3) * alpha[1][0]
    share1 = at(r1, NEXP + 1) + at(r1, NEXP + 2) * alpha[0][0] + at(r1, NEXP + 3) * alpha[1][0]
    weight = [p0 * at(r0, NEXP + 2 + j) + p1 * at(r1, NEXP + 2 + j) for j in range(2)]
    mixed = (
        p0 * eo0
        + p1 * eo1
        + (p0 * share0 + p1 * share1) * normed
        + (weight[0] * alpha[0][1]) * vec[0]
        + (weight[1] * alpha[1][1]) * vec[1]
    )
    out[...] = valid * (res + mixed)

    def rowsum(v):
        return jnp.sum(v, axis=1, keepdims=True)

    s_norm = rowsum(go * normed)
    s_vec = [rowsum(go * vec[j]) for j in range(2)]
    gg0 = rowsum(go * eo0) + share0 * s_norm
    gg1 = rowsum(go * eo1) + share1 * s_norm
    for j in range(2):
        gg0 = gg0 + at(r0, NEXP + 2 + j) * alpha[j][1] * s_vec[j]
        gg1 = gg1 + at(r1, NEXP + 2 + j) * alpha[j][1] * s_vec[j]
    gsum = p0 * gg0 + p1 * gg1
    c0, c1 = p0 * (gg0 - gsum), p1 * (gg1 - gsum)
    wide = lax.broadcasted_iota(jnp.int32, (res.shape[0], 128), 1)
    dl = jnp.where(wide == r0, c0, 0.0) + jnp.where(wide == r1, c1, 0.0)
    coef = p0 * at(r0, NEXP + 1) + p1 * at(r1, NEXP + 1)
    vec_rows = []
    for j in range(2):
        ga0, ga1 = weight[j] * s_norm, weight[j] * s_vec[j]
        mean = alpha[j][0] * ga0 + alpha[j][1] * ga1
        dl = jnp.where(wide == C_CONST + 2 * j, alpha[j][0] * (ga0 - mean), dl)
        dl = jnp.where(wide == C_CONST + 2 * j + 1, alpha[j][1] * (ga1 - mean), dl)
        coef = coef + alpha[j][0] * weight[j]
        vec_rows.append(jnp.sum((alpha[j][1] * weight[j]) * go, axis=0, keepdims=True))
    dl = dl.astype(BF)
    dlt = jnp.transpose(dl)
    proj = dot(dlt, low)
    resid = lax.dot_general(
        jnp.transpose(prev[...]), jnp.where(wide < C_CONST, dl.astype(F32), 0.0), MM,
        precision=lax.Precision.HIGHEST, preferred_element_type=F32,
    )
    gn = gin + coef * go + dot(dl, wpack[...], ANY2)
    gain_row = jnp.sum(gn * xhat, axis=0, keepdims=True)
    row = lax.broadcasted_iota(jnp.int32, (24, 1), 0)
    table = jnp.where(row < C_VEC, proj[:24], 0.0)
    table = jnp.where(row == C_VEC, vec_rows[0], table)
    table = jnp.where(row == C_VEC + 1, vec_rows[1], table)
    sums[:24, :] = jnp.where(row == C_GAIN2, gain_row, table)
    sums[24:, :128] = resid[: sums.shape[0] - 24]
    sums[24:, 128:] = jnp.zeros((sums.shape[0] - 24, sums.shape[1] - 128), F32)
    ghat = gn * gain
    grad = go + rstd * (ghat - xhat * jnp.mean(ghat * xhat, axis=-1, keepdims=True))
    grad_res[...] = grad
    grad_low[...] = grad.astype(BF)


def grad_vec_kernel(idx, mine, other, wos, send, both):
    h = idx[S_HEAD]
    rows = mine.shape[0]
    both[pl.ds(h * rows, rows), :] = mine[...]
    both[pl.ds((1 - h) * rows, rows), :] = other[...]
    part = wos.shape[1]
    g = both[...]
    gv = dot(g, wos[...]).astype(BF)
    slots = send.shape[1]
    n_seq = g.shape[0] // slots
    for p in range(part // 128):
        for q in range(n_seq):
            send[unit_at(q, p)] = gv[q * slots : (q + 1) * slots, p * 128 : (p + 1) * 128]
    for u in idle_units(send.shape[0], n_seq, part // 128):
        send[u] = jnp.zeros(send.shape[1:], BF)


def pay_kernel(idx, both, attn, sums, more_sums, keep, give, pay):
    part = attn.shape[1]
    dw = dot(jnp.transpose(both[...]), attn[...])
    total = sums[...] + more_sums[...]
    table = jnp.concatenate([total[:24], jnp.zeros((104, total.shape[1]), F32)], axis=0)
    columns = jnp.transpose(table)
    n, owned, _ = pay.shape
    resid = jnp.concatenate([total[24:, :128], jnp.zeros((88 + 24, 128), F32)], axis=0)
    block = pltpu.roll(resid[:owned, :], RESID, 1)
    for i in range(n):
        at = i * owned
        pay[i, :, :part] = dw[at : at + owned]
        pay[i, :, part:] = columns[at : at + owned] + block
    for k, offset in enumerate(halving_order(n)):
        value = pay[idx[S_BLOCK] ^ offset]
        if k < n // 2:
            keep[k] = value
        else:
            give[k - n // 2] = value.astype(BF)


def halve_kernel(mine, came, keep, give):
    half = keep.shape[0]
    keep[...] = mine[:half] + came[:half].astype(F32)
    give[...] = (mine[half:] + came[half:].astype(F32)).astype(BF)


def last_add_kernel(n_all, mine, came, dw, gain2, router, const, vec, resid):
    total = mine[0] + came[0].astype(F32)
    dw[...] = total[:, : dw.shape[1]]
    table = total[:, dw.shape[1] :]
    rows = jnp.transpose(table)
    router[...] = rows[:n_all]
    const[...] = rows[C_CONST:C_VEC]
    vec[...] = rows[C_VEC : C_VEC + 2]
    gain2[...] = rows[C_GAIN2 : C_GAIN2 + 1]
    resid[...] = table[:n_all, RESID : RESID + n_all]


def unit_back_kernel(idx, grad, w_pair, keep, give, full):
    slots = keep.shape[1]
    block = 256

    def step(start, _):
        at = pl.ds(start, block)
        full[at, :] = dot(grad[at, :], w_pair[...], ANY2)

    each_block(full.shape[0], block, step)
    for k in range(2):
        for n, (far, third, first) in enumerate((a, b, c) for a in (0, 4) for b in (0, 8) for c in (0, 2)):
            which = idx[S_BASE] ^ (k + far + third + first)
            rows = full[pl.ds(pl.multiple_of(which * slots, slots), slots), :]
            if k == 0:
                keep[n] = rows
            else:
                give[n] = rows.astype(BF)


def both_kernel(mine, came, first, second):
    total = mine[...] + came[...].astype(F32)
    half = first.shape[0]
    first[...] = total[:half].astype(BF)
    second[...] = total[half:].astype(BF)


def heads_kernel(a, b, own, away):
    total = a[...].astype(F32) + b[...].astype(F32)
    own[...] = total[0]
    away[...] = total[1].astype(BF)


def total_kernel(idx, stay, far_pair, core_pairs, w, gain, dw, gain_row, pieces):
    part = dw.shape[2]
    owned = dw.shape[1]
    column = jnp.transpose(jnp.broadcast_to(gain[...].astype(F32), (8, owned)))[:, 0:1]
    rowsum = jnp.zeros((owned, 1), F32)
    pieces[0], pieces[2] = stay[0].astype(F32), far_pair[0].astype(F32)
    pieces[1], pieces[3] = core_pairs[0].astype(F32), core_pairs[1].astype(F32)
    this_pair = 2 * idx[S_BIT] + (idx[S_BLOCK] & 1)
    for p in range(part // 128):
        total = pieces[this_pair ^ p]
        for k in range(3):
            piece = total[:, k * 128 : (k + 1) * 128]
            at = slice(p * 128, (p + 1) * 128)
            rowsum = rowsum + jnp.sum(piece * w[k, :, at].astype(F32), axis=1, keepdims=True)
            dw[k, :, at] = piece
    rowsum = rowsum / column
    gain_row[...] = jnp.transpose(jnp.broadcast_to(rowsum, (owned, 128)))[: gain_row.shape[0]]


def pair_add_kernel(n, *refs):
    for i in range(n):
        refs[2 * n + i][...] = (refs[i][...].astype(F32) + refs[n + i][...].astype(F32)).astype(BF)


def place_kernel(e_loc, idx, *refs):
    came, gin, gdown = refs[:e_loc], refs[e_loc], refs[e_loc + 1]
    width = gin.shape[0] // (2 * e_loc)
    strips = width // 256
    for q in range(e_loc):

        @pl.when(idx[S_EXPERT] == q)
        def _():
            for d in range(e_loc):
                e = q ^ d
                for i in range(2):
                    lanes = slice(i * 128, (i + 1) * 128)
                    rows = came[d][0:width, lanes].astype(F32)
                    gin[pl.ds(2 * e + i, width, stride=2 * e_loc), :] = rows
                    for j in range(strips):
                        at = width + j * 128
                        rows = came[d][at : at + 128, lanes].astype(F32)
                        at = (2 * j + i) * 128
                        gdown[:, e, at : at + 128] = rows


def pack_kernel(idx, w_qkv, w_out, router, const, vec, gain1, gain2, keep, swap, give, early, pairs):
    part = w_out.shape[1]
    owned = w_out.shape[0]
    rows = [r[...].astype(F32) for r in (router, const, vec, gain1, gain2)]
    rows.append(jnp.zeros((128 - 20, owned), F32))
    columns = jnp.transpose(jnp.concatenate(rows, axis=0))
    early[:, :part] = w_out[...]
    early[:, part:] = columns.astype(BF)
    for k in range(3):
        for p in range(4):
            if p < part // 128:
                pairs[p, :, k * 128 : (k + 1) * 128] = w_qkv[k, :, p * 128 : (p + 1) * 128]
            else:
                pairs[p, :, k * 128 : (k + 1) * 128] = jnp.zeros((owned, 128), BF)
    near, away = 2 * idx[0], 2 * (1 - idx[0])
    core = idx[1]
    keep[...] = pairs[near + core]
    swap[...] = pairs[away + core]
    give[:owned, :] = pairs[near + 1 - core]
    give[owned:, :] = pairs[away + 1 - core]


def final_kernel(idx, tokens, own, came, grad_res, small, grad, gn_rows):
    slots = own.shape[0]
    first = idx[S_BIT + 1]
    gn_rows[pl.ds(pl.multiple_of(first * slots, slots), slots), :] = own[...]
    gn_rows[pl.ds(pl.multiple_of((1 - first) * slots, slots), slots), :] = came[...].astype(F32)
    x = tokens[...].astype(F32)
    rstd = lax.rsqrt(jnp.mean(x * x, axis=-1, keepdims=True) + EPS)
    xhat = x * rstd
    ghat = gn_rows[...] * small[C_GAIN1 : C_GAIN1 + 1]
    grad[...] = grad_res[...] + rstd * (
        ghat - xhat * jnp.mean(ghat * xhat, axis=-1, keepdims=True)
    )


def per_device(
    tokens, previous_layer_logits, lengths, routes, pair_order, gain_attn, w_qkv, w_out, gain_ffn,
    w_router, w_residual, w_const, const_vec, w_in, w_down, cotangent,
):
    seq_dev, slot_dev, width = tokens.shape
    n_all = previous_layer_logits.shape[2]
    tok = seq_dev * slot_dev
    heads = lax.axis_size("head")
    ring = lax.axis_size("ring")
    n_blk = 2 * ring
    n_seq = seq_dev * heads
    n_slots = slot_dev * n_blk
    e_loc = w_in.shape[1]
    n_share = ring // e_loc
    unit = w_in.shape[3]
    rows_here = gain_attn.shape[0]
    part = w_qkv.shape[2]
    capacity = 9 * 2 * tok // (8 * n_all)
    h = lax.axis_index("head")
    ring_at = lax.axis_index("ring")
    core = lax.axis_index("core")
    b = ring_at * 2 + core
    q = ring_at % e_loc
    swap = [(0, 1), (1, 0)]
    blk = ("ring", "core")
    barrier = lax.optimization_barrier

    def across(x):
        return lax.ppermute(x, "head", swap)

    def partner(x):
        return lax.ppermute(x, "core", swap)

    def join(parts):
        total = unit * len(parts)
        cube = jnp.concatenate([p[:width].reshape(width, 2, unit) for p in parts], axis=2)
        down = [p[width:].reshape(strips, unit, 2 * unit) for p in parts]
        down = [jnp.transpose(p, (1, 0, 2)).reshape(unit, -1, 2 * total) for p in down]
        down = jnp.transpose(jnp.concatenate(down, axis=0), (1, 0, 2))
        return jnp.concatenate(
            [cube.reshape(width, 2 * total), down.reshape(-1, 2 * total)], axis=0)

    def divide(full):
        total = full.shape[1] // 2
        cube = full[:width].reshape(width, 2, total // unit, unit)
        down = jnp.transpose(full[width:].reshape(-1, total, 2 * total), (1, 0, 2))
        down = down.reshape(total // unit, unit, strips, 2 * unit)
        return [
            jnp.concatenate(
                [cube[:, :, d].reshape(width, 2 * unit),
                 jnp.transpose(down[d], (1, 0, 2)).reshape(-1, 2 * unit)], axis=0)
            for d in range(total // unit)]

    def hop(x, d):
        return lax.ppermute(x, "ring", [(i, i ^ d) for i in range(ring)]) if d else x

    bit = [(ring_at >> i) & 1 for i in range(3)]
    more = [1 << i for i in range(3, ring.bit_length() - 1)]
    both_axes = ("head", "ring")

    def to_head(same):
        pairs = []
        for i in range(heads):
            for r in range(ring):
                third = (r >> 2) & 1
                target = third if same else 1 - third
                pairs.append((i * ring + r, target * ring + ((r & ~4) | (i << 2))))
        return pairs

    def xor_blocks(ring_base, offsets):
        ring_off = np.array([d for d, _ in offsets], np.int32)
        core_off = np.array([k for _, k in offsets], np.int32)
        return (ring_base ^ ring_off) * 2 + (core ^ core_off)

    seq_base = (ring_at & ~4) | (h << 2)
    x_off = [(0, 0), (1, 0), (4, 0), (5, 0)]
    for d in more:
        x_off = x_off + [(r ^ d, k) for r, k in x_off]
    x_off = x_off + [(r ^ 2, k) for r, k in x_off]
    x_off = x_off + [(r, 1) for r, _ in x_off]
    w_off = [(0, 0), (0, 1), (2, 0), (2, 1)]
    w_off = w_off + [(r ^ 4, k) for r, k in w_off]
    w_off = w_off + [(r ^ 1, k) for r, k in w_off]
    p_off = [(0, 0)]
    for d in (4, 2, 1):
        p_off = p_off + [(r ^ d, 0) for r, _ in p_off]
    p_off = p_off + [(r, 1) for r, _ in p_off]
    direct = ring == 8
    flat_tokens = tokens.reshape(tok, width)
    near_rows = lax.dynamic_index_in_dim(tokens, bit[0], 0, keepdims=False)
    away_rows = lax.dynamic_index_in_dim(tokens, 1 - bit[0], 0, keepdims=False)
    w_phys = jnp.transpose(w_qkv, (1, 0, 2))
    gain_row_in = gain_attn[None, :]
    keep_w, swap_w, give_w, early = call(
        pack_kernel,
        [sds((rows_here, part), BF), sds((rows_here, part), BF), sds((2 * rows_here, part), BF),
         sds((rows_here, part + 128), BF)],
        [jnp.stack([bit[1], core]), w_phys, w_out, jnp.transpose(w_router), jnp.transpose(w_const),
         jnp.transpose(const_vec), gain_row_in, gain_ffn[None, :]], smem=1,
        scratch=[pltpu.VMEM((4, rows_here, part), BF)], name="pack", far_in=range(1, 8))

    def spread_to(x, d):
        return jnp.concatenate([x, hop(x, d)], axis=0)

    def gathered(x):
        return [lax.all_gather(x, blk, axis=0, tiled=True)]

    p_rows = rows_here if direct else width
    w_rows = rows_here if direct else width
    two_blocks = jnp.concatenate([near_rows, hop(away_rows, 1)], axis=0)
    if direct:
        came_w = partner(give_w)
        early = spread_to(early, 4)
        (two_blocks, routes, pair_order, cotangent, lengths, previous_layer_logits, w_in,
         w_down) = barrier((two_blocks, routes, pair_order, cotangent, lengths,
                            previous_layer_logits, w_in, w_down))
        swapped = [hop(swap_w, 2), hop(came_w[rows_here:], 2)]
    if direct:
        early = spread_to(early, 2)
    x_parts = [lax.ppermute(two_blocks, both_axes, to_head(same)) for same in (True, False)]

    seq = 2 * bit[2] + bit[0]
    seq_len = lax.dynamic_index_in_dim(lengths, seq, 0, keepdims=False)
    base = seq_base * 2 + core
    scalars = [jnp.stack([h, seq_len, base, q, b, bit[1], bit[0], h * 0]), xor_blocks(seq_base, x_off)]
    w_table = S_TABLE + len(x_off)
    if direct:
        scalars += [xor_blocks(ring_at, w_off), xor_blocks(ring_at, p_off)]
        p_table = w_table + len(w_off)
    else:
        scalars += [jnp.zeros((8,), jnp.int32)]
        p_table = w_table
    idx = jnp.concatenate(scalars)

    positions = b * slot_dev + jnp.arange(slot_dev, dtype=jnp.int32)
    own_len = lax.dynamic_slice_in_dim(lengths, h * seq_dev, seq_dev)
    valid = (positions[None, :] < own_len[:, None]).reshape(tok)
    route_rows = jnp.transpose(routes.reshape(tok, 2))
    order = jnp.transpose(pair_order.reshape(tok, 2)).reshape(2 * tok)
    route = route_rows.reshape(2 * tok)
    eligible = jnp.concatenate([valid, valid]) & (route < NEXP)
    before = (
        (route[:, None] == route[None, :]) & (order[None, :] < order[:, None]) & eligible[None, :]
    )
    rank = jnp.sum(before.astype(jnp.int32), axis=1)
    slot = jnp.where(eligible & (rank < capacity), route * capacity + rank, NEXP * capacity)
    slot = slot.reshape(2, tok)
    slot_rows = jnp.concatenate([slot, jnp.zeros((6, tok), jnp.int32)], axis=0)
    ints = jnp.concatenate(
        [routes.reshape(tok, 2), jnp.transpose(slot), valid[:, None].astype(jnp.int32),
         jnp.zeros((tok, 3), jnp.int32)], axis=1)

    strips = width // (2 * unit)
    bundle = jnp.concatenate(
        [jnp.transpose(w_in, (1, 0, 2, 3)).reshape(e_loc, width, 2 * unit),
         jnp.transpose(w_down.reshape(unit, e_loc, strips, 2 * unit), (1, 2, 0, 3)).reshape(
             e_loc, strips * unit, 2 * unit)], axis=1)
    shares = [lax.dynamic_index_in_dim(bundle, q ^ d, 0, keepdims=False) for d in range(e_loc)]

    if direct:
        x_parts, swapped, early, shares, ints, slot_rows, cotangent, lengths = barrier(
            (x_parts, swapped, early, shares, ints, slot_rows, cotangent, lengths))
    for d in more:
        x_parts = x_parts + [hop(a, d) for a in x_parts]
    x_parts = x_parts + [hop(a, 2) for a in x_parts]
    if direct:
        first = jnp.concatenate([keep_w, came_w[:rows_here], *swapped], axis=0)
        w_parts = [first, hop(first, 4), hop(first, 1)]
        early = spread_to(early, 1)
    cot = cotangent.reshape(tok, width)
    per_send = e_loc * capacity
    (send_g,) = call(
        send_grad_kernel, [sds((heads * n_share, per_send, width), BF)], [slot_rows, cot, ints],
        name="send_grad")

    def to_experts(rows):
        flat = rows.reshape(heads * ring * capacity, rows.shape[-1])
        return lax.all_to_all(flat, ("head", "ring"), 0, 0, tiled=True)

    frequency = 10000.0 ** (-(2.0 * jnp.arange(HD // 2, dtype=F32)) / HD)
    slots_here = jnp.arange(n_slots, dtype=jnp.int32) + jnp.minimum(lengths[0], 0)
    angles = slots_here.astype(F32)[:, None] * frequency[None, :]
    cos_all = jnp.concatenate([jnp.cos(angles)] * 4, axis=1)
    sin_all = jnp.concatenate([jnp.sin(angles)] * 4, axis=1)
    prev = previous_layer_logits.reshape(tok, n_all)
    prev_wide = jnp.pad(prev, ((0, 0), (0, 128 - n_all)))
    prev_logits = jnp.pad(
        jnp.dot(prev, w_residual, precision=lax.Precision.HIGHEST), ((0, 0), (0, 128 - n_all)))
    if direct:
        x_parts, w_parts, early, send_g, cos_all, sin_all = barrier(
            (x_parts, w_parts, early, send_g, cos_all, sin_all))
        w_parts = w_parts + [hop(w_parts[1], 1)]
        early_parts = [early, partner(early)]
    else:
        wide_w = jnp.pad(w_qkv, ((0, 0), (0, 0), (0, 512 - part))).reshape(rows_here, 3, 4, 128)
        wide_w = jnp.transpose(wide_w, (0, 2, 1, 3)).reshape(rows_here, -1)
        (whole_w,) = gathered(wide_w)
        w_parts = [lax.dynamic_slice_in_dim(whole_w, (2 * bit[1] + core) * part, part, 1)]
        early_parts = gathered(early)
    x_parts = x_parts + [partner(a) for a in x_parts]
    g_rows = to_experts(send_g)
    x_parts, w_parts, early_parts = barrier((x_parts, w_parts, early_parts))

    attn_unit, lse, xn, qkv, early_all, w_pair = call(
        functools.partial(
            attend_kernel, len(x_parts), len(w_parts), len(early_parts), w_rows, p_rows),
        [sds((n_slots, 128), BF), sds((8, n_slots), F32), sds((n_slots, width), BF),
         sds((n_slots, 384), BF), sds((width, part + 128), BF), sds((width, 384), BF)],
        [idx, *x_parts, *w_parts, *early_parts, cos_all, sin_all], smem=1,
        scratch=[pltpu.VMEM((128, n_slots), BF)],
        flops=2 * n_slots * n_slots * 512 + 2 * n_slots * width * 384, name="attend",
        far_in=range(1, 3 + len(x_parts) + len(w_parts) + len(early_parts)),
        far_out=(0, 1, 2, 3, 4, 5))
    attn_unit, g_rows, shares = barrier((attn_unit, g_rows, shares))

    pieces = [hop(shares[d], d) for d in range(e_loc)]

    def exchange(x):
        flat = x.reshape(n_blk * (x.size // x.shape[-1] // n_blk), x.shape[-1])
        return lax.all_to_all(flat, blk, 0, 0, tiled=True)

    attn_recv = exchange(attn_unit).reshape(n_blk, slot_dev, 128)
    attn_recv, pieces[:-1] = barrier((attn_recv, pieces[:-1]))
    w_out_all = Columns(early_all, part, 0)
    mine, other, attn_low = call(
        out_kernel,
        [sds((tok, width), F32), sds((tok, width), BF), sds((n_seq * slot_dev, part), BF)],
        [idx, attn_recv, w_out_all], smem=1,
        scratch=[pltpu.VMEM((n_seq * slot_dev, width), F32)],
        flops=2 * n_seq * slot_dev * width * part, name="out", far_in=(2,), far_out=(2,))
    w_small_all = Columns(early_all, 128, part)
    send_x, residual, aux, small = call(
        route_kernel,
        [sds((heads * n_share, per_send, width + 128), BF), sds((tok, width), F32),
         sds((tok, 128), F32), sds((24, width), F32)],
        [flat_tokens, mine, across(other), w_small_all, prev_logits, ints, slot_rows],
        flops=tok * width * 1000, name="route", far_in=(3, 4, 5), far_out=(1, 2, 3))
    send_x, pieces = barrier((send_x, pieces))
    pieces = pieces + [partner(p) for p in pieces]
    x_rows = to_experts(send_x)
    x_rows, pieces = barrier((x_rows, pieces))
    group = max(1, 128 // unit)
    if group > 1:
        pieces = [join(pieces[i : i + group]) for i in range(0, len(pieces), group)]
    back_rows, *grad_pieces = experts(x_rows, g_rows, pieces)
    back_recv = to_experts(back_rows)

    if group > 1:
        grad_pieces = [part_of for full in grad_pieces for part_of in divide(full)]
    ours = list(grad_pieces[:e_loc])
    theirs = [partner(p) for p in grad_pieces[e_loc:]]
    recv = back_recv.reshape(heads * n_share, per_send, 2 * width)
    added = call(
        functools.partial(pair_add_kernel, e_loc), [sds(p.shape, BF) for p in ours], ours + theirs,
        name="pair_add", far_in=range(2 * e_loc), far_out=range(e_loc))

    came = [added[0], hop(added[1], 1)]
    half_way = hop(added[3], 2)
    recv, added, came, half_way = barrier((recv, added, came, half_way))
    output, grad_res, grad_low, sums = call(
        combine_kernel,
        [sds((tok, width), F32), sds((tok, width), F32), sds((tok, width), BF), sds((40, width), F32)],
        [recv, residual, cot, small, w_small_all, ints, aux, prev_wide], flops=tok * width * 2000,
        name="combine", far_in=(1, 2, 3, 4, 5, 6, 7), far_out=(0, 1))

    came = came + [hop(added[2], 2), hop(half_way, 1)]
    pay = (n_blk // 2, rows_here, part + 128)
    send_gv, grad_both = call(
        grad_vec_kernel,
        [sds((n_blk, slot_dev, 128), BF), sds((n_seq * slot_dev, width), BF)],
        [idx, grad_low, across(grad_low), w_out_all], smem=1,
        flops=2 * n_seq * slot_dev * width * part, name="grad_vec", far_in=(3,), far_out=(1,))
    dout = exchange(send_gv)
    keep, give = call(
        pay_kernel, [sds(pay, F32), sds(pay, BF)],
        [idx, grad_both, attn_low, sums, across(sums)], smem=1,
        scratch=[pltpu.VMEM((n_blk, rows_here, part + 128), F32)],
        flops=2 * n_seq * slot_dev * width * part, name="pay", far_in=(1, 2, 3), far_out=(0, 1))
    steps = [1 << (i - 1) for i in halving_bits(n_blk)[1:]]

    def halve(keep, came_sum, d):
        half = (keep.shape[0] // 2,) + keep.shape[1:]
        keep, give = call(
            halve_kernel, [sds(half, F32), sds(half, BF)], [keep, came_sum], name="halve")
        return keep, hop(give, d)

    came_sum = partner(give)
    dout, came, came_sum = barrier((dout, came, came_sum))

    keep, came_sum = halve(keep, came_sum, steps[0])
    (grad_unit,) = call(
        attend_back_kernel, [sds((n_slots, 384), BF)],
        [idx, qkv, dout, attn_unit, lse, cos_all, sin_all], smem=1,
        scratch=[pltpu.VMEM((128, n_slots), BF), pltpu.VMEM((n_slots, 128), F32),
                 pltpu.VMEM((n_slots, 128), F32)],
        flops=5 * n_slots * n_slots * 256, name="attend_back", far_in=(1, 3, 4, 5, 6), far_out=())
    grad_unit, came_sum = barrier((grad_unit, came_sum))
    rows8 = (8, slot_dev, width)
    gn_keep, gn_give = call(
        unit_back_kernel, [sds(rows8, F32), sds(rows8, BF)], [idx, grad_unit, w_pair], smem=1,
        scratch=[pltpu.VMEM((n_slots, width), F32)], flops=2 * n_slots * width * 384,
        name="unit_back", far_in=(2,), far_out=(0,))
    gn_came = partner(gn_give)
    owners = (8, rows_here, 384)
    dw_keep, dw_give = call(
        unit_dw_kernel, [sds(owners, F32), sds(owners, BF)], [idx, xn, grad_unit], smem=1,
        scratch=[pltpu.VMEM((n_blk, rows_here, 384), F32)],
        flops=2 * n_slots * width * 384, name="unit_dw", far_in=(1,), room=20)
    gn_came, dw_give, came_sum = barrier((gn_came, dw_give, came_sum))
    dw_came = hop(dw_give, 1)
    gn_keep, gn_came = halve(gn_keep, gn_came, 2)
    keep, came_sum = halve(keep, came_sum, steps[1])
    def by_source(parts):
        chosen = []
        for e in range(e_loc):
            value = parts[e_loc - 1]
            for d in range(e_loc - 1):
                value = jnp.where((q ^ d) == e, parts[d], value)
            chosen.append(value.astype(F32))
        return chosen

    if group == 1:
        in_sum, down_sum = call(
            functools.partial(place_kernel, e_loc),
            [sds((width * e_loc * 2, 128), F32), sds((unit, e_loc, width), F32)],
            [idx, *came], smem=1, name="place", far_in=range(1, e_loc + 1), far_out=(0, 1))
        in_sum = in_sum.reshape(width, e_loc, 2, unit)
    else:
        in_sum = jnp.stack(by_source([p[:width].reshape(width, 2, unit) for p in came]), axis=1)
        down_sum = by_source([p[width:].reshape(strips, unit, 2 * unit) for p in came])
        down_sum = jnp.transpose(jnp.stack(down_sum, axis=0), (2, 0, 1, 3))
        down_sum = down_sum.reshape(unit, e_loc, width)
    gn_came, in_sum, down_sum, came_sum, dw_came = barrier(
        (gn_came, in_sum, down_sum, came_sum, dw_came))
    rows2 = (2, slot_dev, width)
    gn_parts = call(
        both_kernel, [sds(rows2, BF), sds(rows2, BF)], [gn_keep, gn_came], name="both")
    gn_parts = [
        lax.ppermute(a, both_axes, [(t, f) for f, t in to_head(same)])
        for a, same in zip(gn_parts, (True, False))]
    dw_keep, dw_came = halve(dw_keep, dw_came, 4)
    for d in steps[2:]:
        keep, came_sum = halve(keep, came_sum, d)
    gn_parts, came_sum, dw_came = barrier((gn_parts, came_sum, dw_came))
    two_owners = (2, rows_here, 384)
    dw_stay, dw_go = call(
        both_kernel, [sds(two_owners, BF), sds(two_owners, BF)], [dw_keep, dw_came], name="both_dw")
    dw_far = hop(dw_go, 2)
    dw_near = partner(jnp.concatenate([dw_stay[1:], dw_far[1:]], axis=0))
    gn_own, gn_away = call(
        heads_kernel, [sds((slot_dev, width), F32), sds((slot_dev, width), BF)], list(gn_parts),
        name="heads")
    gn_near = hop(gn_away, 1)
    gn_near, dw_near = barrier((gn_near, dw_near))
    qkv_sum, gain1_part = call(
        total_kernel, [sds((3, rows_here, part), F32), sds((8, rows_here), F32)],
        [idx, dw_stay, dw_far, dw_near, w_phys, gain_row_in], smem=1,
        scratch=[pltpu.VMEM((4, rows_here, 384), F32)], name="total", far_in=(4, 5))
    gain1_sum = gain1_part[0] + across(gain1_part)[0]

    out_sum, gain2_sum, router_sum, const_sum, vec_sum, resid_sum = call(
        functools.partial(last_add_kernel, n_all),
        [sds((rows_here, part), F32), sds((1, rows_here), F32), sds((n_all, rows_here), F32),
         sds((4, rows_here), F32), sds((2, rows_here), F32), sds((n_all, n_all), F32)],
        [keep, came_sum], name="last_add")
    (grad_tokens,) = call(
        final_kernel, [sds((tok, width), F32)],
        [idx, flat_tokens, gn_own, gn_near, grad_res, small], smem=1,
        scratch=[pltpu.VMEM((tok, width), F32)], name="final", far_in=(1, 4, 5), far_out=(0,))
    return (
        output.reshape(tokens.shape),
        grad_tokens.reshape(tokens.shape),
        gain1_sum,
        jnp.transpose(qkv_sum, (1, 0, 2)),
        out_sum,
        gain2_sum.reshape(rows_here),
        jnp.transpose(router_sum),
        resid_sum,
        jnp.transpose(const_sum),
        jnp.transpose(vec_sum),
        in_sum,
        down_sum,
    )


def solution(mesh):
    heads, blocks = mesh.devices.shape
    split = Mesh(mesh.devices.reshape(heads, blocks // 2, 2), ("head", "ring", "core"))
    blk = ("ring", "core")
    in_specs = (
        P("head", blk, None),
        P("head", blk, None),
        P(),
        P("head", blk, None),
        P("head", blk, None),
        P(blk),
        P(blk, None, "head"),
        P(blk, "head"),
        P(blk),
        P(blk, None),
        P(),
        P(blk, None),
        P(blk, None),
        P(None, "head", None, blk),
        P(blk, "head", None),
        P("head", blk, None),
    )
    out_specs = (
        P("head", blk, None),
        P("head", blk, None),
        P(blk),
        P(blk, None, "head"),
        P(blk, "head"),
        P(blk),
        P(blk, None),
        P(),
        P(blk, None),
        P(blk, None),
        P(None, "head", None, blk),
        P(blk, "head", None),
    )
    return jax.shard_map(
        per_device, mesh=split, in_specs=in_specs, out_specs=out_specs, check_vma=False
    )
```

```python
import functools
import math

import jax
import jax.numpy as jnp
import numpy as np
from jax import lax
from jax.experimental import pallas as pl
from jax.experimental.pallas import tpu as pltpu
from jax.sharding import Mesh
from jax.sharding import PartitionSpec as P

HD = 64
NEXP = 8
EPS = 1e-05
NEG = -1e30
BF = jnp.bfloat16
F32 = jnp.float32
MIB = 1 << 20
ANY2 = (((1,), (1,)), ((), ()))
MM = (((1,), (0,)), ((), ()))
C_CONST, C_VEC, C_GAIN1, C_GAIN2 = 12, 16, 18, 19
RESID = 32
S_HEAD, S_LEN, S_BASE, S_EXPERT, S_BLOCK, S_BIT, S_TABLE = 0, 1, 2, 3, 4, 5, 8


def dot(a, b, dims=MM):
    return lax.dot_general(a, b, dims, preferred_element_type=F32)


def whole_block(shape):
    return pl.BlockSpec(shape, lambda i: (0,) * len(shape), pipeline_mode=pl.Buffered(1))


def far(x):
    return pltpu.with_memory_space_constraint(x, pltpu.HBM)


class Columns:
    def __init__(self, array, count, at):
        self.array, self.at, self.window = array, (0, at // count), (array.shape[0], count)
        self.shape, self.dtype = self.window, array.dtype


def call(kernel, outs, args, smem=0, scratch=(), room=12, flops=0, name=None,
         far_in=(), far_out=()):
    sm = pl.BlockSpec(memory_space=pltpu.SMEM)
    total = sum(math.prod(a.shape) * a.dtype.itemsize for a in list(args) + list(outs))
    limit = total + sum(math.prod(a.shape) * a.dtype.itemsize for a in scratch) + room * MIB
    specs = [
        pl.BlockSpec(a.window, functools.partial(lambda at, i: at, a.at), pipeline_mode=pl.Buffered(1))
        if isinstance(a, Columns) else whole_block(a.shape) for a in args[smem:]]
    args = [a.array if isinstance(a, Columns) else a for a in args]
    args = [far(a) if i in far_in else a for i, a in enumerate(args)]
    shapes = tuple(pltpu.HBM(o.shape, o.dtype) if i in far_out else o for i, o in enumerate(outs))
    return pl.pallas_call(
        kernel,
        grid=(1,),
        out_shape=shapes,
        in_specs=[sm] * smem + specs,
        out_specs=tuple(whole_block(o.shape) for o in outs),
        scratch_shapes=list(scratch),
        compiler_params=pltpu.CompilerParams(vmem_limit_bytes=min(limit, 60 * MIB)),
        cost_estimate=pl.CostEstimate(flops=flops, bytes_accessed=total, transcendentals=0),
        name=name,
    )(*args)


def sds(shape, dtype):
    return jax.ShapeDtypeStruct(shape, dtype)


def unit_at(seq, pair):
    ring = (seq >> 1) * 4 + (pair >> 1) * 2 + (seq & 1)
    return ring * 2 + (pair & 1)


def idle_units(n_blk, n_seq, pairs):
    busy = {unit_at(q, p) for q in range(n_seq) for p in range(pairs)}
    return [u for u in range(n_blk) if u not in busy]


def halving_bits(n):
    return [0, 1, 3, 2] + list(range(4, n.bit_length() - 1))


def halving_order(n):
    bits = halving_bits(n)
    last = len(bits) - 1
    return [sum(((k >> (last - i)) & 1) << b for i, b in enumerate(bits)) for k in range(n)]


def gather_rows(dst, arrays, idx, base, rows):
    j = base
    for a in arrays:
        for i in range(a.shape[0] // rows):
            at = idx[j] * rows
            if rows % 16 == 0:
                at = pl.multiple_of(at, 16)
            dst[pl.ds(at, rows), :] = a[i * rows : (i + 1) * rows, :]
            j += 1


def lower_lanes(shape):
    return (lax.broadcasted_iota(jnp.int32, shape, 1) & 63) < 32


def turned(values):
    return jnp.where(
        lower_lanes(values.shape), -pltpu.roll(values, 96, 1), pltpu.roll(values, 32, 1)
    )


def head_mask(shape, which):
    lane = lax.broadcasted_iota(jnp.int32, shape, 1)
    return (lane >= 64) if which else (lane < 64)


def only(values, which):
    return jnp.where(head_mask(values.shape, which), values, jnp.zeros_like(values))


def scores_of(k_rows, q_head, first_query, limit_len):
    s = dot(k_rows, q_head, ANY2)
    key = lax.broadcasted_iota(jnp.int32, s.shape, 0)
    query = lax.broadcasted_iota(jnp.int32, (1, s.shape[1]), 1) + first_query
    last = jnp.minimum(query, limit_len - 1)
    return jnp.where(key <= last, s, NEG)


def each_block(total, block, fn):
    if total // block <= 4:
        for i in range(total // block):
            fn(i * block, (i + 1) * block)
    else:

        @pl.loop(0, total // block)
        def _(i):
            fn(pl.multiple_of(i * block, block), total)


def attend_kernel(n_x, n_w, n_p, w_rows, p_rows, idx, *refs):
    xs, ws, ps = refs[:n_x], refs[n_x : n_x + n_w], refs[n_x + n_w : n_x + n_w + n_p]
    cos, sin, out, lse, xn, qkv, early, wg, vt = refs[n_x + n_w + n_p :]
    total = qkv.shape[0]
    block = 256
    slots = 64
    limit_len = idx[S_LEN]
    j = S_TABLE + sum(a.shape[0] // slots for a in xs)
    gather_rows(wg, ws, idx, j, w_rows)
    gather_rows(early, ps, idx, j + sum(a.shape[0] // w_rows for a in ws), p_rows)
    columns = early[:, early.shape[1] - 128 :].astype(F32)
    gain = jnp.transpose(columns)[C_GAIN1 : C_GAIN1 + 1]
    j = S_TABLE
    for a in xs:
        for i in range(a.shape[0] // slots):
            x = a[i * slots : (i + 1) * slots, :].astype(F32)
            rstd = lax.rsqrt(jnp.mean(x * x, axis=-1, keepdims=True) + EPS)
            at = pl.ds(pl.multiple_of(idx[j] * slots, slots), slots)
            xn[at, :] = (x * rstd * gain).astype(BF)
            j += 1

    def project(start, _):
        at = pl.ds(start, block)
        y = dot(xn[at, :], wg[...])
        c, s = cos[at, :], sin[at, :]
        q, k = y[:, 0:128], y[:, 128:256]
        q = (q * c + turned(q) * s) * (1.0 / math.sqrt(HD))
        qkv[at, 0:128] = q.astype(BF)
        qkv[at, 128:256] = (k * c + turned(k) * s).astype(BF)
        qkv[at, 256:384] = y[:, 256:384].astype(BF)

    each_block(total, block, project)
    vt[...] = jnp.transpose(qkv[:, 256:384])

    def step(start, n_keys):
        q = qkv[pl.ds(start, block), 0:128]
        parts = []
        for h in range(2):
            s = scores_of(qkv[0:n_keys, 128:256], only(q, h), start, limit_len)
            m = jnp.max(s, axis=0, keepdims=True)
            p = jnp.exp(s - m)
            total_p = jnp.sum(p, axis=0, keepdims=True)
            o = dot(vt[h * 64 : (h + 1) * 64, 0:n_keys], p.astype(BF))
            parts.append(o / total_p)
            lse[h : h + 1, pl.ds(start, block)] = m + jnp.log(total_p)
        out[pl.ds(start, block), :] = jnp.transpose(jnp.concatenate(parts, axis=0)).astype(BF)

    each_block(total, block, step)


def unit_dw_kernel(idx, xn, grad, keep, give, full):
    dw = dot(jnp.transpose(xn[...]), grad[...])
    owned = full.shape[1]
    for i in range(full.shape[0]):
        full[i] = dw[i * owned : (i + 1) * owned]
    for n, offset in enumerate(a + b + c for a in (0, 8) for b in (0, 4) for c in (0, 1)):
        keep[n] = full[idx[S_BLOCK] ^ offset]
        give[n] = full[idx[S_BLOCK] ^ (offset + 2)].astype(BF)


def attend_back_kernel(idx, qkv, dout, out, lse, cos, sin, grad, kt, dk, dv):
    total = qkv.shape[0]
    block = 256
    limit_len = idx[S_LEN]
    kt[...] = jnp.transpose(qkv[:, 128:256])
    dk[...] = jnp.zeros_like(dk)
    dv[...] = jnp.zeros_like(dv)

    def unrotate(values, at, size):
        c, s = cos[pl.ds(at, size), :], sin[pl.ds(at, size), :]
        return values * c - turned(values) * s

    def step(start, n_keys):
        q = qkv[pl.ds(start, block), 0:128]
        do = dout[pl.ds(start, block), :]
        prod_t = jnp.transpose(do.astype(F32) * out[pl.ds(start, block), :].astype(F32))
        probs, ds, dq = [], [], []
        for h in range(2):
            q_head, do_head = only(q, h), only(do, h)
            s = scores_of(qkv[0:n_keys, 128:256], q_head, start, limit_len)
            p = jnp.exp(s - lse[h : h + 1, pl.ds(start, block)])
            delta = jnp.sum(prod_t[h * 64 : (h + 1) * 64], axis=0, keepdims=True)
            dp = dot(qkv[0:n_keys, 256:384], do_head, ANY2)
            d = (p * (dp - delta)).astype(BF)
            probs.append(p.astype(BF))
            ds.append(d)
            dq.append(dot(kt[h * 64 : (h + 1) * 64, 0:n_keys], d))
        both_q = jnp.concatenate([only(q, 0), only(q, 1)], axis=0)
        both_do = jnp.concatenate([only(do, 0), only(do, 1)], axis=0)
        dv[0:n_keys, :] += dot(jnp.concatenate(probs, axis=1), both_do)
        dk[0:n_keys, :] += dot(jnp.concatenate(ds, axis=1), both_q)
        gq = jnp.transpose(jnp.concatenate(dq, axis=0)) * (1.0 / math.sqrt(HD))
        grad[pl.ds(start, block), 0:128] = unrotate(gq, start, block).astype(BF)

    each_block(total, block, step)

    def finish(start, _):
        at = pl.ds(start, block)
        grad[at, 128:256] = unrotate(dk[at, :], start, block).astype(BF)
        grad[at, 256:384] = dv[at, :].astype(BF)

    each_block(total, block, finish)


def out_kernel(idx, recv, wos, mine, other, attn, full):
    h = idx[S_HEAD]
    part = attn.shape[1]
    slots = recv.shape[1]
    n_seq = attn.shape[0] // slots
    for p in range(part // 128):
        for q in range(n_seq):
            attn[q * slots : (q + 1) * slots, p * 128 : (p + 1) * 128] = recv[unit_at(q, p)]
    full[...] = dot(attn[...], wos[...], ANY2)
    rows = mine.shape[0]
    mine[...] = full[pl.ds(h * rows, rows), :]
    other[...] = full[pl.ds((1 - h) * rows, rows), :].astype(BF)


def onehot_rows(slots, n_rows):
    at = lax.broadcasted_iota(jnp.int32, (n_rows, slots.shape[1]), 0)
    return jnp.where((at == slots[0:1]) | (at == slots[1:2]), 1.0, 0.0).astype(BF)


def spread(rows, send):
    per = send.shape[1]
    copies = send.shape[0] * per // rows.shape[0]
    for i in range(send.shape[0]):
        at = (i // copies) * per
        send[i] = rows[at : at + per]


def send_grad_kernel(slots, cot, ints, send):
    g = (cot[...] * ints[:, 4:5].astype(F32)).astype(BF)
    n_rows = send.shape[1] * 2
    spread(dot(onehot_rows(slots[...], n_rows), g).astype(BF), send)


def norm_two(residual, gain):
    rstd = lax.rsqrt(jnp.mean(residual * residual, axis=-1, keepdims=True) + EPS)
    xhat = residual * rstd
    return rstd, xhat, xhat * gain


def route_kernel(tokens, mine, other, wpack, prev_logits, ints, slots, send, residual, aux, small):
    res = tokens[...].astype(F32) + mine[...] + other[...].astype(F32)
    residual[...] = res
    small[...] = jnp.transpose(wpack[...].astype(F32))[: small.shape[0]]
    _, _, normed = norm_two(res, small[C_GAIN2 : C_GAIN2 + 1])
    low = normed.astype(BF)
    logits = dot(low, wpack[...]) + prev_logits[...]
    lane = lax.broadcasted_iota(jnp.int32, logits.shape, 1)

    def pick(which):
        return jnp.sum(jnp.where(lane == which, logits, 0.0), axis=1, keepdims=True)

    def pair_softmax(a, b):
        top = jnp.maximum(a, b)
        ea, eb = jnp.exp(a - top), jnp.exp(b - top)
        return ea / (ea + eb), eb / (ea + eb)

    p0, p1 = pair_softmax(pick(ints[:, 0:1]), pick(ints[:, 1:2]))
    a00, a01 = pair_softmax(pick(C_CONST), pick(C_CONST + 1))
    a10, a11 = pair_softmax(pick(C_CONST + 2), pick(C_CONST + 3))
    info = jnp.zeros_like(logits)
    for i, v in enumerate((p0, p1, a00, a01, a10, a11)):
        info = jnp.where(lane == i, v, info)
    aux[...] = info
    n_rows = send.shape[1] * 2
    tok = slots.shape[1]
    at = lax.broadcasted_iota(jnp.int32, (n_rows, tok), 0)
    first = jnp.where(at == slots[0:1], 1.0, 0.0).astype(BF)
    second = jnp.where(at == slots[1:2], 1.0, 0.0).astype(BF)

    def split(v, base):
        high = v.astype(BF).astype(F32)
        return jnp.where(lane == 0, high, jnp.where(lane == 1, v - high, base))

    extra = dot(first, split(p0, 0.0).astype(BF)) + dot(second, split(p1, 0.0).astype(BF))
    rows = jnp.concatenate([dot(first + second, low), extra], axis=1)
    spread(rows.astype(BF), send)


def expert_kernel(n_pieces, n_steps, x_ref, g_ref, *refs):
    w, back, grads = refs[:n_pieces], refs[n_pieces], refs[n_pieces + 1 : 2 * n_pieces + 1]
    wd_all = refs[2 * n_pieces + 1]
    acc = refs[2 * n_pieces + 2] if n_steps > 1 else None
    step = pl.program_id(0)
    width = g_ref.shape[1]
    two = w[0].shape[1]
    unit = two // 2
    strips = width // two

    @pl.when(step == 0)
    def _():
        for d in range(n_pieces):
            for j in range(strips):
                at = width + j * unit
                wd_all[d * unit : (d + 1) * unit, j * two : (j + 1) * two] = w[d][at : at + unit, :]

    x = x_ref[:, :width]
    g = g_ref[...]
    prob = jnp.sum(x_ref[:, width:].astype(F32), axis=1, keepdims=True)
    xt = jnp.transpose(x)
    g_scaled = (g.astype(F32) * prob).astype(BF)
    up_grad = dot(g, wd_all[...], ANY2) * prob
    hiddens = []
    grad_in = jnp.zeros((x.shape[0], width), F32)

    def keep(d, start, value):
        at = slice(start, start + value.shape[0])
        if n_steps == 1:
            grads[d][at, :] = value.astype(BF)
            return

        @pl.when(step == 0)
        def _():
            acc[d, at, :] = value

        @pl.when(step > 0)
        def _():
            acc[d, at, :] += value

        @pl.when(step == n_steps - 1)
        def _():
            grads[d][at, :] = acc[d, at, :].astype(BF)

    for d in range(n_pieces):
        both = dot(x, w[d][:width, :])
        gate, up = both[:, :unit], both[:, unit:]
        sig = 1.0 / (1.0 + jnp.exp(-gate))
        act = gate * sig
        hidden = (act * up).astype(BF)
        hiddens.append(hidden)
        gh = up_grad[:, d * unit : (d + 1) * unit]
        g_gate = gh * up * sig * (1.0 + gate * (1.0 - sig))
        g_both = jnp.concatenate([g_gate, gh * act], axis=1).astype(BF)
        grad_in += dot(g_both, w[d][:width, :], ANY2)
        keep(d, 0, dot(xt, g_both))
        gd = dot(jnp.transpose(hidden), g_scaled)
        for j in range(strips):
            keep(d, width + j * unit, gd[:, j * two : (j + 1) * two])
    back[:, :width] = dot(jnp.concatenate(hiddens, axis=1), wd_all[...]).astype(BF)
    back[:, width:] = grad_in.astype(BF)


def experts(x_rows, g_rows, pieces):
    n = len(pieces)
    rows, wide = x_rows.shape
    width = g_rows.shape[1]
    deep, two = pieces[0].shape
    unit = two // 2
    block = 384 if rows % 384 == 0 else rows
    steps = rows // block
    outs = [sds((rows, 2 * width), BF)] + [sds((deep, two), BF)] * n
    scratch = [pltpu.VMEM((n * unit, width), BF)]
    if steps > 1:
        scratch.append(pltpu.VMEM((n, deep, two), F32))
    return pl.pallas_call(
        functools.partial(expert_kernel, n, steps),
        grid=(steps,),
        in_specs=[
            pl.BlockSpec((block, wide), lambda i: (i, 0)),
            pl.BlockSpec((block, width), lambda i: (i, 0)),
        ]
        + [whole_block(a.shape) for a in pieces],
        out_specs=tuple(
            [pl.BlockSpec((block, 2 * width), lambda i: (i, 0))]
            + [whole_block(o.shape) for o in outs[1:]]
        ),
        out_shape=tuple(outs[:1] + [pltpu.HBM(o.shape, o.dtype) for o in outs[1:]]),
        scratch_shapes=scratch,
        compiler_params=pltpu.CompilerParams(vmem_limit_bytes=(30 if steps == 1 else 48) * MIB),
        cost_estimate=pl.CostEstimate(
            flops=18 * rows * width * unit * n,
            bytes_accessed=8 * rows * width + 12 * width * unit * n,
            transcendentals=0,
        ),
        name="experts",
    )(x_rows, far(g_rows), *[far(p) for p in pieces])


def combine_kernel(recv, residual, cot, small, wpack, ints, aux, prev, out, grad_res, grad_low, sums):
    res = residual[...]
    gain = small[C_GAIN2 : C_GAIN2 + 1]
    rstd, xhat, normed = norm_two(res, gain)
    low = normed.astype(BF)
    width = res.shape[1]
    heads = 2
    copies = recv.shape[0] // heads
    groups = []
    for h in range(heads):
        total = recv[h * copies].astype(F32)
        for r in range(1, copies):
            total = total + recv[h * copies + r].astype(F32)
        groups.append(total.astype(BF))
    rows = jnp.concatenate(groups, axis=0)
    valid = ints[:, 4:5].astype(F32)
    go = cot[...] * valid
    lane = lax.broadcasted_iota(jnp.int32, (res.shape[0], rows.shape[0]), 1)
    first = jnp.where(lane == ints[:, 2:3], 1.0, 0.0).astype(BF)
    second = jnp.where(lane == ints[:, 3:4], 1.0, 0.0).astype(BF)
    eo0 = dot(first, rows[:, :width])
    eo1 = dot(second, rows[:, :width])
    gin = dot(first + second, rows[:, width:])
    info = aux[...]
    p0, p1 = info[:, 0:1], info[:, 1:2]
    alpha = ((info[:, 2:3], info[:, 3:4]), (info[:, 4:5], info[:, 5:6]))
    r0, r1 = ints[:, 0:1], ints[:, 1:2]

    def at(route, which):
        return jnp.where(route == which, 1.0, 0.0)

    vec = (small[C_VEC : C_VEC + 1], small[C_VEC + 1 : C_VEC + 2])
    share0 = at(r0, NEXP + 1) + at(r0, NEXP + 2) * alpha[0][0] + at(r0, NEXP + 3) * alpha[1][0]
    share1 = at(r1, NEXP + 1) + at(r1, NEXP + 2) * alpha[0][0] + at(r1, NEXP + 3) * alpha[1][0]
    weight = [p0 * at(r0, NEXP + 2 + j) + p1 * at(r1, NEXP + 2 + j) for j in range(2)]
    mixed = (
        p0 * eo0
        + p1 * eo1
        + (p0 * share0 + p1 * share1) * normed
        + (weight[0] * alpha[0][1]) * vec[0]
        + (weight[1] * alpha[1][1]) * vec[1]
    )
    out[...] = valid * (res + mixed)

    def rowsum(v):
        return jnp.sum(v, axis=1, keepdims=True)

    s_norm = rowsum(go * normed)
    s_vec = [rowsum(go * vec[j]) for j in range(2)]
    gg0 = rowsum(go * eo0) + share0 * s_norm
    gg1 = rowsum(go * eo1) + share1 * s_norm
    for j in range(2):
        gg0 = gg0 + at(r0, NEXP + 2 + j) * alpha[j][1] * s_vec[j]
        gg1 = gg1 + at(r1, NEXP + 2 + j) * alpha[j][1] * s_vec[j]
    gsum = p0 * gg0 + p1 * gg1
    c0, c1 = p0 * (gg0 - gsum), p1 * (gg1 - gsum)
    wide = lax.broadcasted_iota(jnp.int32, (res.shape[0], 128), 1)
    dl = jnp.where(wide == r0, c0, 0.0) + jnp.where(wide == r1, c1, 0.0)
    coef = p0 * at(r0, NEXP + 1) + p1 * at(r1, NEXP + 1)
    vec_rows = []
    for j in range(2):
        ga0, ga1 = weight[j] * s_norm, weight[j] * s_vec[j]
        mean = alpha[j][0] * ga0 + alpha[j][1] * ga1
        dl = jnp.where(wide == C_CONST + 2 * j, alpha[j][0] * (ga0 - mean), dl)
        dl = jnp.where(wide == C_CONST + 2 * j + 1, alpha[j][1] * (ga1 - mean), dl)
        coef = coef + alpha[j][0] * weight[j]
        vec_rows.append(jnp.sum((alpha[j][1] * weight[j]) * go, axis=0, keepdims=True))
    dl = dl.astype(BF)
    dlt = jnp.transpose(dl)
    proj = dot(dlt, low)
    resid = lax.dot_general(
        jnp.transpose(prev[...]), jnp.where(wide < C_CONST, dl.astype(F32), 0.0), MM,
        precision=lax.Precision.HIGHEST, preferred_element_type=F32,
    )
    gn = gin + coef * go + dot(dl, wpack[...], ANY2)
    gain_row = jnp.sum(gn * xhat, axis=0, keepdims=True)
    row = lax.broadcasted_iota(jnp.int32, (24, 1), 0)
    table = jnp.where(row < C_VEC, proj[:24], 0.0)
    table = jnp.where(row == C_VEC, vec_rows[0], table)
    table = jnp.where(row == C_VEC + 1, vec_rows[1], table)
    sums[:24, :] = jnp.where(row == C_GAIN2, gain_row, table)
    sums[24:, :128] = resid[: sums.shape[0] - 24]
    sums[24:, 128:] = jnp.zeros((sums.shape[0] - 24, sums.shape[1] - 128), F32)
    ghat = gn * gain
    grad = go + rstd * (ghat - xhat * jnp.mean(ghat * xhat, axis=-1, keepdims=True))
    grad_res[...] = grad
    grad_low[...] = grad.astype(BF)


def grad_vec_kernel(idx, mine, other, wos, send, both):
    h = idx[S_HEAD]
    rows = mine.shape[0]
    both[pl.ds(h * rows, rows), :] = mine[...]
    both[pl.ds((1 - h) * rows, rows), :] = other[...]
    part = wos.shape[1]
    g = both[...]
    gv = dot(g, wos[...]).astype(BF)
    slots = send.shape[1]
    n_seq = g.shape[0] // slots
    for p in range(part // 128):
        for q in range(n_seq):
            send[unit_at(q, p)] = gv[q * slots : (q + 1) * slots, p * 128 : (p + 1) * 128]
    for u in idle_units(send.shape[0], n_seq, part // 128):
        send[u] = jnp.zeros(send.shape[1:], BF)


def pay_kernel(idx, both, attn, sums, more_sums, keep, give, pay):
    part = attn.shape[1]
    dw = dot(jnp.transpose(both[...]), attn[...])
    total = sums[...] + more_sums[...]
    table = jnp.concatenate([total[:24], jnp.zeros((104, total.shape[1]), F32)], axis=0)
    columns = jnp.transpose(table)
    n, owned, _ = pay.shape
    resid = jnp.concatenate([total[24:, :128], jnp.zeros((88 + 24, 128), F32)], axis=0)
    block = pltpu.roll(resid[:owned, :], RESID, 1)
    for i in range(n):
        at = i * owned
        pay[i, :, :part] = dw[at : at + owned]
        pay[i, :, part:] = columns[at : at + owned] + block
    for k, offset in enumerate(halving_order(n)):
        value = pay[idx[S_BLOCK] ^ offset]
        if k < n // 2:
            keep[k] = value
        else:
            give[k - n // 2] = value.astype(BF)


def halve_kernel(mine, came, keep, give):
    half = keep.shape[0]
    keep[...] = mine[:half] + came[:half].astype(F32)
    give[...] = (mine[half:] + came[half:].astype(F32)).astype(BF)


def last_add_kernel(n_all, mine, came, dw, gain2, router, const, vec, resid):
    total = mine[0] + came[0].astype(F32)
    dw[...] = total[:, : dw.shape[1]]
    table = total[:, dw.shape[1] :]
    rows = jnp.transpose(table)
    router[...] = rows[:n_all]
    const[...] = rows[C_CONST:C_VEC]
    vec[...] = rows[C_VEC : C_VEC + 2]
    gain2[...] = rows[C_GAIN2 : C_GAIN2 + 1]
    resid[...] = table[:n_all, RESID : RESID + n_all]


def unit_back_kernel(idx, grad, w_pair, keep, give, full):
    slots = keep.shape[1]
    block = 256

    def step(start, _):
        at = pl.ds(start, block)
        full[at, :] = dot(grad[at, :], w_pair[...], ANY2)

    each_block(full.shape[0], block, step)
    for k in range(2):
        for n, (far, third, first) in enumerate((a, b, c) for a in (0, 4) for b in (0, 8) for c in (0, 2)):
            which = idx[S_BASE] ^ (k + far + third + first)
            rows = full[pl.ds(pl.multiple_of(which * slots, slots), slots), :]
            if k == 0:
                keep[n] = rows
            else:
                give[n] = rows.astype(BF)


def both_kernel(mine, came, first, second):
    total = mine[...] + came[...].astype(F32)
    half = first.shape[0]
    first[...] = total[:half].astype(BF)
    second[...] = total[half:].astype(BF)


def heads_kernel(a, b, own, away):
    total = a[...].astype(F32) + b[...].astype(F32)
    own[...] = total[0]
    away[...] = total[1].astype(BF)


def total_kernel(idx, stay, far_pair, core_pairs, w, gain, dw, gain_row, pieces):
    part = dw.shape[2]
    owned = dw.shape[1]
    column = jnp.transpose(jnp.broadcast_to(gain[...].astype(F32), (8, owned)))[:, 0:1]
    rowsum = jnp.zeros((owned, 1), F32)
    pieces[0], pieces[2] = stay[0].astype(F32), far_pair[0].astype(F32)
    pieces[1], pieces[3] = core_pairs[0].astype(F32), core_pairs[1].astype(F32)
    this_pair = 2 * idx[S_BIT] + (idx[S_BLOCK] & 1)
    for p in range(part // 128):
        total = pieces[this_pair ^ p]
        for k in range(3):
            piece = total[:, k * 128 : (k + 1) * 128]
            at = slice(p * 128, (p + 1) * 128)
            rowsum = rowsum + jnp.sum(piece * w[k, :, at].astype(F32), axis=1, keepdims=True)
            dw[k, :, at] = piece
    rowsum = rowsum / column
    gain_row[...] = jnp.transpose(jnp.broadcast_to(rowsum, (owned, 128)))[: gain_row.shape[0]]


def pair_add_kernel(n, *refs):
    for i in range(n):
        refs[2 * n + i][...] = (refs[i][...].astype(F32) + refs[n + i][...].astype(F32)).astype(BF)


def place_kernel(e_loc, idx, *refs):
    came, gin, gdown = refs[:e_loc], refs[e_loc], refs[e_loc + 1]
    width = gin.shape[0] // (2 * e_loc)
    strips = width // 256
    for q in range(e_loc):

        @pl.when(idx[S_EXPERT] == q)
        def _():
            for d in range(e_loc):
                e = q ^ d
                for i in range(2):
                    lanes = slice(i * 128, (i + 1) * 128)
                    rows = came[d][0:width, lanes].astype(F32)
                    gin[pl.ds(2 * e + i, width, stride=2 * e_loc), :] = rows
                    for j in range(strips):
                        at = width + j * 128
                        rows = came[d][at : at + 128, lanes].astype(F32)
                        at = (2 * j + i) * 128
                        gdown[:, e, at : at + 128] = rows


def pack_kernel(idx, w_qkv, w_out, router, const, vec, gain1, gain2, keep, swap, give, early, pairs):
    part = w_out.shape[1]
    owned = w_out.shape[0]
    rows = [r[...].astype(F32) for r in (router, const, vec, gain1, gain2)]
    rows.append(jnp.zeros((128 - 20, owned), F32))
    columns = jnp.transpose(jnp.concatenate(rows, axis=0))
    early[:, :part] = w_out[...]
    early[:, part:] = columns.astype(BF)
    for k in range(3):
        for p in range(4):
            if p < part // 128:
                pairs[p, :, k * 128 : (k + 1) * 128] = w_qkv[k, :, p * 128 : (p + 1) * 128]
            else:
                pairs[p, :, k * 128 : (k + 1) * 128] = jnp.zeros((owned, 128), BF)
    near, away = 2 * idx[0], 2 * (1 - idx[0])
    core = idx[1]
    keep[...] = pairs[near + core]
    swap[...] = pairs[away + core]
    give[:owned, :] = pairs[near + 1 - core]
    give[owned:, :] = pairs[away + 1 - core]


def final_kernel(idx, tokens, own, came, grad_res, small, grad, gn_rows):
    slots = own.shape[0]
    first = idx[S_BIT + 1]
    gn_rows[pl.ds(pl.multiple_of(first * slots, slots), slots), :] = own[...]
    gn_rows[pl.ds(pl.multiple_of((1 - first) * slots, slots), slots), :] = came[...].astype(F32)
    x = tokens[...].astype(F32)
    rstd = lax.rsqrt(jnp.mean(x * x, axis=-1, keepdims=True) + EPS)
    xhat = x * rstd
    ghat = gn_rows[...] * small[C_GAIN1 : C_GAIN1 + 1]
    grad[...] = grad_res[...] + rstd * (
        ghat - xhat * jnp.mean(ghat * xhat, axis=-1, keepdims=True)
    )


def per_device(
    tokens, previous_layer_logits, lengths, routes, pair_order, gain_attn, w_qkv, w_out, gain_ffn,
    w_router, w_residual, w_const, const_vec, w_in, w_down, cotangent,
):
    seq_dev, slot_dev, width = tokens.shape
    n_all = previous_layer_logits.shape[2]
    tok = seq_dev * slot_dev
    heads = lax.axis_size("head")
    ring = lax.axis_size("ring")
    n_blk = 2 * ring
    n_seq = seq_dev * heads
    n_slots = slot_dev * n_blk
    e_loc = w_in.shape[1]
    n_share = ring // e_loc
    unit = w_in.shape[3]
    rows_here = gain_attn.shape[0]
    part = w_qkv.shape[2]
    capacity = 9 * 2 * tok // (8 * n_all)
    h = lax.axis_index("head")
    ring_at = lax.axis_index("ring")
    core = lax.axis_index("core")
    b = ring_at * 2 + core
    q = ring_at % e_loc
    swap = [(0, 1), (1, 0)]
    blk = ("ring", "core")
    barrier = lax.optimization_barrier

    def across(x):
        return lax.ppermute(x, "head", swap)

    def partner(x):
        return lax.ppermute(x, "core", swap)

    def join(parts):
        total = unit * len(parts)
        cube = jnp.concatenate([p[:width].reshape(width, 2, unit) for p in parts], axis=2)
        down = [p[width:].reshape(strips, unit, 2 * unit) for p in parts]
        down = [jnp.transpose(p, (1, 0, 2)).reshape(unit, -1, 2 * total) for p in down]
        down = jnp.transpose(jnp.concatenate(down, axis=0), (1, 0, 2))
        return jnp.concatenate(
            [cube.reshape(width, 2 * total), down.reshape(-1, 2 * total)], axis=0)

    def divide(full):
        total = full.shape[1] // 2
        cube = full[:width].reshape(width, 2, total // unit, unit)
        down = jnp.transpose(full[width:].reshape(-1, total, 2 * total), (1, 0, 2))
        down = down.reshape(total // unit, unit, strips, 2 * unit)
        return [
            jnp.concatenate(
                [cube[:, :, d].reshape(width, 2 * unit),
                 jnp.transpose(down[d], (1, 0, 2)).reshape(-1, 2 * unit)], axis=0)
            for d in range(total // unit)]

    def hop(x, d):
        return lax.ppermute(x, "ring", [(i, i ^ d) for i in range(ring)]) if d else x

    bit = [(ring_at >> i) & 1 for i in range(3)]
    more = [1 << i for i in range(3, ring.bit_length() - 1)]
    both_axes = ("head", "ring")

    def to_head(same):
        pairs = []
        for i in range(heads):
            for r in range(ring):
                third = (r >> 2) & 1
                target = third if same else 1 - third
                pairs.append((i * ring + r, target * ring + ((r & ~4) | (i << 2))))
        return pairs

    def xor_blocks(ring_base, offsets):
        ring_off = np.array([d for d, _ in offsets], np.int32)
        core_off = np.array([k for _, k in offsets], np.int32)
        return (ring_base ^ ring_off) * 2 + (core ^ core_off)

    seq_base = (ring_at & ~4) | (h << 2)
    x_off = [(0, 0), (1, 0), (4, 0), (5, 0)]
    for d in more:
        x_off = x_off + [(r ^ d, k) for r, k in x_off]
    x_off = x_off + [(r ^ 2, k) for r, k in x_off]
    x_off = x_off + [(r, 1) for r, _ in x_off]
    w_off = [(0, 0), (0, 1), (2, 0), (2, 1)]
    w_off = w_off + [(r ^ 4, k) for r, k in w_off]
    w_off = w_off + [(r ^ 1, k) for r, k in w_off]
    p_off = [(0, 0)]
    for d in (4, 2, 1):
        p_off = p_off + [(r ^ d, 0) for r, _ in p_off]
    p_off = p_off + [(r, 1) for r, _ in p_off]
    direct = ring == 8
    flat_tokens = tokens.reshape(tok, width)
    near_rows = lax.dynamic_index_in_dim(tokens, bit[0], 0, keepdims=False)
    away_rows = lax.dynamic_index_in_dim(tokens, 1 - bit[0], 0, keepdims=False)
    w_phys = jnp.transpose(w_qkv, (1, 0, 2))
    gain_row_in = gain_attn[None, :]
    keep_w, swap_w, give_w, early = call(
        pack_kernel,
        [sds((rows_here, part), BF), sds((rows_here, part), BF), sds((2 * rows_here, part), BF),
         sds((rows_here, part + 128), BF)],
        [jnp.stack([bit[1], core]), w_phys, w_out, jnp.transpose(w_router), jnp.transpose(w_const),
         jnp.transpose(const_vec), gain_row_in, gain_ffn[None, :]], smem=1,
        scratch=[pltpu.VMEM((4, rows_here, part), BF)], name="pack", far_in=range(1, 8))

    def spread_to(x, d):
        return jnp.concatenate([x, hop(x, d)], axis=0)

    def gathered(x):
        return [lax.all_gather(x, blk, axis=0, tiled=True)]

    p_rows = rows_here if direct else width
    w_rows = rows_here if direct else width
    two_blocks = jnp.concatenate([near_rows, hop(away_rows, 1)], axis=0)
    if direct:
        came_w = partner(give_w)
        early = spread_to(early, 4)
        (two_blocks, routes, pair_order, cotangent, lengths, previous_layer_logits, w_in,
         w_down) = barrier((two_blocks, routes, pair_order, cotangent, lengths,
                            previous_layer_logits, w_in, w_down))
        swapped = [hop(swap_w, 2), hop(came_w[rows_here:], 2)]
    if direct:
        early = spread_to(early, 2)
    x_parts = [lax.ppermute(two_blocks, both_axes, to_head(same)) for same in (True, False)]

    seq = 2 * bit[2] + bit[0]
    seq_len = lax.dynamic_index_in_dim(lengths, seq, 0, keepdims=False)
    base = seq_base * 2 + core
    scalars = [jnp.stack([h, seq_len, base, q, b, bit[1], bit[0], h * 0]), xor_blocks(seq_base, x_off)]
    w_table = S_TABLE + len(x_off)
    if direct:
        scalars += [xor_blocks(ring_at, w_off), xor_blocks(ring_at, p_off)]
        p_table = w_table + len(w_off)
    else:
        scalars += [jnp.zeros((8,), jnp.int32)]
        p_table = w_table
    idx = jnp.concatenate(scalars)

    positions = b * slot_dev + jnp.arange(slot_dev, dtype=jnp.int32)
    own_len = lax.dynamic_slice_in_dim(lengths, h * seq_dev, seq_dev)
    valid = (positions[None, :] < own_len[:, None]).reshape(tok)
    route_rows = jnp.transpose(routes.reshape(tok, 2))
    order = jnp.transpose(pair_order.reshape(tok, 2)).reshape(2 * tok)
    route = route_rows.reshape(2 * tok)
    eligible = jnp.concatenate([valid, valid]) & (route < NEXP)
    before = (
        (route[:, None] == route[None, :]) & (order[None, :] < order[:, None]) & eligible[None, :]
    )
    rank = jnp.sum(before.astype(jnp.int32), axis=1)
    slot = jnp.where(eligible & (rank < capacity), route * capacity + rank, NEXP * capacity)
    slot = slot.reshape(2, tok)
    slot_rows = jnp.concatenate([slot, jnp.zeros((6, tok), jnp.int32)], axis=0)
    ints = jnp.concatenate(
        [routes.reshape(tok, 2), jnp.transpose(slot), valid[:, None].astype(jnp.int32),
         jnp.zeros((tok, 3), jnp.int32)], axis=1)

    strips = width // (2 * unit)
    bundle = jnp.concatenate(
        [jnp.transpose(w_in, (1, 0, 2, 3)).reshape(e_loc, width, 2 * unit),
         jnp.transpose(w_down.reshape(unit, e_loc, strips, 2 * unit), (1, 2, 0, 3)).reshape(
             e_loc, strips * unit, 2 * unit)], axis=1)
    shares = [lax.dynamic_index_in_dim(bundle, q ^ d, 0, keepdims=False) for d in range(e_loc)]

    if direct:
        x_parts, swapped, early, shares, ints, slot_rows, cotangent, lengths = barrier(
            (x_parts, swapped, early, shares, ints, slot_rows, cotangent, lengths))
    for d in more:
        x_parts = x_parts + [hop(a, d) for a in x_parts]
    x_parts = x_parts + [hop(a, 2) for a in x_parts]
    if direct:
        first = jnp.concatenate([keep_w, came_w[:rows_here], *swapped], axis=0)
        w_parts = [first, hop(first, 4), hop(first, 1)]
        early = spread_to(early, 1)
    cot = cotangent.reshape(tok, width)
    per_send = e_loc * capacity
    (send_g,) = call(
        send_grad_kernel, [sds((heads * n_share, per_send, width), BF)], [slot_rows, cot, ints],
        name="send_grad")

    def to_experts(rows):
        flat = rows.reshape(heads * ring * capacity, rows.shape[-1])
        return lax.all_to_all(flat, ("head", "ring"), 0, 0, tiled=True)

    frequency = 10000.0 ** (-(2.0 * jnp.arange(HD // 2, dtype=F32)) / HD)
    slots_here = jnp.arange(n_slots, dtype=jnp.int32) + jnp.minimum(lengths[0], 0)
    angles = slots_here.astype(F32)[:, None] * frequency[None, :]
    cos_all = jnp.concatenate([jnp.cos(angles)] * 4, axis=1)
    sin_all = jnp.concatenate([jnp.sin(angles)] * 4, axis=1)
    prev = previous_layer_logits.reshape(tok, n_all)
    prev_wide = jnp.pad(prev, ((0, 0), (0, 128 - n_all)))
    prev_logits = jnp.pad(
        jnp.dot(prev, w_residual, precision=lax.Precision.HIGHEST), ((0, 0), (0, 128 - n_all)))
    if direct:
        x_parts, w_parts, early, send_g, cos_all, sin_all = barrier(
            (x_parts, w_parts, early, send_g, cos_all, sin_all))
        w_parts = w_parts + [hop(w_parts[1], 1)]
        early_parts = [early, partner(early)]
    else:
        wide_w = jnp.pad(w_qkv, ((0, 0), (0, 0), (0, 512 - part))).reshape(rows_here, 3, 4, 128)
        wide_w = jnp.transpose(wide_w, (0, 2, 1, 3)).reshape(rows_here, -1)
        (whole_w,) = gathered(wide_w)
        w_parts = [lax.dynamic_slice_in_dim(whole_w, (2 * bit[1] + core) * part, part, 1)]
        early_parts = gathered(early)
    x_parts = x_parts + [partner(a) for a in x_parts]
    g_rows = to_experts(send_g)
    x_parts, w_parts, early_parts = barrier((x_parts, w_parts, early_parts))

    attn_unit, lse, xn, qkv, early_all, w_pair = call(
        functools.partial(
            attend_kernel, len(x_parts), len(w_parts), len(early_parts), w_rows, p_rows),
        [sds((n_slots, 128), BF), sds((8, n_slots), F32), sds((n_slots, width), BF),
         sds((n_slots, 384), BF), sds((width, part + 128), BF), sds((width, 384), BF)],
        [idx, *x_parts, *w_parts, *early_parts, cos_all, sin_all], smem=1,
        scratch=[pltpu.VMEM((128, n_slots), BF)],
        flops=2 * n_slots * n_slots * 512 + 2 * n_slots * width * 384, name="attend",
        far_in=range(1, 3 + len(x_parts) + len(w_parts) + len(early_parts)),
        far_out=(0, 1, 2, 3, 4, 5))
    attn_unit, g_rows, shares = barrier((attn_unit, g_rows, shares))

    pieces = [hop(shares[d], d) for d in range(e_loc)]

    def exchange(x):
        flat = x.reshape(n_blk * (x.size // x.shape[-1] // n_blk), x.shape[-1])
        return lax.all_to_all(flat, blk, 0, 0, tiled=True)

    attn_recv = exchange(attn_unit).reshape(n_blk, slot_dev, 128)
    attn_recv, pieces[:-1] = barrier((attn_recv, pieces[:-1]))
    w_out_all = Columns(early_all, part, 0)
    mine, other, attn_low = call(
        out_kernel,
        [sds((tok, width), F32), sds((tok, width), BF), sds((n_seq * slot_dev, part), BF)],
        [idx, attn_recv, w_out_all], smem=1,
        scratch=[pltpu.VMEM((n_seq * slot_dev, width), F32)],
        flops=2 * n_seq * slot_dev * width * part, name="out", far_in=(2,), far_out=(2,))
    w_small_all = Columns(early_all, 128, part)
    send_x, residual, aux, small = call(
        route_kernel,
        [sds((heads * n_share, per_send, width + 128), BF), sds((tok, width), F32),
         sds((tok, 128), F32), sds((24, width), F32)],
        [flat_tokens, mine, across(other), w_small_all, prev_logits, ints, slot_rows],
        flops=tok * width * 1000, name="route", far_in=(3, 4, 5), far_out=(1, 2, 3))
    send_x, pieces = barrier((send_x, pieces))
    pieces = pieces + [partner(p) for p in pieces]
    x_rows = to_experts(send_x)
    x_rows, pieces = barrier((x_rows, pieces))
    group = max(1, 128 // unit)
    if group > 1:
        pieces = [join(pieces[i : i + group]) for i in range(0, len(pieces), group)]
    back_rows, *grad_pieces = experts(x_rows, g_rows, pieces)
    back_recv = to_experts(back_rows)

    if group > 1:
        grad_pieces = [part_of for full in grad_pieces for part_of in divide(full)]
    ours = list(grad_pieces[:e_loc])
    theirs = [partner(p) for p in grad_pieces[e_loc:]]
    recv = back_recv.reshape(heads * n_share, per_send, 2 * width)
    added = call(
        functools.partial(pair_add_kernel, e_loc), [sds(p.shape, BF) for p in ours], ours + theirs,
        name="pair_add", far_in=range(2 * e_loc), far_out=range(e_loc))

    came = [added[0], hop(added[1], 1)]
    half_way = hop(added[3], 2)
    recv, added, came, half_way = barrier((recv, added, came, half_way))
    output, grad_res, grad_low, sums = call(
        combine_kernel,
        [sds((tok, width), F32), sds((tok, width), F32), sds((tok, width), BF), sds((40, width), F32)],
        [recv, residual, cot, small, w_small_all, ints, aux, prev_wide], flops=tok * width * 2000,
        name="combine", far_in=(1, 2, 3, 4, 5, 6, 7), far_out=(0, 1))

    came = came + [hop(added[2], 2), hop(half_way, 1)]
    pay = (n_blk // 2, rows_here, part + 128)
    send_gv, grad_both = call(
        grad_vec_kernel,
        [sds((n_blk, slot_dev, 128), BF), sds((n_seq * slot_dev, width), BF)],
        [idx, grad_low, across(grad_low), w_out_all], smem=1,
        flops=2 * n_seq * slot_dev * width * part, name="grad_vec", far_in=(3,), far_out=(1,))
    dout = exchange(send_gv)
    keep, give = call(
        pay_kernel, [sds(pay, F32), sds(pay, BF)],
        [idx, grad_both, attn_low, sums, across(sums)], smem=1,
        scratch=[pltpu.VMEM((n_blk, rows_here, part + 128), F32)],
        flops=2 * n_seq * slot_dev * width * part, name="pay", far_in=(1, 2, 3), far_out=(0, 1))
    steps = [1 << (i - 1) for i in halving_bits(n_blk)[1:]]

    def halve(keep, came_sum, d):
        half = (keep.shape[0] // 2,) + keep.shape[1:]
        keep, give = call(
            halve_kernel, [sds(half, F32), sds(half, BF)], [keep, came_sum], name="halve")
        return keep, hop(give, d)

    came_sum = partner(give)
    dout, came, came_sum = barrier((dout, came, came_sum))

    keep, came_sum = halve(keep, came_sum, steps[0])
    (grad_unit,) = call(
        attend_back_kernel, [sds((n_slots, 384), BF)],
        [idx, qkv, dout, attn_unit, lse, cos_all, sin_all], smem=1,
        scratch=[pltpu.VMEM((128, n_slots), BF), pltpu.VMEM((n_slots, 128), F32),
                 pltpu.VMEM((n_slots, 128), F32)],
        flops=5 * n_slots * n_slots * 256, name="attend_back", far_in=(1, 3, 4, 5, 6), far_out=())
    grad_unit, came_sum = barrier((grad_unit, came_sum))
    rows8 = (8, slot_dev, width)
    gn_keep, gn_give = call(
        unit_back_kernel, [sds(rows8, F32), sds(rows8, BF)], [idx, grad_unit, w_pair], smem=1,
        scratch=[pltpu.VMEM((n_slots, width), F32)], flops=2 * n_slots * width * 384,
        name="unit_back", far_in=(2,), far_out=(0,))
    gn_came = partner(gn_give)
    owners = (8, rows_here, 384)
    dw_keep, dw_give = call(
        unit_dw_kernel, [sds(owners, F32), sds(owners, BF)], [idx, xn, grad_unit], smem=1,
        scratch=[pltpu.VMEM((n_blk, rows_here, 384), F32)],
        flops=2 * n_slots * width * 384, name="unit_dw", far_in=(1,), room=20)
    gn_came, dw_give, came_sum = barrier((gn_came, dw_give, came_sum))
    dw_came = hop(dw_give, 1)
    gn_keep, gn_came = halve(gn_keep, gn_came, 2)
    keep, came_sum = halve(keep, came_sum, steps[1])
    def by_source(parts):
        chosen = []
        for e in range(e_loc):
            value = parts[e_loc - 1]
            for d in range(e_loc - 1):
                value = jnp.where((q ^ d) == e, parts[d], value)
            chosen.append(value.astype(F32))
        return chosen

    if group == 1:
        in_sum, down_sum = call(
            functools.partial(place_kernel, e_loc),
            [sds((width * e_loc * 2, 128), F32), sds((unit, e_loc, width), F32)],
            [idx, *came], smem=1, name="place", far_in=range(1, e_loc + 1), far_out=(0, 1))
        in_sum = in_sum.reshape(width, e_loc, 2, unit)
    else:
        in_sum = jnp.stack(by_source([p[:width].reshape(width, 2, unit) for p in came]), axis=1)
        down_sum = by_source([p[width:].reshape(strips, unit, 2 * unit) for p in came])
        down_sum = jnp.transpose(jnp.stack(down_sum, axis=0), (2, 0, 1, 3))
        down_sum = down_sum.reshape(unit, e_loc, width)
    gn_came, in_sum, down_sum, came_sum, dw_came = barrier(
        (gn_came, in_sum, down_sum, came_sum, dw_came))
    rows2 = (2, slot_dev, width)
    gn_parts = call(
        both_kernel, [sds(rows2, BF), sds(rows2, BF)], [gn_keep, gn_came], name="both")
    gn_parts = [
        lax.ppermute(a, both_axes, [(t, f) for f, t in to_head(same)])
        for a, same in zip(gn_parts, (True, False))]
    dw_keep, dw_came = halve(dw_keep, dw_came, 4)
    for d in steps[2:]:
        keep, came_sum = halve(keep, came_sum, d)
    gn_parts, came_sum = barrier((gn_parts, came_sum))
    two_owners = (2, rows_here, 384)
    dw_stay, dw_go = call(
        both_kernel, [sds(two_owners, BF), sds(two_owners, BF)], [dw_keep, dw_came], name="both_dw")
    dw_far = hop(dw_go, 2)
    dw_near = partner(jnp.concatenate([dw_stay[1:], dw_far[1:]], axis=0))
    gn_own, gn_away = call(
        heads_kernel, [sds((slot_dev, width), F32), sds((slot_dev, width), BF)], list(gn_parts),
        name="heads")
    gn_near = hop(gn_away, 1)

    out_sum, gain2_sum, router_sum, const_sum, vec_sum, resid_sum = call(
        functools.partial(last_add_kernel, n_all),
        [sds((rows_here, part), F32), sds((1, rows_here), F32), sds((n_all, rows_here), F32),
         sds((4, rows_here), F32), sds((2, rows_here), F32), sds((n_all, n_all), F32)],
        [keep, came_sum], name="last_add")
    (grad_tokens,) = call(
        final_kernel, [sds((tok, width), F32)],
        [idx, flat_tokens, gn_own, gn_near, grad_res, small], smem=1,
        scratch=[pltpu.VMEM((tok, width), F32)], name="final", far_in=(1, 4, 5), far_out=(0,))
    dw_near, grad_tokens = barrier((dw_near, grad_tokens))
    qkv_sum, gain1_part = call(
        total_kernel, [sds((3, rows_here, part), F32), sds((8, rows_here), F32)],
        [idx, dw_stay, dw_far, dw_near, w_phys, gain_row_in], smem=1,
        scratch=[pltpu.VMEM((4, rows_here, 384), F32)], name="total", far_in=(4, 5))
    gain1_sum = gain1_part[0] + across(gain1_part)[0]
    return (
        output.reshape(tokens.shape),
        grad_tokens.reshape(tokens.shape),
        gain1_sum,
        jnp.transpose(qkv_sum, (1, 0, 2)),
        out_sum,
        gain2_sum.reshape(rows_here),
        jnp.transpose(router_sum),
        resid_sum,
        jnp.transpose(const_sum),
        jnp.transpose(vec_sum),
        in_sum,
        down_sum,
    )


def solution(mesh):
    heads, blocks = mesh.devices.shape
    split = Mesh(mesh.devices.reshape(heads, blocks // 2, 2), ("head", "ring", "core"))
    blk = ("ring", "core")
    in_specs = (
        P("head", blk, None),
        P("head", blk, None),
        P(),
        P("head", blk, None),
        P("head", blk, None),
        P(blk),
        P(blk, None, "head"),
        P(blk, "head"),
        P(blk),
        P(blk, None),
        P(),
        P(blk, None),
        P(blk, None),
        P(None, "head", None, blk),
        P(blk, "head", None),
        P("head", blk, None),
    )
    out_specs = (
        P("head", blk, None),
        P("head", blk, None),
        P(blk),
        P(blk, None, "head"),
        P(blk, "head"),
        P(blk),
        P(blk, None),
        P(),
        P(blk, None),
        P(blk, None),
        P(None, "head", None, blk),
        P(blk, "head", None),
    )
    return jax.shard_map(
        per_device, mesh=split, in_specs=in_specs, out_specs=out_specs, check_vma=False
    )
```
